32 devices in a mesh: frame: 4 (over y, x), head: 8 (over z, core).
Axes of the slice: x: 2, y: 2, z: 4, core: 2. Of those that a mesh axis runs over, the one named last changes fastest.
Arguments:
- tokens: float32 [8, 1024, 1024], P('frame', 'head'), may hold values from -48 to 48
- qkv_weight: float32 [1024, 3072], replicated
- out_weight: float32 [1024, 1024], replicated, may hold values from -0.1875 to 0.1875
- norm_gain: float32 [1024], replicated, may hold values from 0.1 to 1.9
- proj_weight: float32 [1024, 256], replicated, may hold values from -0.1875 to 0.1875
- up_weight: bfloat16 [256, 4096], replicated, may hold values from -0.375 to 0.375
- conv_weight: bfloat16 [2, 3, 3, 256, 256], replicated, may hold values from -0.125 to 0.125
- conv_bias: float32 [2, 256], replicated, may hold values from -3 to 3
- block_lists: int32 [64, 13], P('frame'), may hold values from 0 to 63, as said below
- block_counts: int32 [64], P('frame'), may hold values from 1 to 13, as said below
Outputs:
- refined: bfloat16 [8, 128, 128, 256], P('frame', 'head')
The draws below stay inside these ranges and needn't reach their ends.
Inputs may be any that keep to these rules, and one draw needn't show every extreme that they name: `block_lists`: row b names 13 different key blocks and its first entry is block b itself; entries at or after the row's count are padding and are ignored. `block_counts`: some query block in every draw has all 13 entries valid.
All inputs are finite; a program needn't handle non-finite values.
Results may differ from the reference program's by a relative error of at most 0.0057.
Values may be sent and summed in bfloat16 or wider, within the bound.
A program may use at most 128 MiB of HBM per device.

```python
import math
import jax
import jax.numpy as jnp
from jax import lax

D = 1024
HEADS = 16
CH = 256
GRID = 32
BLOCK = 128
FRAMES = 8
BLOCKS = 64
SLOTS = 13


def draw_tokens(key, part):
    base = jax.random.fold_in(key, 101)
    shape = (FRAMES, GRID * GRID, D)
    values = jax.random.normal(base, shape, jnp.float32)
    return jnp.clip(values, -6.0, 6.0)


def draw_qkv_weight(key, part):
    base = jax.random.fold_in(key, 202)
    head_dim = D // HEADS
    values = jax.random.normal(base, (D, HEADS, 3, head_dim), jnp.float32)
    values = jnp.clip(values, -6.0, 6.0) * D ** (-0.5)
    return values.reshape(D, 3 * D)


def draw_block_lists(key, part):
    base = jax.random.fold_in(key, 303)
    row_keys = jax.random.split(base, BLOCKS)
    others = jax.vmap(lambda row_key: jax.random.permutation(row_key, BLOCKS - 1))(row_keys)
    others = others[:, :SLOTS - 1].astype(jnp.int32)
    own_block = jnp.arange(BLOCKS, dtype=jnp.int32)[:, None]
    others = others + (others >= own_block).astype(jnp.int32)
    return jnp.concatenate([own_block, others], axis=1)


def draw_block_counts(key, part):
    base = jax.random.fold_in(key, 404)
    busy_key, forced_key, count_key = jax.random.split(base, 3)
    frame_flags = jax.random.randint(busy_key, (FRAMES,), 0, 4)
    forced = jax.random.randint(forced_key, (), 0, FRAMES)
    frame_ids = jnp.arange(FRAMES, dtype=jnp.int32)
    busy = (frame_flags == 0) | (frame_ids == forced)
    busy_blocks = jnp.repeat(busy, GRID * GRID // BLOCK, total_repeat_length=BLOCKS)
    light = jax.random.randint(count_key, (BLOCKS,), 1, SLOTS // 3 + 1)
    return jnp.where(busy_blocks, SLOTS, light).astype(jnp.int32)


def scatter_about(rng, extent, scale, most, kind=jnp.bfloat16):
    entries = scale * jax.random.normal(rng, extent, jnp.float32)
    return jnp.clip(entries, min=-most, max=most).astype(kind)


def setup_inputs(seed: int = 0) -> dict:
    arg_keys = jax.random.split(jax.random.key(seed), 11)
    tokens = draw_tokens(jax.random.fold_in(arg_keys[10], 71), 0)
    qkv_weight = draw_qkv_weight(jax.random.fold_in(arg_keys[10], 71), 0)
    out_weight = scatter_about(arg_keys[2], (D, D), D ** -0.5, 0.1875, jnp.float32)
    norm_gain = jnp.clip(1.0 + 0.18 * jax.random.normal(arg_keys[3], (D,), jnp.float32), 0.1, 1.9)
    proj_weight = scatter_about(arg_keys[4], (D, CH), D ** -0.5, 0.1875, jnp.float32)
    up_weight = scatter_about(arg_keys[5], (CH, 16 * CH), CH ** -0.5, 0.375)
    conv_weight = scatter_about(arg_keys[6], (2, 3, 3, CH, CH), (9 * CH) ** -0.5, 0.125)
    conv_bias = scatter_about(arg_keys[7], (2, CH), 0.5, 3.0, jnp.float32)
    block_lists = draw_block_lists(jax.random.fold_in(arg_keys[10], 71), 0)
    block_counts = draw_block_counts(jax.random.fold_in(arg_keys[10], 71), 0)
    return dict(tokens=tokens, qkv_weight=qkv_weight, out_weight=out_weight, norm_gain=norm_gain, proj_weight=proj_weight, up_weight=up_weight, conv_weight=conv_weight, conv_bias=conv_bias, block_lists=block_lists, block_counts=block_counts)


highest = lax.Precision.HIGHEST
eps_norm = 1e-05

def attend(queries, key_values, block_ids, counts, factor):
    groups, slot_total = block_ids.shape
    block_size = queries.shape[1]
    picked = key_values[block_ids]
    picked = picked.reshape((groups, slot_total * block_size) + picked.shape[3:])
    scores = jnp.einsum('gihe,gjhe->ghij', queries, picked[:, :, :, 0, :], precision=highest) * factor
    slot_of = jnp.arange(slot_total * block_size, dtype=jnp.int32) // block_size
    usable = slot_of[None, :] < counts[:, None]
    scores = jnp.where(usable[:, None, None, :], scores, -jnp.inf)
    row_max = lax.optimization_barrier(jnp.max(scores, axis=3, keepdims=True))
    weights = jnp.exp(scores - row_max)
    totals = lax.optimization_barrier(jnp.sum(weights, axis=3))
    blended = jnp.einsum('ghij,gjhe->gihe', weights, picked[:, :, :, 1, :], precision=highest)
    return blended / jnp.transpose(totals, (0, 2, 1))[:, :, :, None]

def layer_norm(rows, gain):
    centre = lax.optimization_barrier(jnp.mean(rows, axis=-1, keepdims=True))
    centred = rows - centre
    spread = lax.optimization_barrier(jnp.mean(centred * centred, axis=-1, keepdims=True))
    return centred * lax.rsqrt(spread + eps_norm) * gain

def conv_window(padded, weight):
    frames_here, rows_in, cols_in, channels = padded.shape
    rows_out = rows_in - 2
    cols_out = cols_in - 2
    summed = jnp.zeros((frames_here * rows_out * cols_out, weight.shape[-1]), jnp.float32)
    for row_off in range(3):
        for col_off in range(3):
            window = padded[:, row_off:row_off + rows_out, col_off:col_off + cols_out, :]
            summed = summed + jnp.dot(window.reshape(-1, channels), weight[row_off, col_off], preferred_element_type=jnp.float32)
    return summed.reshape(frames_here, rows_out, cols_out, -1)

def pad_both(image):
    return jnp.pad(image, ((0, 0), (1, 1), (1, 1), (0, 0)))

def reference(tokens, qkv_weight, out_weight, norm_gain, proj_weight, up_weight, conv_weight, conv_bias, block_lists, block_counts):
    model_width = tokens.shape[2]
    head_dim = model_width // HEADS
    flat_rows = tokens.reshape(-1, model_width)
    packed = jnp.dot(flat_rows, qkv_weight, precision=highest, preferred_element_type=jnp.float32)
    packed = packed.reshape(-1, HEADS, 3, head_dim)
    queries = packed[:, :, 0, :].reshape(-1, BLOCK, HEADS, head_dim)
    key_values = packed[:, :, 1:, :].reshape(-1, BLOCK, HEADS, 2, head_dim)
    block_total = queries.shape[0]
    group_blocks = math.gcd(block_total, max(1, 512 // BLOCK))
    group_count = block_total // group_blocks
    factor = head_dim ** (-0.5)

    def one_group(items):
        return attend(items[0], key_values, items[1], items[2], factor)
    attended = lax.map(one_group, (queries.reshape(group_count, group_blocks, BLOCK, HEADS, head_dim), block_lists.reshape(group_count, group_blocks, -1), block_counts.reshape(group_count, group_blocks)))
    attended = attended.reshape(-1, model_width)
    stream = flat_rows + jnp.dot(attended, out_weight, precision=highest, preferred_element_type=jnp.float32)
    normed = layer_norm(stream, norm_gain)
    features = jnp.dot(normed, proj_weight, precision=highest, preferred_element_type=jnp.float32).astype(jnp.bfloat16)
    channels = features.shape[1]
    lifted = jnp.dot(features, up_weight, preferred_element_type=jnp.float32).astype(jnp.bfloat16)
    lifted = lifted.reshape(-1, GRID, GRID, 4, 4, channels)
    upsampled = jnp.transpose(lifted, (0, 1, 3, 2, 4, 5)).reshape(-1, 4 * GRID, 4 * GRID, channels)
    activated = jnp.maximum(upsampled, jnp.zeros((), jnp.bfloat16))
    first_conv = conv_window(pad_both(activated), conv_weight[0]) + conv_bias[0]
    hidden = jnp.maximum(first_conv, 0.0).astype(jnp.bfloat16)
    second = conv_window(pad_both(hidden), conv_weight[1]) + conv_bias[1]
    return (upsampled.astype(jnp.float32) + second).astype(jnp.bfloat16)
```

```python
import functools

import jax
import jax.numpy as jnp
from jax import lax
from jax.experimental import pallas as pl
from jax.experimental.pallas import tpu as pltpu
from jax.sharding import PartitionSpec as P

HEADS = 16
GRID = 32
BLOCK = 128
eps_norm = 1e-05
highest = lax.Precision.HIGHEST
f32 = jnp.float32
bf16 = jnp.bfloat16


def divisor_upto(count, most):
    return max(d for d in range(1, most + 1) if count % d == 0)


def split_hi_lo(value):
    hi = value.astype(bf16)
    return hi, (value - hi.astype(f32)).astype(bf16)


def mxu(a, b):
    return jnp.dot(a, b, preferred_element_type=f32)


def qkv_kernel(local_heads, head_dim, x_ref, w_ref, q_ref, kv_ref, x_hi, x_lo):
    @pl.when(pl.program_id(0) == 0)
    def _():
        hi, lo = split_hi_lo(x_ref[...])
        x_hi[...] = hi
        x_lo[...] = lo

    w_hi, w_lo = split_hi_lo(w_ref[...])
    acc = mxu(x_hi[...], w_lo) + mxu(x_lo[...], w_hi)
    acc = acc + mxu(x_hi[...], w_hi)
    pair = 2 * head_dim
    frames, _, strip, _ = q_ref.shape
    rows = frames * strip
    first = lax.broadcasted_iota(jnp.int32, (rows, pair), 1) < head_dim
    parts = [acc[:, n * pair : (n + 1) * pair] for n in range(3)]
    turned = [pltpu.roll(part, head_dim, 1) for part in parts]

    def coded(value):
        rest = value - value.astype(bf16).astype(f32)
        return jnp.where(first, value, rest).astype(bf16).reshape(frames, strip, pair)

    factor = head_dim ** (-0.5)
    queries = [
        coded(jnp.where(first, parts[0], turned[0]) * factor),
        coded(jnp.where(first, turned[1], parts[1]) * factor),
    ]
    keys = [
        coded(jnp.where(first, turned[0], parts[0])),
        coded(jnp.where(first, parts[2], turned[2])),
    ]
    if local_heads == 2:
        for h in range(2):
            q_ref[:, 0, :, h * pair : (h + 1) * pair] = queries[h]
            kv_ref[:, 0, :, h * pair : (h + 1) * pair] = keys[h]
        values = jnp.where(first, parts[1], parts[2]).astype(bf16)
        kv_ref[:, 0, :, 2 * pair :] = values.reshape(frames, strip, pair)
    else:
        for h, values in enumerate((parts[1], turned[2])):
            q_ref[:, h] = queries[h]
            kv_ref[:, h, :, :pair] = keys[h]
            values = values[:, :head_dim].astype(bf16)
            kv_ref[:, h, :, pair:] = values.reshape(frames, strip, head_dim)


def project(tokens, weight, head_groups, head_dim):
    frames, strip, width = tokens.shape
    local_heads = HEADS // head_groups
    share = 2 // local_heads
    columns = 6 * head_dim
    q_width, kv_width = local_heads * 2 * head_dim, local_heads * 3 * head_dim
    return pl.pallas_call(
        functools.partial(qkv_kernel, local_heads, head_dim),
        grid=(HEADS // 2,),
        in_specs=[
            pl.BlockSpec((frames * strip, width), lambda i: (0, 0)),
            pl.BlockSpec((width, columns), lambda i: (0, i)),
        ],
        out_specs=[
            pl.BlockSpec((frames, share, strip, q_width), lambda i: (0, i, 0, 0)),
            pl.BlockSpec((frames, share, strip, kv_width), lambda i: (0, i, 0, 0)),
        ],
        out_shape=[
            jax.ShapeDtypeStruct((frames, head_groups, strip, q_width), bf16),
            jax.ShapeDtypeStruct((frames, head_groups, strip, kv_width), bf16),
        ],
        scratch_shapes=[pltpu.VMEM((frames * strip, width), bf16)] * 2,
        compiler_params=pltpu.CompilerParams(vmem_limit_bytes=48 << 20),
        name="qkv",
    )(tokens.reshape(-1, width), weight)


MESH = pl.DeviceIdType.MESH


def near_first(count):
    return sorted(range(1, count), key=lambda j: (min(j, count - j), j))


def greet(peers):
    barrier = pltpu.get_barrier_semaphore()
    for peer in peers:
        pl.semaphore_signal(barrier, inc=1, device_id=peer, device_id_type=MESH)
    pl.semaphore_wait(barrier, len(peers))


def exchange_kernel(
    groups, teams, q_ref, kv_ref, q_out, pairs, own_sem,
    q_send, q_recv, z_send, z_recv, f_send, f_recv, r_send, r_recv,
):
    frames = q_ref.shape[0]
    team, me = lax.axis_index("frame"), lax.axis_index("head")
    square = teams == 4
    if square:
        side = lax.rem(team, 2)
        beside, across = team + 1 - 2 * side, lax.rem(team + 2, 4)
        direct = [(beside, beside), (across, across)]
    else:
        direct = [
            (lax.rem(team + k, teams), lax.rem(team + teams - k, teams)) for k in range(1, teams)
        ]
    order = near_first(groups)
    peers = [(team, lax.rem(me + j, groups)) for j in order] + [(to, me) for to, _ in direct]
    greet(peers)

    def remote(src, dst, send, recv, target):
        return pltpu.make_async_remote_copy(
            src_ref=src, dst_ref=dst, send_sem=send, recv_sem=recv,
            device_id=target, device_id_type=MESH,
        )

    def z_copy(f, j):
        to = lax.rem(me + j, groups)
        return remote(
            kv_ref.at[f, to], pairs.at[team * frames + f, me],
            z_send.at[f, j], z_recv.at[f, j], (team, to),
        )

    def q_copy(f, j):
        to = lax.rem(me + j, groups)
        return remote(
            q_ref.at[f, to], q_out.at[f, me], q_send.at[f, j], q_recv.at[f, j], (team, to)
        )

    def piece(owner, f, j):
        return pairs.at[owner * frames + f, lax.rem(me + groups - j, groups)]

    def f_copy(k, f, j):
        src = kv_ref.at[f, me] if j == 0 else piece(team, f, j)
        return remote(
            src, piece(team, f, j), f_send.at[k, f, j], f_recv.at[k, f, j], (direct[k][0], me)
        )

    def r_copy(f, j):
        origin, to = (beside, across) if f % 2 == 0 else (across, beside)
        here = piece(origin, f, j)
        return remote(here, here, r_send.at[f, j], r_recv.at[f, j], (to, me))

    own = []
    for f in range(frames):
        own.append(
            pltpu.make_async_copy(kv_ref.at[f, me], pairs.at[team * frames + f, me], own_sem.at[0, f])
        )
        own.append(pltpu.make_async_copy(q_ref.at[f, me], q_out.at[f, me], own_sem.at[1, f]))
    schedule = [(f, j) for j in [0] + order for f in range(frames)]
    for f, j in schedule:
        if j:
            z_copy(f, j).start()
    for f, j in schedule:
        if j:
            q_copy(f, j).start()
    for copy in own:
        copy.start()
    lag = 2 * frames
    for n in range(len(schedule) + lag):
        if n < len(schedule):
            f, j = schedule[n]
            if j:
                z_copy(f, j).wait_recv()
            for k in range(len(direct)):
                f_copy(k, f, j).start()
        if n >= lag and square:
            f, j = schedule[n - lag]
            f_copy(f % 2, f, j).wait_recv()
            r_copy(f, j).start()
    for f, j in schedule:
        for k in range(len(direct)):
            f_copy(k, f, j).wait_send()
            if not (square and k == f % 2):
                f_copy(k, f, j).wait_recv()
        if square:
            r_copy(f, j).wait()
        if j:
            z_copy(f, j).wait_send()
            q_copy(f, j).wait()
    for copy in own:
        copy.wait()


def exchange(queries, own_pairs, groups, teams):
    frames = queries.shape[0]
    sems = lambda *shape: pltpu.SemaphoreType.DMA(shape)
    hops = 2 if teams == 4 else teams - 1
    vmem = pl.BlockSpec(memory_space=pltpu.VMEM)
    anywhere = pl.BlockSpec(memory_space=pl.ANY)
    return pl.pallas_call(
        functools.partial(exchange_kernel, groups, teams),
        in_specs=[vmem, vmem],
        out_specs=[anywhere, anywhere],
        out_shape=[
            jax.ShapeDtypeStruct(queries.shape, bf16),
            jax.ShapeDtypeStruct((teams * frames,) + own_pairs.shape[1:], bf16),
        ],
        scratch_shapes=[sems(2, frames)]
        + [sems(frames, groups)] * 4
        + [sems(hops, frames, groups)] * 2
        + [sems(frames, groups)] * 2,
        compiler_params=pltpu.CompilerParams(collective_id=0, has_side_effects=True),
        name="exchange",
    )(queries, own_pairs)


def hand_back_kernel(groups, src, dst, own_sem, send, recv):
    team, me = lax.axis_index("frame"), lax.axis_index("head")
    order = near_first(groups)
    greet([(team, lax.rem(me + j, groups)) for j in order])
    copies = []
    for j in reversed(order):
        to = lax.rem(me + j, groups)
        copies.append(
            pltpu.make_async_remote_copy(
                src_ref=src.at[:, to], dst_ref=dst.at[me],
                send_sem=send.at[j], recv_sem=recv.at[j],
                device_id=(team, to), device_id_type=MESH,
            )
        )
    copies.append(pltpu.make_async_copy(src.at[:, me], dst.at[me], own_sem))
    for copy in copies:
        copy.start()
    for copy in copies:
        copy.wait()


def hand_back(attended):
    frames, groups, strip, width = attended.shape
    vmem = pl.BlockSpec(memory_space=pltpu.VMEM)
    return pl.pallas_call(
        functools.partial(hand_back_kernel, groups),
        in_specs=[vmem],
        out_specs=vmem,
        out_shape=jax.ShapeDtypeStruct((groups, frames, strip, width), bf16),
        scratch_shapes=[pltpu.SemaphoreType.DMA] + [pltpu.SemaphoreType.DMA((groups,))] * 2,
        compiler_params=pltpu.CompilerParams(collective_id=1, has_side_effects=True),
        name="hand_back",
    )(attended)


def attend_kernel(local_heads, head_dim, span, lists, counts, q_ref, kv_ref, o_ref):
    b = pl.program_id(0)
    count = counts[b]
    pair = 2 * head_dim
    v_at = local_heads * pair
    v_width = local_heads * head_dim
    first = lax.broadcasted_iota(jnp.int32, (BLOCK, pair), 1) < head_dim
    stacked = []
    for h in range(local_heads):
        coded = q_ref[:, h * pair : (h + 1) * pair].astype(f32)
        turned = pltpu.roll(coded, head_dim, 1)
        high, low = jnp.where(first, coded, turned), jnp.where(first, turned, coded)
        stacked.append(jnp.concatenate([high, low], axis=0).astype(bf16))

    def chunk(c, carry):
        offsets = []
        valid = []
        for t in range(span):
            slot = c * span + t
            block = lists[b, jnp.minimum(slot, count - 1)]
            offsets.append(pl.multiple_of(block * BLOCK, BLOCK))
            valid.append(slot < count)
        values = jnp.concatenate(
            [kv_ref[pl.ds(at, BLOCK), v_at : v_at + v_width] for at in offsets], axis=0
        )
        out = []
        for h in range(local_heads):
            top, total, blend = carry[h]
            scores = []
            for at, ok in zip(offsets, valid):
                keys = kv_ref[pl.ds(at, BLOCK), h * pair : (h + 1) * pair]
                both = lax.dot_general(
                    stacked[h], keys, (((1,), (1,)), ((), ())), preferred_element_type=f32
                )
                scores.append(jnp.where(ok, both[:BLOCK] + both[BLOCK:], -jnp.inf))
            peak = functools.reduce(jnp.maximum, scores)
            new_top = jnp.maximum(top, jnp.max(peak, axis=1, keepdims=True))
            scale = jnp.exp(top - new_top)
            weights = [jnp.exp(s - new_top) for s in scores]
            total = total * scale + functools.reduce(jnp.add, weights)
            packed = jnp.concatenate([w.astype(bf16) for w in weights], axis=1)
            blend = blend * scale + mxu(packed, values)
            out.append((new_top, total, blend))
        return tuple(out)

    start = tuple(
        (
            jnp.full((BLOCK, 1), -jnp.inf, f32),
            jnp.zeros((BLOCK, BLOCK), f32),
            jnp.zeros((BLOCK, v_width), f32),
        )
        for _ in range(local_heads)
    )
    final = lax.fori_loop(0, (count + span - 1) // span, chunk, start)
    owner = lax.broadcasted_iota(jnp.int32, (BLOCK, v_width), 1) // head_dim
    result = jnp.zeros((BLOCK, v_width), f32)
    for h in range(local_heads):
        _, total, blend = final[h]
        ready = blend / jnp.sum(total, axis=1, keepdims=True)
        result = jnp.where(owner == h, ready, result)
    o_ref[...] = result.astype(bf16)


def attend(queries, pairs, lists, counts, local_heads, head_dim):
    blocks, slots = lists.shape
    span = -(-slots // (-(-slots // 7)))
    width = local_heads * head_dim
    return pl.pallas_call(
        functools.partial(attend_kernel, local_heads, head_dim, span),
        grid_spec=pltpu.PrefetchScalarGridSpec(
            num_scalar_prefetch=2,
            grid=(blocks,),
            in_specs=[
                pl.BlockSpec((BLOCK, queries.shape[1]), lambda i, *_: (i, 0)),
                pl.BlockSpec(pairs.shape, lambda i, *_: (0, 0), pipeline_mode=pl.Buffered(1)),
            ],
            out_specs=pl.BlockSpec((BLOCK, width), lambda i, *_: (i, 0)),
        ),
        out_shape=jax.ShapeDtypeStruct((blocks * BLOCK, width), bf16),
        compiler_params=pltpu.CompilerParams(vmem_limit_bytes=48 << 20),
        name="attend",
    )(lists, counts, queries, pairs)


def scatter_order(teams, halves, k):
    far = halves - 1 - lax.rem(k, halves)
    turn = lax.rem(k // halves + 1 + 2 * far, teams)
    return turn, far


def scatter_kernel(
    teams, groups, head_dim, x_ref, w_hbm, lists_ref, counts_ref,
    kv_out, q_out, lists_out, counts_out,
    w_buf, x_hi, x_lo, msg, msg_scale, got, got_scale, kv_dec, q_dec,
    w_sem, m_send, m_recv, s_send, s_recv, kv_sem, q_sem, f_send, f_recv, l_own, l_send, l_recv,
):
    planes = groups // 2
    halves = planes // 2
    pairs = teams * halves
    chips = teams * planes
    columns = 6 * head_dim
    lanes = 2 * head_dim
    rows = x_ref.shape[0]
    team, group = lax.axis_index("frame"), lax.axis_index("head")
    plane, core = group // 2, lax.rem(group, 2)
    half, parity = plane // 2, lax.rem(plane, 2)
    me = team * planes + plane
    sibling = (team, group + 1 - 2 * core)

    def place(k):
        turn, far = scatter_order(teams, halves, k)
        return lax.rem(team + turn, teams), lax.rem(half + far, halves)

    def weight(k):
        to_team, to_half = place(k)
        at = pl.multiple_of((to_team * halves + to_half) * columns, columns)
        return pltpu.make_async_copy(w_hbm.at[:, pl.ds(at, columns)], w_buf.at[k], w_sem.at[k])

    for k in range(pairs):
        weight(k).start()

    barrier = pltpu.get_barrier_semaphore()
    for step in range(1, chips):
        dt, dz = step // planes, step % planes
        peer = (lax.rem(team + dt, teams), lax.rem(plane + dz, planes) * 2 + core)
        pl.semaphore_signal(barrier, inc=1, device_id=peer, device_id_type=MESH)
    pl.semaphore_signal(barrier, inc=1, device_id=sibling, device_id_type=MESH)

    hi, lo = split_hi_lo(x_ref[...])
    x_hi[...] = hi
    x_lo[...] = lo
    first = lax.broadcasted_iota(jnp.int32, (rows, lanes), 1) < head_dim
    lane = lax.broadcasted_iota(jnp.int32, (BLOCK, lanes), 1)
    top = 32766.0

    pl.semaphore_wait(barrier, chips)

    def list_copies(step):
        to = lax.rem(team + step, teams)
        out = []
        for n, (src, dst) in enumerate(((lists_ref, lists_out), (counts_ref, counts_out))):
            out.append(
                pltpu.make_async_remote_copy(
                    src_ref=src, dst_ref=dst.at[team],
                    send_sem=l_send.at[n, step], recv_sem=l_recv.at[n, step],
                    device_id=(to, group), device_id_type=MESH,
                )
            )
        return out

    own_lists = [
        pltpu.make_async_copy(lists_ref, lists_out.at[team], l_own.at[0]),
        pltpu.make_async_copy(counts_ref, counts_out.at[team], l_own.at[1]),
    ]
    for copy in own_lists:
        copy.start()
    for step in range(1, teams):
        for copy in list_copies(step):
            copy.start()

    def message(to_team, to_plane):
        to = to_team * planes + to_plane
        target = (to_team, to_plane * 2 + core)
        return [
            pltpu.make_async_remote_copy(
                src_ref=msg.at[to], dst_ref=got.at[me],
                send_sem=m_send.at[to], recv_sem=m_recv.at[me],
                device_id=target, device_id_type=MESH,
            ),
            pltpu.make_async_remote_copy(
                src_ref=msg_scale.at[to], dst_ref=got_scale.at[me],
                send_sem=s_send.at[to], recv_sem=s_recv.at[me],
                device_id=target, device_id_type=MESH,
            ),
        ]

    def peak(value):
        return jnp.maximum(jnp.max(jnp.abs(value), axis=1, keepdims=True), 1e-30)

    def send_step(k, carry):
        weight(k).wait()
        w_hi, w_lo = split_hi_lo(w_buf[k])
        acc = mxu(x_hi[...], w_lo) + mxu(x_lo[...], w_hi)
        acc = acc + mxu(x_hi[...], w_hi)
        p0, p1, p2 = [acc[:, n * lanes : (n + 1) * lanes] for n in range(3)]
        t0, t1 = pltpu.roll(p0, head_dim, 1), pltpu.roll(p1, head_dim, 1)
        key_value = [jnp.where(first, t0, t1), p2]
        up, down = slice(0, BLOCK), slice(BLOCK, 2 * BLOCK)
        query = [
            jnp.where(first[up], p0[up], t0[down]),
            jnp.where(first[up], t1[up], p1[down]),
        ]
        to_team, to_half = place(k)
        for i in range(2):
            to_plane = to_half * 2 + i
            to = to_team * planes + to_plane
            kv, q = key_value[i], query[i]
            peak_k = peak(jnp.where(first, kv, 0.0))
            peak_v = peak(jnp.where(first, 0.0, kv))
            peak_q0 = peak(jnp.where(first[up], q, 0.0))
            peak_q1 = peak(jnp.where(first[up], 0.0, q))
            kv = kv * jnp.where(first, top / peak_k, top / peak_v)
            q = q * jnp.where(first[up], top / peak_q0, top / peak_q1)
            msg[to, 0:2] = jnp.round(kv).astype(jnp.int32).astype(jnp.int16).reshape(2, BLOCK, lanes)
            msg[to, 2] = jnp.round(q).astype(jnp.int32).astype(jnp.int16)
            columns_of = [peak_k[up], peak_k[down], peak_v[up], peak_v[down], peak_q0, peak_q1]
            table = jnp.zeros((BLOCK, lanes), f32)
            for n, column in enumerate(columns_of):
                table = jnp.where(lane == n, column * (1.0 / top), table)
            msg_scale[to] = jnp.transpose(table)[:8]

            @pl.when(to != me)
            def _():
                for copy in message(to_team, to_plane):
                    copy.start()

            @pl.when(to == me)
            def _():
                got[to] = msg[to]
                got_scale[to] = msg_scale[to]

        return carry

    lax.fori_loop(0, pairs, send_step, 0)

    factor = head_dim ** (-0.5) * 1.4426950408889634

    def source(n):
        far = n // (2 * teams)
        turn = lax.rem(lax.rem(n, 2 * teams) // 2 + 1 + 2 * far, teams)
        from_team = lax.rem(team + teams - turn, teams)
        from_plane = lax.rem(half + halves - far, halves) * 2 + lax.rem(parity + 1 + n, 2)
        return from_team, from_plane

    def arrival(src):
        return [
            pltpu.make_async_remote_copy(
                src_ref=msg.at[src], dst_ref=got.at[src],
                send_sem=m_send.at[src], recv_sem=m_recv.at[src],
                device_id=sibling, device_id_type=MESH,
            ),
            pltpu.make_async_remote_copy(
                src_ref=msg_scale.at[src], dst_ref=got_scale.at[src],
                send_sem=s_send.at[src], recv_sem=s_recv.at[src],
                device_id=sibling, device_id_type=MESH,
            ),
        ]

    def handing(from_team, from_plane):
        src = from_team * planes + from_plane
        piece = kv_out.at[from_team, :, from_plane * 2 + core]
        return [
            pltpu.make_async_copy(kv_dec.at[src], piece, kv_sem.at[src]),
            pltpu.make_async_copy(q_dec.at[src], q_out.at[src], q_sem.at[src]),
        ]

    def forward(from_team, from_plane):
        src = from_team * planes + from_plane
        piece = kv_out.at[from_team, :, from_plane * 2 + core]
        return pltpu.make_async_remote_copy(
            src_ref=kv_dec.at[src], dst_ref=piece,
            send_sem=f_send.at[src], recv_sem=f_recv.at[src],
            device_id=sibling, device_id_type=MESH,
        )

    def take_step(n, carry):
        from_team, from_plane = source(n)
        src = from_team * planes + from_plane

        @pl.when(src != me)
        def _():
            for copy in arrival(src):
                copy.wait_recv()

        scale = jnp.transpose(jnp.concatenate([got_scale[src]] * (BLOCK // 8), axis=0))
        near = lane < head_dim
        for f in range(2):
            kv = got[src, f].astype(jnp.int32).astype(f32)
            kv = kv * jnp.where(near, scale[:, f : f + 1], scale[:, 2 + f : 3 + f])
            high = kv.astype(bf16).astype(f32)
            low = pltpu.roll(kv - high, head_dim, 1)
            kv_dec[src, f, :, :lanes] = jnp.where(near, high, low).astype(bf16)
            value = jnp.where(near, pltpu.roll(kv, head_dim, 1), 1.0)
            kv_dec[src, f, :, lanes:] = value.astype(bf16)
        q = got[src, 2].astype(jnp.int32).astype(f32)
        q = q * (factor * jnp.where(near, scale[:, 4:5], scale[:, 5:6]))
        high = q.astype(bf16).astype(f32)
        low = q - high
        high_turned, low_turned = pltpu.roll(high, head_dim, 1), pltpu.roll(low, head_dim, 1)
        q_dec[src, 0, :, :lanes] = jnp.where(near, high, high_turned).astype(bf16)
        q_dec[src, 0, :, lanes:] = jnp.where(near, low, low_turned).astype(bf16)
        q_dec[src, 1, :, :lanes] = jnp.where(near, high_turned, high).astype(bf16)
        q_dec[src, 1, :, lanes:] = jnp.where(near, low_turned, low).astype(bf16)
        forward(from_team, from_plane).start()
        for copy in handing(from_team, from_plane):
            copy.start()
        return carry

    lax.fori_loop(0, chips, take_step, 0)

    def end_step(n, carry):
        from_team, from_plane = source(n)
        src = from_team * planes + from_plane

        @pl.when(src != me)
        def _():
            for copy in arrival(src):
                copy.wait_send()

        copy = forward(from_team, from_plane)
        copy.wait_send()
        copy.wait_recv()
        for copy in handing(from_team, from_plane):
            copy.wait()
        return carry

    lax.fori_loop(0, chips, end_step, 0)
    for copy in own_lists:
        copy.wait()
    for step in range(1, teams):
        for copy in list_copies(step):
            copy.wait()


def scatter(tokens, weight, lists, counts, teams, groups):
    frames, strip, width = tokens.shape
    head_dim = width // HEADS
    lanes = 2 * head_dim
    rows = frames * strip
    chips = HEADS
    pairs = HEADS // 2
    dma = lambda *shape: pltpu.SemaphoreType.DMA(shape)
    vmem = pl.BlockSpec(memory_space=pltpu.VMEM)
    anywhere = pl.BlockSpec(memory_space=pl.ANY)
    return pl.pallas_call(
        functools.partial(scatter_kernel, teams, groups, head_dim),
        in_specs=[vmem, anywhere, vmem, vmem],
        out_specs=[anywhere] * 4,
        out_shape=[
            jax.ShapeDtypeStruct((teams, frames, groups, BLOCK, 2 * lanes), bf16),
            jax.ShapeDtypeStruct((chips, frames, BLOCK, 2 * lanes), bf16),
            jax.ShapeDtypeStruct((teams,) + lists.shape, jnp.int32),
            jax.ShapeDtypeStruct((teams,) + counts.shape, jnp.int32),
        ],
        scratch_shapes=[
            pltpu.VMEM((pairs, width, 6 * head_dim), f32),
            pltpu.VMEM((rows, width), bf16),
            pltpu.VMEM((rows, width), bf16),
            pltpu.VMEM((chips, 3, BLOCK, lanes), jnp.int16),
            pltpu.VMEM((chips, 8, BLOCK), f32),
            pltpu.VMEM((chips, 3, BLOCK, lanes), jnp.int16),
            pltpu.VMEM((chips, 8, BLOCK), f32),
            pltpu.VMEM((chips, frames, BLOCK, 2 * lanes), bf16),
            pltpu.VMEM((chips, frames, BLOCK, 2 * lanes), bf16),
            dma(pairs),
        ]
        + [dma(chips)] * 8
        + [dma(2), dma(2, teams), dma(2, teams)],
        compiler_params=pltpu.CompilerParams(
            collective_id=0, has_side_effects=True, vmem_limit_bytes=48 << 20
        ),
        name="scatter",
    )(tokens.reshape(rows, width), weight, lists, counts)


def sparse_kernel(teams, planes, span, lists, counts, q_ref, kv_ref, o_ref):
    src = pl.program_id(0)
    core = lax.rem(lax.axis_index("head"), 2)
    team, plane = src // planes, lax.rem(src, planes)
    lanes = o_ref.shape[-1]
    head_dim = lanes // 2
    ready = []
    for f in range(2):
        row = f * 2 * planes + plane * 2 + core
        count = counts[team, row]
        query = q_ref[0, f]

        def chunk(c, carry):
            top, blend = carry
            scores, values = [], []
            for t in range(span):
                slot = c * span + t
                block = lists[team, row, jnp.minimum(slot, count - 1)]
                at = pl.ds(pl.multiple_of(block * BLOCK, BLOCK), BLOCK)
                keys = kv_ref[at, :lanes]
                score = lax.dot_general(
                    query, jnp.concatenate([keys, keys], axis=1), (((1,), (1,)), ((), ())),
                    preferred_element_type=f32,
                )
                scores.append(jnp.where(slot < count, score, -jnp.inf))
                values.append(kv_ref[at, lanes:])
            peak = jnp.max(functools.reduce(jnp.maximum, scores), axis=1, keepdims=True)
            new_top = jnp.maximum(top, peak)
            packed = jnp.concatenate([jnp.exp2(s - new_top).astype(bf16) for s in scores], axis=1)
            blend = blend * jnp.exp2(top - new_top) + mxu(packed, jnp.concatenate(values, axis=0))
            return new_top, blend

        start = (jnp.full((BLOCK, 1), -jnp.inf, f32), jnp.zeros((BLOCK, lanes), f32))
        _, blend = lax.fori_loop(0, (count + span - 1) // span, chunk, start)
        ready.append(blend / blend[:, head_dim : head_dim + 1])
    near = lax.broadcasted_iota(jnp.int32, (BLOCK, lanes), 1) < head_dim
    o_ref[0] = jnp.where(near, ready[0], pltpu.roll(ready[1], head_dim, 1)).astype(bf16)


def sparse(queries, pairs, lists, counts, teams, groups):
    chips, frames, _, wide = queries.shape
    lanes = wide // 2
    pairs = pairs.reshape(-1, wide)
    slots = lists.shape[-1]
    span = min(slots, 4)
    return pl.pallas_call(
        functools.partial(sparse_kernel, teams, groups // 2, span),
        grid_spec=pltpu.PrefetchScalarGridSpec(
            num_scalar_prefetch=2,
            grid=(chips,),
            in_specs=[
                pl.BlockSpec((1, frames, BLOCK, wide), lambda i, *_: (i, 0, 0, 0)),
                pl.BlockSpec(pairs.shape, lambda i, *_: (0, 0), pipeline_mode=pl.Buffered(1)),
            ],
            out_specs=pl.BlockSpec((1, BLOCK, lanes), lambda i, *_: (i, 0, 0)),
        ),
        out_shape=jax.ShapeDtypeStruct((chips, BLOCK, lanes), bf16),
        compiler_params=pltpu.CompilerParams(vmem_limit_bytes=48 << 20),
        name="sparse",
    )(lists, counts, queries, pairs)


def gather_kernel(
    teams, groups, att_ref, x_ref, w_hbm, gain_ref, proj_ref, ext_ref,
    w_buf, got, w_sem, a_send, a_recv, h_send, h_recv,
):
    planes = groups // 2
    halves = planes // 2
    pairs = teams * halves
    chips = teams * planes
    team, group = lax.axis_index("frame"), lax.axis_index("head")
    plane, core = group // 2, lax.rem(group, 2)
    half = plane // 2
    me = team * planes + plane
    lanes = att_ref.shape[-1]
    head_dim = lanes // 2
    channels = proj_ref.shape[-1]

    def pair_at(n):
        return lax.rem(team + n, teams) * halves + lax.rem(half + n // teams, halves)

    def weight(n):
        at = pl.multiple_of(pair_at(n) * lanes, lanes)
        return pltpu.make_async_copy(
            w_hbm.at[pl.ds(at, lanes)], w_buf.at[pl.ds(n * lanes, lanes)], w_sem.at[n]
        )

    for n in range(pairs):
        weight(n).start()

    above = (team, lax.rem(group + groups - 1, groups))
    below = (team, lax.rem(group + 1, groups))
    barrier = pltpu.get_barrier_semaphore()
    steps = [(s // planes, s % planes) for s in range(1, chips)]
    peers = [
        (lax.rem(team + dt, teams), lax.rem(plane + dz, planes) * 2 + core) for dt, dz in steps
    ]
    for peer in peers + [above, below]:
        pl.semaphore_signal(barrier, inc=1, device_id=peer, device_id_type=MESH)
    got[me] = att_ref[me]
    pl.semaphore_wait(barrier, chips + 1)

    def copy_to(dt, dz):
        to_team, to_plane = lax.rem(team + dt, teams), lax.rem(plane + dz, planes)
        to = to_team * planes + to_plane
        return pltpu.make_async_remote_copy(
            src_ref=att_ref.at[to], dst_ref=got.at[me],
            send_sem=a_send.at[to], recv_sem=a_recv.at[me],
            device_id=(to_team, to_plane * 2 + core), device_id_type=MESH,
        )

    def arrival(src):
        return pltpu.make_async_remote_copy(
            src_ref=att_ref.at[src], dst_ref=got.at[src],
            send_sem=a_send.at[src], recv_sem=a_recv.at[src],
            device_id=below, device_id_type=MESH,
        )

    for dt, dz in sorted(steps, key=lambda s: (s[1] != planes // 2, s[0] == 0)):
        copy_to(dt, dz).start()

    near = lax.broadcasted_iota(jnp.int32, (BLOCK, lanes), 1) < head_dim
    stream = x_ref[...]
    for part in range(halves):
        pieces = []
        for n in range(part * teams, (part + 1) * teams):
            at = pair_at(n) * 2
            weight(n).wait()
            for i in range(2):
                @pl.when(at + i != me)
                def _():
                    arrival(at + i).wait_recv()

            one, two = got[at].astype(f32), got[at + 1].astype(f32)
            upper = jnp.where(near, one, pltpu.roll(two, head_dim, 1))
            lower = jnp.where(near, pltpu.roll(one, head_dim, 1), two)
            pieces.append(jnp.concatenate([upper, lower], axis=0).astype(bf16))
        attended = jnp.concatenate(pieces, axis=1)
        deep = teams * lanes
        w_hi, w_lo = split_hi_lo(w_buf[part * deep : (part + 1) * deep])
        stream = stream + (mxu(attended, w_hi) + mxu(attended, w_lo))
    centre = jnp.mean(stream, axis=-1, keepdims=True)
    centred = stream - centre
    spread = jnp.mean(centred * centred, axis=-1, keepdims=True)
    normed = centred * lax.rsqrt(spread + eps_norm) * gain_ref[...]
    n_hi, n_lo = split_hi_lo(normed)
    p_hi, p_lo = split_hi_lo(proj_ref[...])
    features = mxu(n_hi, p_lo) + mxu(n_lo, p_hi)
    features = (features + mxu(n_hi, p_hi)).astype(bf16)
    ext_ref[:, GRID : GRID + BLOCK, :] = features.reshape(2, BLOCK, channels)

    def halo(side, f):
        at = (GRID, BLOCK)[side]
        to = (GRID + BLOCK, 0)[side]
        return pltpu.make_async_remote_copy(
            src_ref=ext_ref.at[f, pl.ds(at, GRID)], dst_ref=ext_ref.at[f, pl.ds(to, GRID)],
            send_sem=h_send.at[side, f], recv_sem=h_recv.at[side, f],
            device_id=(above, below)[side], device_id_type=MESH,
        )

    for side in range(2):
        for f in range(2):
            halo(side, f).start()
    for dt, dz in steps:
        copy_to(dt, dz).wait_send()
    for side in range(2):
        for f in range(2):
            halo(side, f).wait()

    blank = jnp.zeros((2, GRID, channels), bf16)

    @pl.when(group == 0)
    def _():
        ext_ref[:, 0:GRID, :] = blank

    @pl.when(group == groups - 1)
    def _():
        ext_ref[:, GRID + BLOCK :, :] = blank


def gather(attended, tokens, out_weight, gain, proj, teams, groups):
    frames, strip, width = tokens.shape
    chips, _, lanes = attended.shape
    channels = proj.shape[1]
    dma = lambda *shape: pltpu.SemaphoreType.DMA(shape)
    vmem = pl.BlockSpec(memory_space=pltpu.VMEM)
    anywhere = pl.BlockSpec(memory_space=pl.ANY)
    return pl.pallas_call(
        functools.partial(gather_kernel, teams, groups),
        in_specs=[vmem, vmem, anywhere, vmem, vmem],
        out_specs=vmem,
        out_shape=jax.ShapeDtypeStruct((frames, strip + 2 * GRID, channels), bf16),
        scratch_shapes=[
            pltpu.VMEM((width, width), f32),
            pltpu.VMEM((chips, BLOCK, lanes), bf16),
            dma(chips // 2), dma(chips), dma(chips), dma(2, 2), dma(2, 2),
        ],
        compiler_params=pltpu.CompilerParams(
            collective_id=1, has_side_effects=True, vmem_limit_bytes=48 << 20
        ),
        name="gather",
    )(attended, tokens.reshape(-1, width), out_weight, gain.reshape(1, width), proj)


def head_kernel(
    token_rows, place, feat_ref, up_ref, conv_ref, bias_ref, out_ref, up_map, act_map, hid_map, flat
):
    channels = feat_ref.shape[-1]
    ext = token_rows + 2
    pixel_cols = 4 * GRID
    feat = feat_ref[0]
    for a in range(4):
        for e in range(4):
            at = (4 * a + e) * channels
            lifted = mxu(feat, up_ref[:, at : at + channels]).astype(bf16)
            for r in range(ext):
                piece = lifted[r * GRID : (r + 1) * GRID]
                up_map[4 * r + a, e * GRID : (e + 1) * GRID, :] = piece
                act_map[4 * r + a, e * GRID : (e + 1) * GRID, :] = jnp.maximum(
                    piece, jnp.zeros((), bf16)
                )

    def conv_rows(source, first, rows, which):
        taps = jnp.concatenate(
            [
                source[pl.ds(first + dy, rows)].reshape(rows * pixel_cols, channels)
                for dy in range(3)
            ],
            axis=1,
        )
        part = []
        for dx in range(3):
            weight = jnp.concatenate([conv_ref[which, dy, dx] for dy in range(3)], axis=0)
            part.append(mxu(taps, weight).reshape(rows, 4, GRID, channels))
        column = lax.broadcasted_iota(jnp.int32, (rows * GRID, channels), 0) % GRID

        def moved(block, step):
            block = block.reshape(rows * GRID, channels)
            turned = pltpu.roll(block, step % (rows * GRID), 0)
            rim = 0 if step > 0 else GRID - 1
            return jnp.where(column == rim, 0.0, turned).reshape(rows, GRID, channels)

        left, centre, right = part
        shifted = []
        for e in range(4):
            low = left[:, e - 1] if e > 0 else moved(left[:, 3], 1)
            high = right[:, e + 1] if e < 3 else moved(right[:, 0], -1)
            shifted.append(low + centre[:, e] + high + bias_ref[which][None, None, :])
        return shifted

    hidden_rows = 4 * token_rows + 2
    group = divisor_upto(hidden_rows, 6)
    top = place[0] == 0
    bottom = place[0] == place[1] - 1
    for g in range(hidden_rows // group):
        pieces = conv_rows(act_map, g * group + 2, group, 0)
        for e in range(4):
            value = jnp.maximum(pieces[e], 0.0).astype(bf16)
            hid_map[g * group : (g + 1) * group, e * GRID : (e + 1) * GRID, :] = value

    @pl.when(top)
    def _():
        hid_map[0] = jnp.zeros((pixel_cols, channels), bf16)

    @pl.when(bottom)
    def _():
        hid_map[hidden_rows - 1] = jnp.zeros((pixel_cols, channels), bf16)

    out_rows = 4 * token_rows
    group2 = divisor_upto(out_rows, 4)
    lanes = 128
    for g in range(out_rows // group2):
        pieces = conv_rows(hid_map, g * group2, group2, 1)
        for r in range(group2):
            y = g * group2 + r
            for e in range(4):
                value = pieces[e][r] + up_map[y + 4, e * GRID : (e + 1) * GRID, :].astype(f32)
                for n in range(channels // lanes):
                    flat[y % 2, n, pl.ds(e, GRID, stride=4), :] = value[:, n * lanes : (n + 1) * lanes]
            for n in range(channels // lanes):
                out_ref[0, y, :, n * lanes : (n + 1) * lanes] = flat[y % 2, n].astype(bf16)


def predict(features, up_weight, conv_weight, conv_bias, place, token_rows):
    frames, ext_tokens, channels = features.shape
    pixel_rows, pixel_cols = 4 * token_rows, 4 * GRID
    once = pl.Buffered(1)
    return pl.pallas_call(
        functools.partial(head_kernel, token_rows),
        grid_spec=pltpu.PrefetchScalarGridSpec(
            num_scalar_prefetch=1,
            grid=(frames,),
            in_specs=[
                pl.BlockSpec((1, ext_tokens, channels), lambda i, *_: (i, 0, 0)),
                pl.BlockSpec(up_weight.shape, lambda i, *_: (0, 0), pipeline_mode=once),
                pl.BlockSpec(conv_weight.shape, lambda i, *_: (0, 0, 0, 0, 0), pipeline_mode=once),
                pl.BlockSpec(conv_bias.shape, lambda i, *_: (0, 0), pipeline_mode=once),
            ],
            out_specs=pl.BlockSpec(
                (1, pixel_rows, pixel_cols, channels), lambda i, *_: (i, 0, 0, 0)
            ),
            scratch_shapes=[
                pltpu.VMEM((pixel_rows + 8, pixel_cols, channels), bf16),
                pltpu.VMEM((pixel_rows + 8, pixel_cols, channels), bf16),
                pltpu.VMEM((pixel_rows + 2, pixel_cols, channels), bf16),
                pltpu.VMEM((2, channels // 128, pixel_cols, 128), f32),
            ],
        ),
        out_shape=jax.ShapeDtypeStruct((frames, pixel_rows, pixel_cols, channels), bf16),
        compiler_params=pltpu.CompilerParams(vmem_limit_bytes=56 << 20),
        name="head",
    )(place, features, up_weight, conv_weight, conv_bias)


def layer_norm(rows, gain):
    centre = jnp.mean(rows, axis=-1, keepdims=True)
    centred = rows - centre
    spread = jnp.mean(centred * centred, axis=-1, keepdims=True)
    return centred * lax.rsqrt(spread + eps_norm) * gain


def by_teams(
    tokens, qkv_weight, out_weight, norm_gain, proj_weight, block_lists, block_counts
):
    local_frames, strip_tokens, model_width = tokens.shape
    head_groups = lax.axis_size("head")
    local_heads = HEADS // head_groups
    head_dim = model_width // HEADS
    own_queries, own_pairs = project(tokens, qkv_weight, head_groups, head_dim)
    queries, all_pairs = exchange(own_queries, own_pairs, head_groups, lax.axis_size("frame"))
    queries = queries.reshape(-1, queries.shape[-1])
    all_pairs = all_pairs.reshape(-1, all_pairs.shape[-1])
    attended = attend(queries, all_pairs, block_lists, block_counts, local_heads, head_dim)
    attended = attended.reshape(local_frames, head_groups, strip_tokens, local_heads * head_dim)
    attended = hand_back(attended).reshape(head_groups, -1, local_heads * head_dim)
    attended = jnp.transpose(attended, (1, 0, 2)).reshape(-1, model_width)
    stream = tokens.reshape(-1, model_width) + jnp.dot(
        attended.astype(f32), out_weight, precision=highest, preferred_element_type=f32
    )
    normed = layer_norm(stream, norm_gain)
    features = jnp.dot(
        normed, proj_weight, precision=highest, preferred_element_type=f32
    ).astype(bf16)
    channels = features.shape[1]
    features = features.reshape(local_frames, strip_tokens, channels)
    forward = [(i, i + 1) for i in range(head_groups - 1)]
    backward = [(i + 1, i) for i in range(head_groups - 1)]
    above = lax.ppermute(features[:, strip_tokens - GRID :], "head", forward)
    below = lax.ppermute(features[:, :GRID], "head", backward)
    return jnp.concatenate([above, features, below], axis=1)


def on_device(
    tokens,
    qkv_weight,
    out_weight,
    norm_gain,
    proj_weight,
    up_weight,
    conv_weight,
    conv_bias,
    block_lists,
    block_counts,
):
    local_frames, strip_tokens, model_width = tokens.shape
    groups, teams = lax.axis_size("head"), lax.axis_size("frame")
    place = jnp.stack([lax.axis_index("head").astype(jnp.int32), jnp.full((), groups, jnp.int32)])
    one_head_a_chip = (
        teams * groups == 2 * HEADS and groups % 4 == 0 and strip_tokens == BLOCK and local_frames == 2
        and model_width == 64 * HEADS
    )
    if one_head_a_chip:
        pairs, queries, lists, counts = scatter(
            tokens, qkv_weight, block_lists, block_counts, teams, groups
        )
        attended = sparse(queries, pairs, lists, counts, teams, groups)
        extended = gather(attended, tokens, out_weight, norm_gain, proj_weight, teams, groups)
    else:
        extended = by_teams(
            tokens, qkv_weight, out_weight, norm_gain, proj_weight, block_lists, block_counts
        )
    return predict(extended, up_weight, conv_weight, conv_bias, place, strip_tokens // GRID)


def solution(mesh):
    in_specs = (
        P("frame", "head", None),
        P(),
        P(),
        P(),
        P(),
        P(),
        P(),
        P(),
        P("frame", None),
        P("frame"),
    )
    out_specs = P("frame", "head", None, None)
    return jax.shard_map(
        on_device, mesh=mesh, in_specs=in_specs, out_specs=out_specs, check_vma=False
    )
```

```python
import functools

import jax
import jax.numpy as jnp
from jax import lax
from jax.experimental import pallas as pl
from jax.experimental.pallas import tpu as pltpu
from jax.sharding import PartitionSpec as P

HEADS = 16
GRID = 32
BLOCK = 128
eps_norm = 1e-05
highest = lax.Precision.HIGHEST
f32 = jnp.float32
bf16 = jnp.bfloat16


def divisor_upto(count, most):
    return max(d for d in range(1, most + 1) if count % d == 0)


def split_hi_lo(value):
    hi = value.astype(bf16)
    return hi, (value - hi.astype(f32)).astype(bf16)


def mxu(a, b):
    return jnp.dot(a, b, preferred_element_type=f32)


def qkv_kernel(local_heads, head_dim, x_ref, w_ref, q_ref, kv_ref, x_hi, x_lo):
    @pl.when(pl.program_id(0) == 0)
    def _():
        hi, lo = split_hi_lo(x_ref[...])
        x_hi[...] = hi
        x_lo[...] = lo

    w_hi, w_lo = split_hi_lo(w_ref[...])
    acc = mxu(x_hi[...], w_lo) + mxu(x_lo[...], w_hi)
    acc = acc + mxu(x_hi[...], w_hi)
    pair = 2 * head_dim
    frames, _, strip, _ = q_ref.shape
    rows = frames * strip
    first = lax.broadcasted_iota(jnp.int32, (rows, pair), 1) < head_dim
    parts = [acc[:, n * pair : (n + 1) * pair] for n in range(3)]
    turned = [pltpu.roll(part, head_dim, 1) for part in parts]

    def coded(value):
        rest = value - value.astype(bf16).astype(f32)
        return jnp.where(first, value, rest).astype(bf16).reshape(frames, strip, pair)

    factor = head_dim ** (-0.5)
    queries = [
        coded(jnp.where(first, parts[0], turned[0]) * factor),
        coded(jnp.where(first, turned[1], parts[1]) * factor),
    ]
    keys = [
        coded(jnp.where(first, turned[0], parts[0])),
        coded(jnp.where(first, parts[2], turned[2])),
    ]
    if local_heads == 2:
        for h in range(2):
            q_ref[:, 0, :, h * pair : (h + 1) * pair] = queries[h]
            kv_ref[:, 0, :, h * pair : (h + 1) * pair] = keys[h]
        values = jnp.where(first, parts[1], parts[2]).astype(bf16)
        kv_ref[:, 0, :, 2 * pair :] = values.reshape(frames, strip, pair)
    else:
        for h, values in enumerate((parts[1], turned[2])):
            q_ref[:, h] = queries[h]
            kv_ref[:, h, :, :pair] = keys[h]
            values = values[:, :head_dim].astype(bf16)
            kv_ref[:, h, :, pair:] = values.reshape(frames, strip, head_dim)


def project(tokens, weight, head_groups, head_dim):
    frames, strip, width = tokens.shape
    local_heads = HEADS // head_groups
    share = 2 // local_heads
    columns = 6 * head_dim
    q_width, kv_width = local_heads * 2 * head_dim, local_heads * 3 * head_dim
    return pl.pallas_call(
        functools.partial(qkv_kernel, local_heads, head_dim),
        grid=(HEADS // 2,),
        in_specs=[
            pl.BlockSpec((frames * strip, width), lambda i: (0, 0)),
            pl.BlockSpec((width, columns), lambda i: (0, i)),
        ],
        out_specs=[
            pl.BlockSpec((frames, share, strip, q_width), lambda i: (0, i, 0, 0)),
            pl.BlockSpec((frames, share, strip, kv_width), lambda i: (0, i, 0, 0)),
        ],
        out_shape=[
            jax.ShapeDtypeStruct((frames, head_groups, strip, q_width), bf16),
            jax.ShapeDtypeStruct((frames, head_groups, strip, kv_width), bf16),
        ],
        scratch_shapes=[pltpu.VMEM((frames * strip, width), bf16)] * 2,
        compiler_params=pltpu.CompilerParams(vmem_limit_bytes=48 << 20),
        name="qkv",
    )(tokens.reshape(-1, width), weight)


MESH = pl.DeviceIdType.MESH


def near_first(count):
    return sorted(range(1, count), key=lambda j: (min(j, count - j), j))


def greet(peers):
    barrier = pltpu.get_barrier_semaphore()
    for peer in peers:
        pl.semaphore_signal(barrier, inc=1, device_id=peer, device_id_type=MESH)
    pl.semaphore_wait(barrier, len(peers))


def exchange_kernel(
    groups, teams, q_ref, kv_ref, q_out, pairs, own_sem,
    q_send, q_recv, z_send, z_recv, f_send, f_recv, r_send, r_recv,
):
    frames = q_ref.shape[0]
    team, me = lax.axis_index("frame"), lax.axis_index("head")
    square = teams == 4
    if square:
        side = lax.rem(team, 2)
        beside, across = team + 1 - 2 * side, lax.rem(team + 2, 4)
        direct = [(beside, beside), (across, across)]
    else:
        direct = [
            (lax.rem(team + k, teams), lax.rem(team + teams - k, teams)) for k in range(1, teams)
        ]
    order = near_first(groups)
    peers = [(team, lax.rem(me + j, groups)) for j in order] + [(to, me) for to, _ in direct]
    greet(peers)

    def remote(src, dst, send, recv, target):
        return pltpu.make_async_remote_copy(
            src_ref=src, dst_ref=dst, send_sem=send, recv_sem=recv,
            device_id=target, device_id_type=MESH,
        )

    def z_copy(f, j):
        to = lax.rem(me + j, groups)
        return remote(
            kv_ref.at[f, to], pairs.at[team * frames + f, me],
            z_send.at[f, j], z_recv.at[f, j], (team, to),
        )

    def q_copy(f, j):
        to = lax.rem(me + j, groups)
        return remote(
            q_ref.at[f, to], q_out.at[f, me], q_send.at[f, j], q_recv.at[f, j], (team, to)
        )

    def piece(owner, f, j):
        return pairs.at[owner * frames + f, lax.rem(me + groups - j, groups)]

    def f_copy(k, f, j):
        src = kv_ref.at[f, me] if j == 0 else piece(team, f, j)
        return remote(
            src, piece(team, f, j), f_send.at[k, f, j], f_recv.at[k, f, j], (direct[k][0], me)
        )

    def r_copy(f, j):
        origin, to = (beside, across) if f % 2 == 0 else (across, beside)
        here = piece(origin, f, j)
        return remote(here, here, r_send.at[f, j], r_recv.at[f, j], (to, me))

    own = []
    for f in range(frames):
        own.append(
            pltpu.make_async_copy(kv_ref.at[f, me], pairs.at[team * frames + f, me], own_sem.at[0, f])
        )
        own.append(pltpu.make_async_copy(q_ref.at[f, me], q_out.at[f, me], own_sem.at[1, f]))
    schedule = [(f, j) for j in [0] + order for f in range(frames)]
    for f, j in schedule:
        if j:
            z_copy(f, j).start()
    for f, j in schedule:
        if j:
            q_copy(f, j).start()
    for copy in own:
        copy.start()
    lag = 2 * frames
    for n in range(len(schedule) + lag):
        if n < len(schedule):
            f, j = schedule[n]
            if j:
                z_copy(f, j).wait_recv()
            for k in range(len(direct)):
                f_copy(k, f, j).start()
        if n >= lag and square:
            f, j = schedule[n - lag]
            f_copy(f % 2, f, j).wait_recv()
            r_copy(f, j).start()
    for f, j in schedule:
        for k in range(len(direct)):
            f_copy(k, f, j).wait_send()
            if not (square and k == f % 2):
                f_copy(k, f, j).wait_recv()
        if square:
            r_copy(f, j).wait()
        if j:
            z_copy(f, j).wait_send()
            q_copy(f, j).wait()
    for copy in own:
        copy.wait()


def exchange(queries, own_pairs, groups, teams):
    frames = queries.shape[0]
    sems = lambda *shape: pltpu.SemaphoreType.DMA(shape)
    hops = 2 if teams == 4 else teams - 1
    vmem = pl.BlockSpec(memory_space=pltpu.VMEM)
    anywhere = pl.BlockSpec(memory_space=pl.ANY)
    return pl.pallas_call(
        functools.partial(exchange_kernel, groups, teams),
        in_specs=[vmem, vmem],
        out_specs=[anywhere, anywhere],
        out_shape=[
            jax.ShapeDtypeStruct(queries.shape, bf16),
            jax.ShapeDtypeStruct((teams * frames,) + own_pairs.shape[1:], bf16),
        ],
        scratch_shapes=[sems(2, frames)]
        + [sems(frames, groups)] * 4
        + [sems(hops, frames, groups)] * 2
        + [sems(frames, groups)] * 2,
        compiler_params=pltpu.CompilerParams(collective_id=0, has_side_effects=True),
        name="exchange",
    )(queries, own_pairs)


def hand_back_kernel(groups, src, dst, own_sem, send, recv):
    team, me = lax.axis_index("frame"), lax.axis_index("head")
    order = near_first(groups)
    greet([(team, lax.rem(me + j, groups)) for j in order])
    copies = []
    for j in reversed(order):
        to = lax.rem(me + j, groups)
        copies.append(
            pltpu.make_async_remote_copy(
                src_ref=src.at[:, to], dst_ref=dst.at[me],
                send_sem=send.at[j], recv_sem=recv.at[j],
                device_id=(team, to), device_id_type=MESH,
            )
        )
    copies.append(pltpu.make_async_copy(src.at[:, me], dst.at[me], own_sem))
    for copy in copies:
        copy.start()
    for copy in copies:
        copy.wait()


def hand_back(attended):
    frames, groups, strip, width = attended.shape
    vmem = pl.BlockSpec(memory_space=pltpu.VMEM)
    return pl.pallas_call(
        functools.partial(hand_back_kernel, groups),
        in_specs=[vmem],
        out_specs=vmem,
        out_shape=jax.ShapeDtypeStruct((groups, frames, strip, width), bf16),
        scratch_shapes=[pltpu.SemaphoreType.DMA] + [pltpu.SemaphoreType.DMA((groups,))] * 2,
        compiler_params=pltpu.CompilerParams(collective_id=1, has_side_effects=True),
        name="hand_back",
    )(attended)


def attend_kernel(local_heads, head_dim, span, lists, counts, q_ref, kv_ref, o_ref):
    b = pl.program_id(0)
    count = counts[b]
    pair = 2 * head_dim
    v_at = local_heads * pair
    v_width = local_heads * head_dim
    first = lax.broadcasted_iota(jnp.int32, (BLOCK, pair), 1) < head_dim
    stacked = []
    for h in range(local_heads):
        coded = q_ref[:, h * pair : (h + 1) * pair].astype(f32)
        turned = pltpu.roll(coded, head_dim, 1)
        high, low = jnp.where(first, coded, turned), jnp.where(first, turned, coded)
        stacked.append(jnp.concatenate([high, low], axis=0).astype(bf16))

    def chunk(c, carry):
        offsets = []
        valid = []
        for t in range(span):
            slot = c * span + t
            block = lists[b, jnp.minimum(slot, count - 1)]
            offsets.append(pl.multiple_of(block * BLOCK, BLOCK))
            valid.append(slot < count)
        values = jnp.concatenate(
            [kv_ref[pl.ds(at, BLOCK), v_at : v_at + v_width] for at in offsets], axis=0
        )
        out = []
        for h in range(local_heads):
            top, total, blend = carry[h]
            scores = []
            for at, ok in zip(offsets, valid):
                keys = kv_ref[pl.ds(at, BLOCK), h * pair : (h + 1) * pair]
                both = lax.dot_general(
                    stacked[h], keys, (((1,), (1,)), ((), ())), preferred_element_type=f32
                )
                scores.append(jnp.where(ok, both[:BLOCK] + both[BLOCK:], -jnp.inf))
            peak = functools.reduce(jnp.maximum, scores)
            new_top = jnp.maximum(top, jnp.max(peak, axis=1, keepdims=True))
            scale = jnp.exp(top - new_top)
            weights = [jnp.exp(s - new_top) for s in scores]
            total = total * scale + functools.reduce(jnp.add, weights)
            packed = jnp.concatenate([w.astype(bf16) for w in weights], axis=1)
            blend = blend * scale + mxu(packed, values)
            out.append((new_top, total, blend))
        return tuple(out)

    start = tuple(
        (
            jnp.full((BLOCK, 1), -jnp.inf, f32),
            jnp.zeros((BLOCK, BLOCK), f32),
            jnp.zeros((BLOCK, v_width), f32),
        )
        for _ in range(local_heads)
    )
    final = lax.fori_loop(0, (count + span - 1) // span, chunk, start)
    owner = lax.broadcasted_iota(jnp.int32, (BLOCK, v_width), 1) // head_dim
    result = jnp.zeros((BLOCK, v_width), f32)
    for h in range(local_heads):
        _, total, blend = final[h]
        ready = blend / jnp.sum(total, axis=1, keepdims=True)
        result = jnp.where(owner == h, ready, result)
    o_ref[...] = result.astype(bf16)


def attend(queries, pairs, lists, counts, local_heads, head_dim):
    blocks, slots = lists.shape
    span = -(-slots // (-(-slots // 7)))
    width = local_heads * head_dim
    return pl.pallas_call(
        functools.partial(attend_kernel, local_heads, head_dim, span),
        grid_spec=pltpu.PrefetchScalarGridSpec(
            num_scalar_prefetch=2,
            grid=(blocks,),
            in_specs=[
                pl.BlockSpec((BLOCK, queries.shape[1]), lambda i, *_: (i, 0)),
                pl.BlockSpec(pairs.shape, lambda i, *_: (0, 0), pipeline_mode=pl.Buffered(1)),
            ],
            out_specs=pl.BlockSpec((BLOCK, width), lambda i, *_: (i, 0)),
        ),
        out_shape=jax.ShapeDtypeStruct((blocks * BLOCK, width), bf16),
        compiler_params=pltpu.CompilerParams(vmem_limit_bytes=48 << 20),
        name="attend",
    )(lists, counts, queries, pairs)


def scatter_order(teams, halves, k):
    far = halves - 1 - lax.rem(k, halves)
    turn = lax.rem(k // halves + 1 + 2 * far, teams)
    return turn, far


def scatter_kernel(
    teams, groups, head_dim, x_ref, w_hbm, lists_ref, counts_ref,
    kv_out, q_out, lists_out, counts_out,
    w_buf, x_hi, x_lo, msg, msg_scale, got, got_scale, kv_dec, q_dec,
    w_sem, m_send, m_recv, s_send, s_recv, kv_sem, q_sem, f_send, f_recv, l_own, l_send, l_recv,
):
    planes = groups // 2
    halves = planes // 2
    pairs = teams * halves
    chips = teams * planes
    columns = 6 * head_dim
    lanes = 2 * head_dim
    rows = x_ref.shape[0]
    team, group = lax.axis_index("frame"), lax.axis_index("head")
    plane, core = group // 2, lax.rem(group, 2)
    half, parity = plane // 2, lax.rem(plane, 2)
    me = team * planes + plane
    sibling = (team, group + 1 - 2 * core)

    def place(k):
        turn, far = scatter_order(teams, halves, k)
        return lax.rem(team + turn, teams), lax.rem(half + far, halves)

    def weight(k):
        to_team, to_half = place(k)
        at = pl.multiple_of((to_team * halves + to_half) * columns, columns)
        return pltpu.make_async_copy(w_hbm.at[:, pl.ds(at, columns)], w_buf.at[k], w_sem.at[k])

    for k in range(pairs):
        weight(k).start()

    barrier = pltpu.get_barrier_semaphore()
    for step in range(1, chips):
        dt, dz = step // planes, step % planes
        peer = (lax.rem(team + dt, teams), lax.rem(plane + dz, planes) * 2 + core)
        pl.semaphore_signal(barrier, inc=1, device_id=peer, device_id_type=MESH)
    pl.semaphore_signal(barrier, inc=1, device_id=sibling, device_id_type=MESH)

    hi, lo = split_hi_lo(x_ref[...])
    x_hi[...] = hi
    x_lo[...] = lo
    first = lax.broadcasted_iota(jnp.int32, (rows, lanes), 1) < head_dim
    lane = lax.broadcasted_iota(jnp.int32, (BLOCK, lanes), 1)
    top = 32766.0

    pl.semaphore_wait(barrier, chips)

    def list_copies(step):
        to = lax.rem(team + step, teams)
        out = []
        for n, (src, dst) in enumerate(((lists_ref, lists_out), (counts_ref, counts_out))):
            out.append(
                pltpu.make_async_remote_copy(
                    src_ref=src, dst_ref=dst.at[team],
                    send_sem=l_send.at[n, step], recv_sem=l_recv.at[n, step],
                    device_id=(to, group), device_id_type=MESH,
                )
            )
        return out

    own_lists = [
        pltpu.make_async_copy(lists_ref, lists_out.at[team], l_own.at[0]),
        pltpu.make_async_copy(counts_ref, counts_out.at[team], l_own.at[1]),
    ]
    for copy in own_lists:
        copy.start()
    for step in range(1, teams):
        for copy in list_copies(step):
            copy.start()

    def message(to_team, to_plane):
        to = to_team * planes + to_plane
        target = (to_team, to_plane * 2 + core)
        return [
            pltpu.make_async_remote_copy(
                src_ref=msg.at[to], dst_ref=got.at[me],
                send_sem=m_send.at[to], recv_sem=m_recv.at[me],
                device_id=target, device_id_type=MESH,
            ),
            pltpu.make_async_remote_copy(
                src_ref=msg_scale.at[to], dst_ref=got_scale.at[me],
                send_sem=s_send.at[to], recv_sem=s_recv.at[me],
                device_id=target, device_id_type=MESH,
            ),
        ]

    def peak(value):
        return jnp.maximum(jnp.max(jnp.abs(value), axis=1, keepdims=True), 1e-30)

    def send_step(k, carry):
        weight(k).wait()
        w_hi, w_lo = split_hi_lo(w_buf[k])
        acc = mxu(x_hi[...], w_lo) + mxu(x_lo[...], w_hi)
        acc = acc + mxu(x_hi[...], w_hi)
        p0, p1, p2 = [acc[:, n * lanes : (n + 1) * lanes] for n in range(3)]
        t0, t1 = pltpu.roll(p0, head_dim, 1), pltpu.roll(p1, head_dim, 1)
        key_value = [jnp.where(first, t0, t1), p2]
        up, down = slice(0, BLOCK), slice(BLOCK, 2 * BLOCK)
        query = [
            jnp.where(first[up], p0[up], t0[down]),
            jnp.where(first[up], t1[up], p1[down]),
        ]
        to_team, to_half = place(k)
        for i in range(2):
            to_plane = to_half * 2 + i
            to = to_team * planes + to_plane
            kv, q = key_value[i], query[i]
            peak_k = peak(jnp.where(first, kv, 0.0))
            peak_v = peak(jnp.where(first, 0.0, kv))
            peak_q0 = peak(jnp.where(first[up], q, 0.0))
            peak_q1 = peak(jnp.where(first[up], 0.0, q))
            kv = kv * jnp.where(first, top / peak_k, top / peak_v)
            q = q * jnp.where(first[up], top / peak_q0, top / peak_q1)
            msg[to, 0:2] = jnp.round(kv).astype(jnp.int32).astype(jnp.int16).reshape(2, BLOCK, lanes)
            msg[to, 2] = jnp.round(q).astype(jnp.int32).astype(jnp.int16)
            columns_of = [peak_k[up], peak_k[down], peak_v[up], peak_v[down], peak_q0, peak_q1]
            table = jnp.zeros((BLOCK, lanes), f32)
            for n, column in enumerate(columns_of):
                table = jnp.where(lane == n, column * (1.0 / top), table)
            msg_scale[to] = jnp.transpose(table)[:8]

            @pl.when(to != me)
            def _():
                for copy in message(to_team, to_plane):
                    copy.start()

            @pl.when(to == me)
            def _():
                got[to] = msg[to]
                got_scale[to] = msg_scale[to]

        return carry

    lax.fori_loop(0, pairs, send_step, 0)

    factor = head_dim ** (-0.5) * 1.4426950408889634

    def source(n):
        far = n // (2 * teams)
        turn = lax.rem(lax.rem(n, 2 * teams) // 2 + 1 + 2 * far, teams)
        from_team = lax.rem(team + teams - turn, teams)
        from_plane = lax.rem(half + halves - far, halves) * 2 + lax.rem(parity + 1 + n, 2)
        return from_team, from_plane

    def arrival(src):
        return [
            pltpu.make_async_remote_copy(
                src_ref=msg.at[src], dst_ref=got.at[src],
                send_sem=m_send.at[src], recv_sem=m_recv.at[src],
                device_id=sibling, device_id_type=MESH,
            ),
            pltpu.make_async_remote_copy(
                src_ref=msg_scale.at[src], dst_ref=got_scale.at[src],
                send_sem=s_send.at[src], recv_sem=s_recv.at[src],
                device_id=sibling, device_id_type=MESH,
            ),
        ]

    def handing(from_team, from_plane):
        src = from_team * planes + from_plane
        piece = kv_out.at[from_team, :, from_plane * 2 + core]
        return [
            pltpu.make_async_copy(kv_dec.at[src], piece, kv_sem.at[src]),
            pltpu.make_async_copy(q_dec.at[src], q_out.at[src], q_sem.at[src]),
        ]

    def forward(from_team, from_plane):
        src = from_team * planes + from_plane
        piece = kv_out.at[from_team, :, from_plane * 2 + core]
        return pltpu.make_async_remote_copy(
            src_ref=kv_dec.at[src], dst_ref=piece,
            send_sem=f_send.at[src], recv_sem=f_recv.at[src],
            device_id=sibling, device_id_type=MESH,
        )

    def take_step(n, carry):
        from_team, from_plane = source(n)
        src = from_team * planes + from_plane

        @pl.when(src != me)
        def _():
            for copy in arrival(src):
                copy.wait_recv()

        scale = jnp.transpose(jnp.concatenate([got_scale[src]] * (BLOCK // 8), axis=0))
        near = lane < head_dim
        for f in range(2):
            kv = got[src, f].astype(jnp.int32).astype(f32)
            kv = kv * jnp.where(near, scale[:, f : f + 1], scale[:, 2 + f : 3 + f])
            high = kv.astype(bf16).astype(f32)
            low = pltpu.roll(kv - high, head_dim, 1)
            kv_dec[src, f, :, :lanes] = jnp.where(near, high, low).astype(bf16)
            value = jnp.where(near, pltpu.roll(kv, head_dim, 1), 1.0)
            kv_dec[src, f, :, lanes:] = value.astype(bf16)
        q = got[src, 2].astype(jnp.int32).astype(f32)
        q = q * (factor * jnp.where(near, scale[:, 4:5], scale[:, 5:6]))
        high = q.astype(bf16).astype(f32)
        low = q - high
        high_turned, low_turned = pltpu.roll(high, head_dim, 1), pltpu.roll(low, head_dim, 1)
        q_dec[src, 0, :, :lanes] = jnp.where(near, high, high_turned).astype(bf16)
        q_dec[src, 0, :, lanes:] = jnp.where(near, low, low_turned).astype(bf16)
        q_dec[src, 1, :, :lanes] = jnp.where(near, high_turned, high).astype(bf16)
        q_dec[src, 1, :, lanes:] = jnp.where(near, low_turned, low).astype(bf16)
        forward(from_team, from_plane).start()
        for copy in handing(from_team, from_plane):
            copy.start()
        return carry

    lax.fori_loop(0, chips, take_step, 0)

    def end_step(n, carry):
        from_team, from_plane = source(n)
        src = from_team * planes + from_plane

        @pl.when(src != me)
        def _():
            for copy in arrival(src):
                copy.wait_send()

        copy = forward(from_team, from_plane)
        copy.wait_send()
        copy.wait_recv()
        for copy in handing(from_team, from_plane):
            copy.wait()
        return carry

    lax.fori_loop(0, chips, end_step, 0)
    for copy in own_lists:
        copy.wait()
    for step in range(1, teams):
        for copy in list_copies(step):
            copy.wait()


def scatter(tokens, weight, lists, counts, teams, groups):
    frames, strip, width = tokens.shape
    head_dim = width // HEADS
    lanes = 2 * head_dim
    rows = frames * strip
    chips = HEADS
    pairs = HEADS // 2
    dma = lambda *shape: pltpu.SemaphoreType.DMA(shape)
    vmem = pl.BlockSpec(memory_space=pltpu.VMEM)
    anywhere = pl.BlockSpec(memory_space=pl.ANY)
    return pl.pallas_call(
        functools.partial(scatter_kernel, teams, groups, head_dim),
        in_specs=[vmem, anywhere, pl.BlockSpec(memory_space=pltpu.HBM), pl.BlockSpec(memory_space=pltpu.HBM)],
        out_specs=[anywhere] * 4,
        out_shape=[
            jax.ShapeDtypeStruct((teams, frames, groups, BLOCK, 2 * lanes), bf16),
            jax.ShapeDtypeStruct((chips, frames, BLOCK, 2 * lanes), bf16),
            jax.ShapeDtypeStruct((teams,) + lists.shape, jnp.int32),
            jax.ShapeDtypeStruct((teams,) + counts.shape, jnp.int32),
        ],
        scratch_shapes=[
            pltpu.VMEM((pairs, width, 6 * head_dim), f32),
            pltpu.VMEM((rows, width), bf16),
            pltpu.VMEM((rows, width), bf16),
            pltpu.VMEM((chips, 3, BLOCK, lanes), jnp.int16),
            pltpu.VMEM((chips, 8, BLOCK), f32),
            pltpu.VMEM((chips, 3, BLOCK, lanes), jnp.int16),
            pltpu.VMEM((chips, 8, BLOCK), f32),
            pltpu.VMEM((chips, frames, BLOCK, 2 * lanes), bf16),
            pltpu.VMEM((chips, frames, BLOCK, 2 * lanes), bf16),
            dma(pairs),
        ]
        + [dma(chips)] * 8
        + [dma(2), dma(2, teams), dma(2, teams)],
        compiler_params=pltpu.CompilerParams(
            collective_id=0, has_side_effects=True, vmem_limit_bytes=48 << 20
        ),
        name="scatter",
    )(tokens.reshape(rows, width), weight, lists, counts)


def blend_kernel(
    teams, groups, slots, lists, counts, q_hbm, kv_hbm, x_hbm, w_hbm, gain_ref, proj_ref, ext_ref,
    q_ref, kv_ref, stream, w_buf, ready, sent, got, l_sem, a_send, a_recv, h_send, h_recv,
):
    planes = groups // 2
    chips = teams * planes
    team, group = lax.axis_index("frame"), lax.axis_index("head")
    plane, core = group // 2, lax.rem(group, 2)
    me = team * planes + plane
    lanes = sent.shape[-1]
    head_dim = lanes // 2
    deep = planes * head_dim
    channels = proj_ref.shape[-1]
    loads = [
        pltpu.make_async_copy(src, dst, l_sem.at[n])
        for n, (src, dst) in enumerate(
            [(kv_hbm, kv_ref), (q_hbm, q_ref), (x_hbm, stream), (w_hbm, w_buf)]
        )
    ]
    for copy in loads:
        copy.start()

    above = (team, lax.rem(group + groups - 1, groups))
    below = (team, lax.rem(group + 1, groups))
    barrier = pltpu.get_barrier_semaphore()
    for n in range(1, chips):
        peer = (lax.rem(team + n // planes, teams), lax.rem(plane + n % planes, planes) * 2 + core)
        pl.semaphore_signal(barrier, inc=1, device_id=peer, device_id_type=MESH)
    for peer in (above, below):
        pl.semaphore_signal(barrier, inc=1, device_id=peer, device_id_type=MESH)
    loads[0].wait()
    loads[1].wait()
    pl.semaphore_wait(barrier, chips + 1)

    near = lax.broadcasted_iota(jnp.int32, (BLOCK, lanes), 1) < head_dim

    def copy_to(to_team, to_plane):
        to = to_team * planes + to_plane
        return pltpu.make_async_remote_copy(
            src_ref=sent.at[to], dst_ref=got.at[me],
            send_sem=a_send.at[to], recv_sem=a_recv.at[me],
            device_id=(to_team, to_plane * 2 + core), device_id_type=MESH,
        )

    def arrival(src):
        return pltpu.make_async_remote_copy(
            src_ref=sent.at[src], dst_ref=got.at[src],
            send_sem=a_send.at[src], recv_sem=a_recv.at[src],
            device_id=below, device_id_type=MESH,
        )

    def attend_frame(to_team, f):
        scores, values = [], []
        for i in range(planes):
            row = f * groups + i * 2 + core
            count = counts[to_team, row]
            query = q_ref[to_team * planes + i, f]
            for slot in range(slots):
                block = lists[to_team, row, slot]
                keys = kv_ref[block, :, :lanes]
                score = lax.dot_general(
                    query, jnp.concatenate([keys, keys], axis=1), (((1,), (1,)), ((), ())),
                    preferred_element_type=f32,
                )
                scores.append(score if slot == 0 else jnp.where(slot < count, score, -jnp.inf))
                values.append(kv_ref[block, :, lanes:])
        for i in range(planes):
            own = slice(i * slots, (i + 1) * slots)
            peak = jnp.max(functools.reduce(jnp.maximum, scores[own]), axis=1, keepdims=True)
            packed = jnp.concatenate([jnp.exp2(s - peak).astype(bf16) for s in scores[own]], axis=1)
            total = mxu(packed, jnp.concatenate(values[own], axis=0))
            ready[f, i] = total / total[:, head_dim : head_dim + 1]

    def attend_team(k):
        to_team = lax.rem(team + k, teams)
        for f in range(2):
            attend_frame(to_team, f)
        for i in range(planes):
            to = to_team * planes + i
            both = jnp.where(near, ready[0, i], pltpu.roll(ready[1, i], head_dim, 1)).astype(bf16)
            sent[to] = both

            @pl.when(to != me)
            def _():
                copy_to(to_team, i).start()

            @pl.when(to == me)
            def _():
                got[to] = both

    def absorb(k):
        from_team = lax.rem(team + teams - k, teams)
        pieces = []
        for i in range(0, planes, 2):
            at = from_team * planes + i
            for j in range(2):
                @pl.when(at + j != me)
                def _():
                    arrival(at + j).wait_recv()

            one, two = got[at].astype(f32), got[at + 1].astype(f32)
            upper = jnp.where(near, one, pltpu.roll(two, head_dim, 1))
            lower = jnp.where(near, pltpu.roll(one, head_dim, 1), two)
            pieces.append(jnp.concatenate([upper, lower], axis=0).astype(bf16))
        attended = jnp.concatenate(pieces, axis=1)
        rows = pl.ds(pl.multiple_of(from_team * deep, deep), deep)
        w_hi, w_lo = split_hi_lo(w_buf[rows, :])
        stream[...] += mxu(attended, w_hi) + mxu(attended, w_lo)

    attend_team(1)
    loads[2].wait()
    loads[3].wait()

    def team_step(k, carry):
        attend_team(k)
        absorb(k - 1)
        return carry

    lax.fori_loop(2, teams + 1, team_step, 0)
    absorb(teams)

    rows = stream[...]
    centre = jnp.mean(rows, axis=-1, keepdims=True)
    centred = rows - centre
    spread = jnp.mean(centred * centred, axis=-1, keepdims=True)
    normed = centred * lax.rsqrt(spread + eps_norm) * gain_ref[...]
    n_hi, n_lo = split_hi_lo(normed)
    p_hi, p_lo = split_hi_lo(proj_ref[...])
    features = mxu(n_hi, p_lo) + mxu(n_lo, p_hi)
    features = (features + mxu(n_hi, p_hi)).astype(bf16)
    ext_ref[:, GRID : GRID + BLOCK, :] = features.reshape(2, BLOCK, channels)

    def halo(side, f):
        at = (GRID, BLOCK)[side]
        to = (GRID + BLOCK, 0)[side]
        return pltpu.make_async_remote_copy(
            src_ref=ext_ref.at[f, pl.ds(at, GRID)], dst_ref=ext_ref.at[f, pl.ds(to, GRID)],
            send_sem=h_send.at[side, f], recv_sem=h_recv.at[side, f],
            device_id=(above, below)[side], device_id_type=MESH,
        )

    for side in range(2):
        for f in range(2):
            halo(side, f).start()
    for n in range(1, chips):
        to_team, to_plane = lax.rem(team + n // planes, teams), lax.rem(plane + n % planes, planes)
        copy_to(to_team, to_plane).wait_send()
    for side in range(2):
        for f in range(2):
            halo(side, f).wait()

    blank = jnp.zeros((2, GRID, channels), bf16)

    @pl.when(group == 0)
    def _():
        ext_ref[:, 0:GRID, :] = blank

    @pl.when(group == groups - 1)
    def _():
        ext_ref[:, GRID + BLOCK :, :] = blank


def blend(queries, pairs, lists, counts, tokens, out_weight, gain, proj, teams, groups):
    frames, strip, width = tokens.shape
    chips, _, _, wide = queries.shape
    lanes = wide // 2
    rows = frames * strip
    pairs = pairs.reshape(-1, BLOCK, wide)
    slots = lists.shape[-1]
    channels = proj.shape[1]
    dma = lambda *shape: pltpu.SemaphoreType.DMA(shape)
    smem = pl.BlockSpec(memory_space=pltpu.SMEM)
    vmem = pl.BlockSpec(memory_space=pltpu.VMEM)
    anywhere = pl.BlockSpec(memory_space=pl.ANY)
    return pl.pallas_call(
        functools.partial(blend_kernel, teams, groups, slots),
        in_specs=[smem, smem, anywhere, anywhere, anywhere, anywhere, vmem, vmem],
        out_specs=vmem,
        out_shape=jax.ShapeDtypeStruct((frames, strip + 2 * GRID, channels), bf16),
        scratch_shapes=[
            pltpu.VMEM(queries.shape, bf16),
            pltpu.VMEM(pairs.shape, bf16),
            pltpu.VMEM((rows, width), f32),
            pltpu.VMEM((width, width), f32),
            pltpu.VMEM((2, chips // teams, BLOCK, lanes), f32),
            pltpu.VMEM((chips, BLOCK, lanes), bf16),
            pltpu.VMEM((chips, BLOCK, lanes), bf16),
            dma(4), dma(chips), dma(chips), dma(2, 2), dma(2, 2),
        ],
        compiler_params=pltpu.CompilerParams(
            collective_id=1, has_side_effects=True, vmem_limit_bytes=48 << 20
        ),
        name="blend",
    )(lists, counts, queries, pairs, tokens.reshape(rows, width), out_weight, gain.reshape(1, width), proj)


def head_kernel(
    token_rows, feat_ref, up_ref, conv_ref, bias_ref, out_ref, up_map, act_map, hid_map, flat
):
    channels = feat_ref.shape[-1]
    ext = token_rows + 2
    pixel_cols = 4 * GRID
    feat = feat_ref[0]
    for a in range(4):
        for e in range(4):
            at = (4 * a + e) * channels
            lifted = mxu(feat, up_ref[:, at : at + channels]).astype(bf16)
            for r in range(ext):
                piece = lifted[r * GRID : (r + 1) * GRID]
                up_map[4 * r + a, e * GRID : (e + 1) * GRID, :] = piece
                act_map[4 * r + a, e * GRID : (e + 1) * GRID, :] = jnp.maximum(
                    piece, jnp.zeros((), bf16)
                )

    def conv_rows(source, first, rows, which):
        taps = jnp.concatenate(
            [
                source[pl.ds(first + dy, rows)].reshape(rows * pixel_cols, channels)
                for dy in range(3)
            ],
            axis=1,
        )
        part = []
        for dx in range(3):
            weight = jnp.concatenate([conv_ref[which, dy, dx] for dy in range(3)], axis=0)
            part.append(mxu(taps, weight).reshape(rows, 4, GRID, channels))
        column = lax.broadcasted_iota(jnp.int32, (rows * GRID, channels), 0) % GRID

        def moved(block, step):
            block = block.reshape(rows * GRID, channels)
            turned = pltpu.roll(block, step % (rows * GRID), 0)
            rim = 0 if step > 0 else GRID - 1
            return jnp.where(column == rim, 0.0, turned).reshape(rows, GRID, channels)

        left, centre, right = part
        shifted = []
        for e in range(4):
            low = left[:, e - 1] if e > 0 else moved(left[:, 3], 1)
            high = right[:, e + 1] if e < 3 else moved(right[:, 0], -1)
            shifted.append(low + centre[:, e] + high + bias_ref[which][None, None, :])
        return shifted

    hidden_rows = 4 * token_rows + 2
    group = divisor_upto(hidden_rows, 6)
    top = lax.axis_index("head") == 0
    bottom = lax.axis_index("head") == lax.axis_size("head") - 1
    for g in range(hidden_rows // group):
        pieces = conv_rows(act_map, g * group + 2, group, 0)
        for e in range(4):
            value = jnp.maximum(pieces[e], 0.0).astype(bf16)
            hid_map[g * group : (g + 1) * group, e * GRID : (e + 1) * GRID, :] = value

    @pl.when(top)
    def _():
        hid_map[0] = jnp.zeros((pixel_cols, channels), bf16)

    @pl.when(bottom)
    def _():
        hid_map[hidden_rows - 1] = jnp.zeros((pixel_cols, channels), bf16)

    out_rows = 4 * token_rows
    group2 = divisor_upto(out_rows, 4)
    lanes = 128
    for g in range(out_rows // group2):
        pieces = conv_rows(hid_map, g * group2, group2, 1)
        for r in range(group2):
            y = g * group2 + r
            for e in range(4):
                value = pieces[e][r] + up_map[y + 4, e * GRID : (e + 1) * GRID, :].astype(f32)
                for n in range(channels // lanes):
                    flat[y % 2, n, pl.ds(e, GRID, stride=4), :] = value[:, n * lanes : (n + 1) * lanes]
            for n in range(channels // lanes):
                out_ref[0, y, :, n * lanes : (n + 1) * lanes] = flat[y % 2, n].astype(bf16)


def predict(features, up_weight, conv_weight, conv_bias, token_rows):
    frames, ext_tokens, channels = features.shape
    pixel_rows, pixel_cols = 4 * token_rows, 4 * GRID
    once = pl.Buffered(1)
    return pl.pallas_call(
        functools.partial(head_kernel, token_rows),
        grid_spec=pltpu.PrefetchScalarGridSpec(
            num_scalar_prefetch=0,
            grid=(frames,),
            in_specs=[
                pl.BlockSpec((1, ext_tokens, channels), lambda i, *_: (i, 0, 0)),
                pl.BlockSpec(up_weight.shape, lambda i, *_: (0, 0), pipeline_mode=once),
                pl.BlockSpec(conv_weight.shape, lambda i, *_: (0, 0, 0, 0, 0), pipeline_mode=once),
                pl.BlockSpec(conv_bias.shape, lambda i, *_: (0, 0), pipeline_mode=once),
            ],
            out_specs=pl.BlockSpec(
                (1, pixel_rows, pixel_cols, channels), lambda i, *_: (i, 0, 0, 0)
            ),
            scratch_shapes=[
                pltpu.VMEM((pixel_rows + 8, pixel_cols, channels), bf16),
                pltpu.VMEM((pixel_rows + 8, pixel_cols, channels), bf16),
                pltpu.VMEM((pixel_rows + 2, pixel_cols, channels), bf16),
                pltpu.VMEM((2, channels // 128, pixel_cols, 128), f32),
            ],
        ),
        out_shape=jax.ShapeDtypeStruct((frames, pixel_rows, pixel_cols, channels), bf16),
        compiler_params=pltpu.CompilerParams(vmem_limit_bytes=56 << 20),
        name="head",
    )(features, up_weight, conv_weight, conv_bias)


def layer_norm(rows, gain):
    centre = jnp.mean(rows, axis=-1, keepdims=True)
    centred = rows - centre
    spread = jnp.mean(centred * centred, axis=-1, keepdims=True)
    return centred * lax.rsqrt(spread + eps_norm) * gain


def by_teams(
    tokens, qkv_weight, out_weight, norm_gain, proj_weight, block_lists, block_counts
):
    local_frames, strip_tokens, model_width = tokens.shape
    head_groups = lax.axis_size("head")
    local_heads = HEADS // head_groups
    head_dim = model_width // HEADS
    own_queries, own_pairs = project(tokens, qkv_weight, head_groups, head_dim)
    queries, all_pairs = exchange(own_queries, own_pairs, head_groups, lax.axis_size("frame"))
    queries = queries.reshape(-1, queries.shape[-1])
    all_pairs = all_pairs.reshape(-1, all_pairs.shape[-1])
    attended = attend(queries, all_pairs, block_lists, block_counts, local_heads, head_dim)
    attended = attended.reshape(local_frames, head_groups, strip_tokens, local_heads * head_dim)
    attended = hand_back(attended).reshape(head_groups, -1, local_heads * head_dim)
    attended = jnp.transpose(attended, (1, 0, 2)).reshape(-1, model_width)
    stream = tokens.reshape(-1, model_width) + jnp.dot(
        attended.astype(f32), out_weight, precision=highest, preferred_element_type=f32
    )
    normed = layer_norm(stream, norm_gain)
    features = jnp.dot(
        normed, proj_weight, precision=highest, preferred_element_type=f32
    ).astype(bf16)
    channels = features.shape[1]
    features = features.reshape(local_frames, strip_tokens, channels)
    forward = [(i, i + 1) for i in range(head_groups - 1)]
    backward = [(i + 1, i) for i in range(head_groups - 1)]
    above = lax.ppermute(features[:, strip_tokens - GRID :], "head", forward)
    below = lax.ppermute(features[:, :GRID], "head", backward)
    return jnp.concatenate([above, features, below], axis=1)


def on_device(
    tokens,
    qkv_weight,
    out_weight,
    norm_gain,
    proj_weight,
    up_weight,
    conv_weight,
    conv_bias,
    block_lists,
    block_counts,
):
    local_frames, strip_tokens, model_width = tokens.shape
    groups, teams = lax.axis_size("head"), lax.axis_size("frame")
    one_head_a_chip = (
        teams * groups == 2 * HEADS and groups % 4 == 0 and strip_tokens == BLOCK and local_frames == 2
        and model_width == 64 * HEADS
    )
    if one_head_a_chip:
        pairs, queries, lists, counts = scatter(
            tokens, qkv_weight, block_lists, block_counts, teams, groups
        )
        extended = blend(
            queries, pairs, lists, counts, tokens, out_weight, norm_gain, proj_weight, teams, groups
        )
    else:
        extended = by_teams(
            tokens, qkv_weight, out_weight, norm_gain, proj_weight, block_lists, block_counts
        )
    return predict(extended, up_weight, conv_weight, conv_bias, strip_tokens // GRID)


def solution(mesh):
    in_specs = (
        P("frame", "head", None),
        P(),
        P(),
        P(),
        P(),
        P(),
        P(),
        P(),
        P("frame", None),
        P("frame"),
    )
    out_specs = P("frame", "head", None, None)
    return jax.shard_map(
        on_device, mesh=mesh, in_specs=in_specs, out_specs=out_specs, check_vma=False
    )
```

```python
import functools

import jax
import jax.numpy as jnp
from jax import lax
from jax.experimental import pallas as pl
from jax.experimental.pallas import tpu as pltpu
from jax.sharding import PartitionSpec as P

HEADS = 16
GRID = 32
BLOCK = 128
eps_norm = 1e-05
highest = lax.Precision.HIGHEST
f32 = jnp.float32
bf16 = jnp.bfloat16


def divisor_upto(count, most):
    return max(d for d in range(1, most + 1) if count % d == 0)


def split_hi_lo(value):
    hi = value.astype(bf16)
    return hi, (value - hi.astype(f32)).astype(bf16)


def mxu(a, b):
    return jnp.dot(a, b, preferred_element_type=f32)


def qkv_kernel(local_heads, head_dim, x_ref, w_ref, q_ref, kv_ref, x_hi, x_lo):
    @pl.when(pl.program_id(0) == 0)
    def _():
        hi, lo = split_hi_lo(x_ref[...])
        x_hi[...] = hi
        x_lo[...] = lo

    w_hi, w_lo = split_hi_lo(w_ref[...])
    acc = mxu(x_hi[...], w_lo) + mxu(x_lo[...], w_hi)
    acc = acc + mxu(x_hi[...], w_hi)
    pair = 2 * head_dim
    frames, _, strip, _ = q_ref.shape
    rows = frames * strip
    first = lax.broadcasted_iota(jnp.int32, (rows, pair), 1) < head_dim
    parts = [acc[:, n * pair : (n + 1) * pair] for n in range(3)]
    turned = [pltpu.roll(part, head_dim, 1) for part in parts]

    def coded(value):
        rest = value - value.astype(bf16).astype(f32)
        return jnp.where(first, value, rest).astype(bf16).reshape(frames, strip, pair)

    factor = head_dim ** (-0.5)
    queries = [
        coded(jnp.where(first, parts[0], turned[0]) * factor),
        coded(jnp.where(first, turned[1], parts[1]) * factor),
    ]
    keys = [
        coded(jnp.where(first, turned[0], parts[0])),
        coded(jnp.where(first, parts[2], turned[2])),
    ]
    if local_heads == 2:
        for h in range(2):
            q_ref[:, 0, :, h * pair : (h + 1) * pair] = queries[h]
            kv_ref[:, 0, :, h * pair : (h + 1) * pair] = keys[h]
        values = jnp.where(first, parts[1], parts[2]).astype(bf16)
        kv_ref[:, 0, :, 2 * pair :] = values.reshape(frames, strip, pair)
    else:
        for h, values in enumerate((parts[1], turned[2])):
            q_ref[:, h] = queries[h]
            kv_ref[:, h, :, :pair] = keys[h]
            values = values[:, :head_dim].astype(bf16)
            kv_ref[:, h, :, pair:] = values.reshape(frames, strip, head_dim)


def project(tokens, weight, head_groups, head_dim):
    frames, strip, width = tokens.shape
    local_heads = HEADS // head_groups
    share = 2 // local_heads
    columns = 6 * head_dim
    q_width, kv_width = local_heads * 2 * head_dim, local_heads * 3 * head_dim
    return pl.pallas_call(
        functools.partial(qkv_kernel, local_heads, head_dim),
        grid=(HEADS // 2,),
        in_specs=[
            pl.BlockSpec((frames * strip, width), lambda i: (0, 0)),
            pl.BlockSpec((width, columns), lambda i: (0, i)),
        ],
        out_specs=[
            pl.BlockSpec((frames, share, strip, q_width), lambda i: (0, i, 0, 0)),
            pl.BlockSpec((frames, share, strip, kv_width), lambda i: (0, i, 0, 0)),
        ],
        out_shape=[
            jax.ShapeDtypeStruct((frames, head_groups, strip, q_width), bf16),
            jax.ShapeDtypeStruct((frames, head_groups, strip, kv_width), bf16),
        ],
        scratch_shapes=[pltpu.VMEM((frames * strip, width), bf16)] * 2,
        compiler_params=pltpu.CompilerParams(vmem_limit_bytes=48 << 20),
        name="qkv",
    )(tokens.reshape(-1, width), weight)


MESH = pl.DeviceIdType.MESH


def near_first(count):
    return sorted(range(1, count), key=lambda j: (min(j, count - j), j))


def greet(peers):
    barrier = pltpu.get_barrier_semaphore()
    for peer in peers:
        pl.semaphore_signal(barrier, inc=1, device_id=peer, device_id_type=MESH)
    pl.semaphore_wait(barrier, len(peers))


def exchange_kernel(
    groups, teams, q_ref, kv_ref, q_out, pairs, own_sem,
    q_send, q_recv, z_send, z_recv, f_send, f_recv, r_send, r_recv,
):
    frames = q_ref.shape[0]
    team, me = lax.axis_index("frame"), lax.axis_index("head")
    square = teams == 4
    if square:
        side = lax.rem(team, 2)
        beside, across = team + 1 - 2 * side, lax.rem(team + 2, 4)
        direct = [(beside, beside), (across, across)]
    else:
        direct = [
            (lax.rem(team + k, teams), lax.rem(team + teams - k, teams)) for k in range(1, teams)
        ]
    order = near_first(groups)
    peers = [(team, lax.rem(me + j, groups)) for j in order] + [(to, me) for to, _ in direct]
    greet(peers)

    def remote(src, dst, send, recv, target):
        return pltpu.make_async_remote_copy(
            src_ref=src, dst_ref=dst, send_sem=send, recv_sem=recv,
            device_id=target, device_id_type=MESH,
        )

    def z_copy(f, j):
        to = lax.rem(me + j, groups)
        return remote(
            kv_ref.at[f, to], pairs.at[team * frames + f, me],
            z_send.at[f, j], z_recv.at[f, j], (team, to),
        )

    def q_copy(f, j):
        to = lax.rem(me + j, groups)
        return remote(
            q_ref.at[f, to], q_out.at[f, me], q_send.at[f, j], q_recv.at[f, j], (team, to)
        )

    def piece(owner, f, j):
        return pairs.at[owner * frames + f, lax.rem(me + groups - j, groups)]

    def f_copy(k, f, j):
        src = kv_ref.at[f, me] if j == 0 else piece(team, f, j)
        return remote(
            src, piece(team, f, j), f_send.at[k, f, j], f_recv.at[k, f, j], (direct[k][0], me)
        )

    def r_copy(f, j):
        origin, to = (beside, across) if f % 2 == 0 else (across, beside)
        here = piece(origin, f, j)
        return remote(here, here, r_send.at[f, j], r_recv.at[f, j], (to, me))

    own = []
    for f in range(frames):
        own.append(
            pltpu.make_async_copy(kv_ref.at[f, me], pairs.at[team * frames + f, me], own_sem.at[0, f])
        )
        own.append(pltpu.make_async_copy(q_ref.at[f, me], q_out.at[f, me], own_sem.at[1, f]))
    schedule = [(f, j) for j in [0] + order for f in range(frames)]
    for f, j in schedule:
        if j:
            z_copy(f, j).start()
    for f, j in schedule:
        if j:
            q_copy(f, j).start()
    for copy in own:
        copy.start()
    lag = 2 * frames
    for n in range(len(schedule) + lag):
        if n < len(schedule):
            f, j = schedule[n]
            if j:
                z_copy(f, j).wait_recv()
            for k in range(len(direct)):
                f_copy(k, f, j).start()
        if n >= lag and square:
            f, j = schedule[n - lag]
            f_copy(f % 2, f, j).wait_recv()
            r_copy(f, j).start()
    for f, j in schedule:
        for k in range(len(direct)):
            f_copy(k, f, j).wait_send()
            if not (square and k == f % 2):
                f_copy(k, f, j).wait_recv()
        if square:
            r_copy(f, j).wait()
        if j:
            z_copy(f, j).wait_send()
            q_copy(f, j).wait()
    for copy in own:
        copy.wait()


def exchange(queries, own_pairs, groups, teams):
    frames = queries.shape[0]
    sems = lambda *shape: pltpu.SemaphoreType.DMA(shape)
    hops = 2 if teams == 4 else teams - 1
    vmem = pl.BlockSpec(memory_space=pltpu.VMEM)
    anywhere = pl.BlockSpec(memory_space=pl.ANY)
    return pl.pallas_call(
        functools.partial(exchange_kernel, groups, teams),
        in_specs=[vmem, vmem],
        out_specs=[anywhere, anywhere],
        out_shape=[
            jax.ShapeDtypeStruct(queries.shape, bf16),
            jax.ShapeDtypeStruct((teams * frames,) + own_pairs.shape[1:], bf16),
        ],
        scratch_shapes=[sems(2, frames)]
        + [sems(frames, groups)] * 4
        + [sems(hops, frames, groups)] * 2
        + [sems(frames, groups)] * 2,
        compiler_params=pltpu.CompilerParams(collective_id=0, has_side_effects=True),
        name="exchange",
    )(queries, own_pairs)


def hand_back_kernel(groups, src, dst, own_sem, send, recv):
    team, me = lax.axis_index("frame"), lax.axis_index("head")
    order = near_first(groups)
    greet([(team, lax.rem(me + j, groups)) for j in order])
    copies = []
    for j in reversed(order):
        to = lax.rem(me + j, groups)
        copies.append(
            pltpu.make_async_remote_copy(
                src_ref=src.at[:, to], dst_ref=dst.at[me],
                send_sem=send.at[j], recv_sem=recv.at[j],
                device_id=(team, to), device_id_type=MESH,
            )
        )
    copies.append(pltpu.make_async_copy(src.at[:, me], dst.at[me], own_sem))
    for copy in copies:
        copy.start()
    for copy in copies:
        copy.wait()


def hand_back(attended):
    frames, groups, strip, width = attended.shape
    vmem = pl.BlockSpec(memory_space=pltpu.VMEM)
    return pl.pallas_call(
        functools.partial(hand_back_kernel, groups),
        in_specs=[vmem],
        out_specs=vmem,
        out_shape=jax.ShapeDtypeStruct((groups, frames, strip, width), bf16),
        scratch_shapes=[pltpu.SemaphoreType.DMA] + [pltpu.SemaphoreType.DMA((groups,))] * 2,
        compiler_params=pltpu.CompilerParams(collective_id=1, has_side_effects=True),
        name="hand_back",
    )(attended)


def attend_kernel(local_heads, head_dim, span, lists, counts, q_ref, kv_ref, o_ref):
    b = pl.program_id(0)
    count = counts[b]
    pair = 2 * head_dim
    v_at = local_heads * pair
    v_width = local_heads * head_dim
    first = lax.broadcasted_iota(jnp.int32, (BLOCK, pair), 1) < head_dim
    stacked = []
    for h in range(local_heads):
        coded = q_ref[:, h * pair : (h + 1) * pair].astype(f32)
        turned = pltpu.roll(coded, head_dim, 1)
        high, low = jnp.where(first, coded, turned), jnp.where(first, turned, coded)
        stacked.append(jnp.concatenate([high, low], axis=0).astype(bf16))

    def chunk(c, carry):
        offsets = []
        valid = []
        for t in range(span):
            slot = c * span + t
            block = lists[b, jnp.minimum(slot, count - 1)]
            offsets.append(pl.multiple_of(block * BLOCK, BLOCK))
            valid.append(slot < count)
        values = jnp.concatenate(
            [kv_ref[pl.ds(at, BLOCK), v_at : v_at + v_width] for at in offsets], axis=0
        )
        out = []
        for h in range(local_heads):
            top, total, blend = carry[h]
            scores = []
            for at, ok in zip(offsets, valid):
                keys = kv_ref[pl.ds(at, BLOCK), h * pair : (h + 1) * pair]
                both = lax.dot_general(
                    stacked[h], keys, (((1,), (1,)), ((), ())), preferred_element_type=f32
                )
                scores.append(jnp.where(ok, both[:BLOCK] + both[BLOCK:], -jnp.inf))
            peak = functools.reduce(jnp.maximum, scores)
            new_top = jnp.maximum(top, jnp.max(peak, axis=1, keepdims=True))
            scale = jnp.exp(top - new_top)
            weights = [jnp.exp(s - new_top) for s in scores]
            total = total * scale + functools.reduce(jnp.add, weights)
            packed = jnp.concatenate([w.astype(bf16) for w in weights], axis=1)
            blend = blend * scale + mxu(packed, values)
            out.append((new_top, total, blend))
        return tuple(out)

    start = tuple(
        (
            jnp.full((BLOCK, 1), -jnp.inf, f32),
            jnp.zeros((BLOCK, BLOCK), f32),
            jnp.zeros((BLOCK, v_width), f32),
        )
        for _ in range(local_heads)
    )
    final = lax.fori_loop(0, (count + span - 1) // span, chunk, start)
    owner = lax.broadcasted_iota(jnp.int32, (BLOCK, v_width), 1) // head_dim
    result = jnp.zeros((BLOCK, v_width), f32)
    for h in range(local_heads):
        _, total, blend = final[h]
        ready = blend / jnp.sum(total, axis=1, keepdims=True)
        result = jnp.where(owner == h, ready, result)
    o_ref[...] = result.astype(bf16)


def attend(queries, pairs, lists, counts, local_heads, head_dim):
    blocks, slots = lists.shape
    span = -(-slots // (-(-slots // 7)))
    width = local_heads * head_dim
    return pl.pallas_call(
        functools.partial(attend_kernel, local_heads, head_dim, span),
        grid_spec=pltpu.PrefetchScalarGridSpec(
            num_scalar_prefetch=2,
            grid=(blocks,),
            in_specs=[
                pl.BlockSpec((BLOCK, queries.shape[1]), lambda i, *_: (i, 0)),
                pl.BlockSpec(pairs.shape, lambda i, *_: (0, 0), pipeline_mode=pl.Buffered(1)),
            ],
            out_specs=pl.BlockSpec((BLOCK, width), lambda i, *_: (i, 0)),
        ),
        out_shape=jax.ShapeDtypeStruct((blocks * BLOCK, width), bf16),
        compiler_params=pltpu.CompilerParams(vmem_limit_bytes=48 << 20),
        name="attend",
    )(lists, counts, queries, pairs)


def scatter_order(teams, halves, k):
    far = halves - 1 - lax.rem(k, halves)
    turn = lax.rem(k // halves + 1 + 2 * far, teams)
    return turn, far


def front_kernel(
    teams, groups, slots, x_hbm, w_hbm, lists_hbm, counts_hbm, out_hbm, gain_ref, proj_ref, ext_ref,
    w_buf, x_hi, x_lo, msg, msg_scale, got, got_scale, q_ref, kv_ref, stream, out_buf,
    ready, sent, back, lists_all, counts_all, lists, counts,
    w_sem, l_sem, i_sem, m_send, m_recv, s_send, s_recv, f_send, f_recv, a_send, a_recv,
    i_send, i_recv, h_send, h_recv,
):
    planes = groups // 2
    halves = planes // 2
    pairs = teams * halves
    chips = teams * planes
    lanes = msg.shape[-1]
    head_dim = lanes // 2
    columns = 3 * lanes
    rows = stream.shape[0]
    channels = proj_ref.shape[-1]
    team, group = lax.axis_index("frame"), lax.axis_index("head")
    plane, core = group // 2, lax.rem(group, 2)
    half, parity = plane // 2, lax.rem(plane, 2)
    me = team * planes + plane
    sibling = (team, group + 1 - 2 * core)
    above = (team, lax.rem(group + groups - 1, groups))
    below = (team, lax.rem(group + 1, groups))

    def place(k):
        turn, far = scatter_order(teams, halves, k)
        return lax.rem(team + turn, teams), lax.rem(half + far, halves)

    def weight(k):
        to_team, to_half = place(k)
        at = pl.multiple_of((to_team * halves + to_half) * columns, columns)
        return pltpu.make_async_copy(w_hbm.at[:, pl.ds(at, columns)], w_buf.at[k], w_sem.at[k])

    load_x = pltpu.make_async_copy(x_hbm, stream, l_sem.at[0])
    load_out = pltpu.make_async_copy(out_hbm, out_buf, l_sem.at[1])
    load_lists = [
        pltpu.make_async_copy(lists_hbm, lists_all.at[team], l_sem.at[2]),
        pltpu.make_async_copy(counts_hbm, counts_all.at[team], l_sem.at[3]),
    ]
    load_x.start()
    for k in range(pairs):
        weight(k).start()
    for copy in load_lists:
        copy.start()
    load_out.start()

    barrier = pltpu.get_barrier_semaphore()
    for n in range(1, chips):
        peer = (lax.rem(team + n // planes, teams), lax.rem(plane + n % planes, planes) * 2 + core)
        pl.semaphore_signal(barrier, inc=1, device_id=peer, device_id_type=MESH)
    for peer in (above, below):
        pl.semaphore_signal(barrier, inc=1, device_id=peer, device_id_type=MESH)

    first = lax.broadcasted_iota(jnp.int32, (rows, lanes), 1) < head_dim
    lane = lax.broadcasted_iota(jnp.int32, (BLOCK, lanes), 1)
    near = lane < head_dim
    top = 32766.0

    def message(to_team, to_plane):
        to = to_team * planes + to_plane
        target = (to_team, to_plane * 2 + core)
        return [
            pltpu.make_async_remote_copy(
                src_ref=msg.at[to], dst_ref=got.at[me],
                send_sem=m_send.at[to], recv_sem=m_recv.at[me],
                device_id=target, device_id_type=MESH,
            ),
            pltpu.make_async_remote_copy(
                src_ref=msg_scale.at[to], dst_ref=got_scale.at[me],
                send_sem=s_send.at[to], recv_sem=s_recv.at[me],
                device_id=target, device_id_type=MESH,
            ),
        ]

    def peak(value):
        return jnp.maximum(jnp.max(jnp.abs(value), axis=1, keepdims=True), 1e-30)

    def encode(k):
        weight(k).wait()
        w_hi, w_lo = split_hi_lo(w_buf[k])
        acc = mxu(x_hi[...], w_lo) + mxu(x_lo[...], w_hi)
        acc = acc + mxu(x_hi[...], w_hi)
        p0, p1, p2 = [acc[:, n * lanes : (n + 1) * lanes] for n in range(3)]
        t0, t1 = pltpu.roll(p0, head_dim, 1), pltpu.roll(p1, head_dim, 1)
        key_value = [jnp.where(first, t0, t1), p2]
        up, down = slice(0, BLOCK), slice(BLOCK, 2 * BLOCK)
        query = [jnp.where(near, p0[up], t0[down]), jnp.where(near, t1[up], p1[down])]
        to_team, to_half = place(k)
        for i in range(2):
            to = to_team * planes + to_half * 2 + i
            kv, q = key_value[i], query[i]
            peak_k = peak(jnp.where(first, kv, 0.0))
            peak_v = peak(jnp.where(first, 0.0, kv))
            peak_q0 = peak(jnp.where(near, q, 0.0))
            peak_q1 = peak(jnp.where(near, 0.0, q))
            kv = kv * jnp.where(first, top / peak_k, top / peak_v)
            q = q * jnp.where(near, top / peak_q0, top / peak_q1)
            msg[to, 0:2] = jnp.round(kv).astype(jnp.int32).astype(jnp.int16).reshape(2, BLOCK, lanes)
            msg[to, 2] = jnp.round(q).astype(jnp.int32).astype(jnp.int16)
            columns_of = [peak_k[up], peak_k[down], peak_v[up], peak_v[down], peak_q0, peak_q1]
            table = jnp.zeros((BLOCK, lanes), f32)
            for n, column in enumerate(columns_of):
                table = jnp.where(lane == n, column * (1.0 / top), table)
            msg_scale[to] = jnp.transpose(table)[:8]

    def post(k):
        to_team, to_half = place(k)
        for i in range(2):
            to_plane = to_half * 2 + i
            to = to_team * planes + to_plane

            @pl.when(to != me)
            def _():
                for copy in message(to_team, to_plane):
                    copy.start()

            @pl.when(to == me)
            def _():
                got[to] = msg[to]
                got_scale[to] = msg_scale[to]

    load_x.wait()
    hi, lo = split_hi_lo(stream[...])
    x_hi[...] = hi
    x_lo[...] = lo
    encode(0)
    for copy in load_lists:
        copy.wait()
    pl.semaphore_wait(barrier, chips + 1)
    post(0)

    def list_copies(step):
        return [
            pltpu.make_async_remote_copy(
                src_ref=whole.at[team], dst_ref=whole.at[team],
                send_sem=i_send.at[n, step], recv_sem=i_recv.at[n, step],
                device_id=(lax.rem(team + step, teams), group), device_id_type=MESH,
            )
            for n, whole in enumerate((lists_all, counts_all))
        ]

    def list_arrivals(step):
        origin = lax.rem(team + teams - step, teams)
        return [
            pltpu.make_async_remote_copy(
                src_ref=whole.at[origin], dst_ref=whole.at[origin],
                send_sem=i_send.at[n, step], recv_sem=i_recv.at[n, step],
                device_id=sibling, device_id_type=MESH,
            )
            for n, whole in enumerate((lists_all, counts_all))
        ]

    for step in range(1, teams):
        for copy in list_copies(step):
            copy.start()

    def send_step(k, carry):
        encode(k)
        post(k)
        return carry

    lax.fori_loop(1, pairs, send_step, 0)

    for step in range(1, teams):
        for copy in list_arrivals(step):
            copy.wait_recv()
    to_smem = [
        pltpu.make_async_copy(lists_all, lists, i_sem.at[0]),
        pltpu.make_async_copy(counts_all, counts, i_sem.at[1]),
    ]
    for copy in to_smem:
        copy.start()

    factor = head_dim ** (-0.5) * 1.4426950408889634

    def source(n):
        far = n // (2 * teams)
        turn = lax.rem(lax.rem(n, 2 * teams) // 2 + 1 + 2 * far, teams)
        from_team = lax.rem(team + teams - turn, teams)
        from_plane = lax.rem(half + halves - far, halves) * 2 + lax.rem(parity + 1 + n, 2)
        return from_team, from_plane

    def arrival(src):
        return [
            pltpu.make_async_remote_copy(
                src_ref=msg.at[src], dst_ref=got.at[src],
                send_sem=m_send.at[src], recv_sem=m_recv.at[src],
                device_id=sibling, device_id_type=MESH,
            ),
            pltpu.make_async_remote_copy(
                src_ref=msg_scale.at[src], dst_ref=got_scale.at[src],
                send_sem=s_send.at[src], recv_sem=s_recv.at[src],
                device_id=sibling, device_id_type=MESH,
            ),
        ]

    def forward(from_team, from_plane, f, whose):
        src = from_team * planes + from_plane
        block = kv_ref.at[(from_team * 2 + f) * groups + from_plane * 2 + whose]
        return pltpu.make_async_remote_copy(
            src_ref=block, dst_ref=block,
            send_sem=f_send.at[f, src], recv_sem=f_recv.at[f, src],
            device_id=sibling, device_id_type=MESH,
        )

    def take_step(n, carry):
        from_team, from_plane = source(n)
        src = from_team * planes + from_plane

        @pl.when(src != me)
        def _():
            for copy in arrival(src):
                copy.wait_recv()

        scale = jnp.transpose(jnp.concatenate([got_scale[src]] * (BLOCK // 8), axis=0))
        for f in range(2):
            at = (from_team * 2 + f) * groups + from_plane * 2 + core
            kv = got[src, f].astype(jnp.int32).astype(f32)
            kv = kv * jnp.where(near, scale[:, f : f + 1], scale[:, 2 + f : 3 + f])
            high = kv.astype(bf16).astype(f32)
            low = pltpu.roll(kv - high, head_dim, 1)
            kv_ref[at, :, :lanes] = jnp.where(near, high, low).astype(bf16)
            value = jnp.where(near, pltpu.roll(kv, head_dim, 1), 1.0)
            kv_ref[at, :, lanes:] = value.astype(bf16)
            forward(from_team, from_plane, f, core).start()
        q = got[src, 2].astype(jnp.int32).astype(f32)
        q = q * (factor * jnp.where(near, scale[:, 4:5], scale[:, 5:6]))
        high = q.astype(bf16).astype(f32)
        low = q - high
        high_turned, low_turned = pltpu.roll(high, head_dim, 1), pltpu.roll(low, head_dim, 1)
        q_ref[src, 0, :, :lanes] = jnp.where(near, high, high_turned).astype(bf16)
        q_ref[src, 0, :, lanes:] = jnp.where(near, low, low_turned).astype(bf16)
        q_ref[src, 1, :, :lanes] = jnp.where(near, high_turned, high).astype(bf16)
        q_ref[src, 1, :, lanes:] = jnp.where(near, low_turned, low).astype(bf16)
        return carry

    lax.fori_loop(0, chips, take_step, 0)

    def end_step(n, carry):
        from_team, from_plane = source(n)
        src = from_team * planes + from_plane
        for f in range(2):
            forward(from_team, from_plane, f, 1 - core).wait_recv()
        return carry

    for copy in to_smem:
        copy.wait()
    lax.fori_loop(0, chips, end_step, 0)

    def copy_to(to_team, to_plane):
        to = to_team * planes + to_plane
        return pltpu.make_async_remote_copy(
            src_ref=sent.at[to], dst_ref=back.at[me],
            send_sem=a_send.at[to], recv_sem=a_recv.at[me],
            device_id=(to_team, to_plane * 2 + core), device_id_type=MESH,
        )

    def returned(src):
        return pltpu.make_async_remote_copy(
            src_ref=sent.at[src], dst_ref=back.at[src],
            send_sem=a_send.at[src], recv_sem=a_recv.at[src],
            device_id=sibling, device_id_type=MESH,
        )

    def attend_frame(to_team, f):
        scores, values = [], []
        for i in range(planes):
            row = f * groups + i * 2 + core
            count = counts[to_team, row]
            query = q_ref[to_team * planes + i, f]
            for slot in range(slots):
                block = lists[to_team, row, slot]
                keys = kv_ref[block, :, :lanes]
                score = lax.dot_general(
                    query, jnp.concatenate([keys, keys], axis=1), (((1,), (1,)), ((), ())),
                    preferred_element_type=f32,
                )
                scores.append(score if slot == 0 else jnp.where(slot < count, score, -jnp.inf))
                values.append(kv_ref[block, :, lanes:])
        for i in range(planes):
            own = slice(i * slots, (i + 1) * slots)
            top_score = jnp.max(functools.reduce(jnp.maximum, scores[own]), axis=1, keepdims=True)
            packed = jnp.concatenate(
                [jnp.exp2(s - top_score).astype(bf16) for s in scores[own]], axis=1
            )
            total = mxu(packed, jnp.concatenate(values[own], axis=0))
            ready[f, i] = total / total[:, head_dim : head_dim + 1]

    def attend_team(k):
        to_team = lax.rem(team + k, teams)
        for f in range(2):
            attend_frame(to_team, f)
        for i in range(planes):
            to = to_team * planes + i
            both = jnp.where(near, ready[0, i], pltpu.roll(ready[1, i], head_dim, 1)).astype(bf16)
            sent[to] = both

            @pl.when(to != me)
            def _():
                copy_to(to_team, i).start()

            @pl.when(to == me)
            def _():
                back[to] = both

    def absorb(k):
        from_team = lax.rem(team + teams - k, teams)
        deep = planes * head_dim
        pieces = []
        for i in range(0, planes, 2):
            at = from_team * planes + i
            for j in range(2):
                @pl.when(at + j != me)
                def _():
                    returned(at + j).wait_recv()

            one, two = back[at].astype(f32), back[at + 1].astype(f32)
            upper = jnp.where(near, one, pltpu.roll(two, head_dim, 1))
            lower = jnp.where(near, pltpu.roll(one, head_dim, 1), two)
            pieces.append(jnp.concatenate([upper, lower], axis=0).astype(bf16))
        attended = jnp.concatenate(pieces, axis=1)
        w_hi, w_lo = split_hi_lo(out_buf[pl.ds(pl.multiple_of(from_team * deep, deep), deep), :])
        stream[...] += mxu(attended, w_hi) + mxu(attended, w_lo)

    load_out.wait()
    attend_team(1)

    def team_step(k, carry):
        attend_team(k)
        absorb(k - 1)
        return carry

    lax.fori_loop(2, teams + 1, team_step, 0)
    absorb(teams)

    summed = stream[...]
    centre = jnp.mean(summed, axis=-1, keepdims=True)
    centred = summed - centre
    spread = jnp.mean(centred * centred, axis=-1, keepdims=True)
    normed = centred * lax.rsqrt(spread + eps_norm) * gain_ref[...]
    n_hi, n_lo = split_hi_lo(normed)
    p_hi, p_lo = split_hi_lo(proj_ref[...])
    features = mxu(n_hi, p_lo) + mxu(n_lo, p_hi)
    features = (features + mxu(n_hi, p_hi)).astype(bf16)
    ext_ref[:, GRID : GRID + BLOCK, :] = features.reshape(2, BLOCK, channels)

    def halo(side, f):
        at = (GRID, BLOCK)[side]
        to = (GRID + BLOCK, 0)[side]
        return pltpu.make_async_remote_copy(
            src_ref=ext_ref.at[f, pl.ds(at, GRID)], dst_ref=ext_ref.at[f, pl.ds(to, GRID)],
            send_sem=h_send.at[side, f], recv_sem=h_recv.at[side, f],
            device_id=(above, below)[side], device_id_type=MESH,
        )

    for side in range(2):
        for f in range(2):
            halo(side, f).start()

    def drain_step(n, carry):
        from_team, from_plane = source(n)
        src = from_team * planes + from_plane
        for f in range(2):
            forward(from_team, from_plane, f, core).wait_send()

        @pl.when(src != me)
        def _():
            for copy in arrival(src):
                copy.wait_send()
            returned(src).wait_send()

        return carry

    lax.fori_loop(0, chips, drain_step, 0)
    for step in range(1, teams):
        for copy in list_copies(step):
            copy.wait_send()
    for side in range(2):
        for f in range(2):
            halo(side, f).wait()

    blank = jnp.zeros((2, GRID, channels), bf16)

    @pl.when(group == 0)
    def _():
        ext_ref[:, 0:GRID, :] = blank

    @pl.when(group == groups - 1)
    def _():
        ext_ref[:, GRID + BLOCK :, :] = blank


def front(tokens, weight, lists, counts, out_weight, gain, proj, teams, groups):
    frames, strip, width = tokens.shape
    head_dim = width // HEADS
    lanes = 2 * head_dim
    rows = frames * strip
    chips, pairs = HEADS, HEADS // 2
    blocks, slots = lists.shape
    channels = proj.shape[1]
    dma = lambda *shape: pltpu.SemaphoreType.DMA(shape)
    vmem = pl.BlockSpec(memory_space=pltpu.VMEM)
    hbm = pl.BlockSpec(memory_space=pltpu.HBM)
    listed, counted = (teams, blocks, slots), (teams, blocks)
    return pl.pallas_call(
        functools.partial(front_kernel, teams, groups, slots),
        in_specs=[hbm, hbm, hbm, hbm, hbm, vmem, vmem],
        out_specs=vmem,
        out_shape=jax.ShapeDtypeStruct((frames, strip + 2 * GRID, channels), bf16),
        scratch_shapes=[
            pltpu.VMEM((pairs, width, 6 * head_dim), f32),
            pltpu.VMEM((rows, width), bf16),
            pltpu.VMEM((rows, width), bf16),
            pltpu.VMEM((chips, 3, BLOCK, lanes), jnp.int16),
            pltpu.VMEM((chips, 8, BLOCK), f32),
            pltpu.VMEM((chips, 3, BLOCK, lanes), jnp.int16),
            pltpu.VMEM((chips, 8, BLOCK), f32),
            pltpu.VMEM((chips, frames, BLOCK, 2 * lanes), bf16),
            pltpu.VMEM((teams * frames * groups, BLOCK, 2 * lanes), bf16),
            pltpu.VMEM((rows, width), f32),
            pltpu.VMEM((width, width), f32),
            pltpu.VMEM((frames, groups // 2, BLOCK, lanes), f32),
            pltpu.VMEM((chips, BLOCK, lanes), bf16),
            pltpu.VMEM((chips, BLOCK, lanes), bf16),
            pltpu.VMEM(listed, jnp.int32),
            pltpu.VMEM(counted, jnp.int32),
            pltpu.SMEM(listed, jnp.int32),
            pltpu.SMEM(counted, jnp.int32),
            dma(pairs), dma(4), dma(2),
        ]
        + [dma(chips)] * 4
        + [dma(frames, chips)] * 2
        + [dma(chips)] * 2
        + [dma(2, teams)] * 2
        + [dma(2, 2)] * 2,
        compiler_params=pltpu.CompilerParams(
            collective_id=0, has_side_effects=True, vmem_limit_bytes=56 << 20
        ),
        name="front",
    )(tokens.reshape(rows, width), weight, lists, counts, out_weight, gain.reshape(1, width), proj)


def head_kernel(
    token_rows, feat_ref, up_ref, conv_ref, bias_ref, out_ref, up_map, act_map, hid_map, flat
):
    channels = feat_ref.shape[-1]
    ext = token_rows + 2
    pixel_cols = 4 * GRID
    feat = feat_ref[0]
    for a in range(4):
        for e in range(4):
            at = (4 * a + e) * channels
            lifted = mxu(feat, up_ref[:, at : at + channels]).astype(bf16)
            for r in range(ext):
                piece = lifted[r * GRID : (r + 1) * GRID]
                up_map[4 * r + a, e * GRID : (e + 1) * GRID, :] = piece
                act_map[4 * r + a, e * GRID : (e + 1) * GRID, :] = jnp.maximum(
                    piece, jnp.zeros((), bf16)
                )

    def conv_rows(source, first, rows, which):
        taps = jnp.concatenate(
            [
                source[pl.ds(first + dy, rows)].reshape(rows * pixel_cols, channels)
                for dy in range(3)
            ],
            axis=1,
        )
        part = []
        for dx in range(3):
            weight = jnp.concatenate([conv_ref[which, dy, dx] for dy in range(3)], axis=0)
            part.append(mxu(taps, weight).reshape(rows, 4, GRID, channels))
        column = lax.broadcasted_iota(jnp.int32, (rows * GRID, channels), 0) % GRID

        def moved(block, step):
            block = block.reshape(rows * GRID, channels)
            turned = pltpu.roll(block, step % (rows * GRID), 0)
            rim = 0 if step > 0 else GRID - 1
            return jnp.where(column == rim, 0.0, turned).reshape(rows, GRID, channels)

        left, centre, right = part
        shifted = []
        for e in range(4):
            low = left[:, e - 1] if e > 0 else moved(left[:, 3], 1)
            high = right[:, e + 1] if e < 3 else moved(right[:, 0], -1)
            shifted.append(low + centre[:, e] + high + bias_ref[which][None, None, :])
        return shifted

    hidden_rows = 4 * token_rows + 2
    group = divisor_upto(hidden_rows, 6)
    top = lax.axis_index("head") == 0
    bottom = lax.axis_index("head") == lax.axis_size("head") - 1
    for g in range(hidden_rows // group):
        pieces = conv_rows(act_map, g * group + 2, group, 0)
        for e in range(4):
            value = jnp.maximum(pieces[e], 0.0).astype(bf16)
            hid_map[g * group : (g + 1) * group, e * GRID : (e + 1) * GRID, :] = value

    @pl.when(top)
    def _():
        hid_map[0] = jnp.zeros((pixel_cols, channels), bf16)

    @pl.when(bottom)
    def _():
        hid_map[hidden_rows - 1] = jnp.zeros((pixel_cols, channels), bf16)

    out_rows = 4 * token_rows
    group2 = divisor_upto(out_rows, 4)
    lanes = 128
    for g in range(out_rows // group2):
        pieces = conv_rows(hid_map, g * group2, group2, 1)
        for r in range(group2):
            y = g * group2 + r
            for e in range(4):
                value = pieces[e][r] + up_map[y + 4, e * GRID : (e + 1) * GRID, :].astype(f32)
                for n in range(channels // lanes):
                    flat[y % 2, n, pl.ds(e, GRID, stride=4), :] = value[:, n * lanes : (n + 1) * lanes]
            for n in range(channels // lanes):
                out_ref[0, y, :, n * lanes : (n + 1) * lanes] = flat[y % 2, n].astype(bf16)


def predict(features, up_weight, conv_weight, conv_bias, token_rows):
    frames, ext_tokens, channels = features.shape
    pixel_rows, pixel_cols = 4 * token_rows, 4 * GRID
    once = pl.Buffered(1)
    return pl.pallas_call(
        functools.partial(head_kernel, token_rows),
        grid_spec=pltpu.PrefetchScalarGridSpec(
            num_scalar_prefetch=0,
            grid=(frames,),
            in_specs=[
                pl.BlockSpec((1, ext_tokens, channels), lambda i, *_: (i, 0, 0)),
                pl.BlockSpec(up_weight.shape, lambda i, *_: (0, 0), pipeline_mode=once),
                pl.BlockSpec(conv_weight.shape, lambda i, *_: (0, 0, 0, 0, 0), pipeline_mode=once),
                pl.BlockSpec(conv_bias.shape, lambda i, *_: (0, 0), pipeline_mode=once),
            ],
            out_specs=pl.BlockSpec(
                (1, pixel_rows, pixel_cols, channels), lambda i, *_: (i, 0, 0, 0)
            ),
            scratch_shapes=[
                pltpu.VMEM((pixel_rows + 8, pixel_cols, channels), bf16),
                pltpu.VMEM((pixel_rows + 8, pixel_cols, channels), bf16),
                pltpu.VMEM((pixel_rows + 2, pixel_cols, channels), bf16),
                pltpu.VMEM((2, channels // 128, pixel_cols, 128), f32),
            ],
        ),
        out_shape=jax.ShapeDtypeStruct((frames, pixel_rows, pixel_cols, channels), bf16),
        compiler_params=pltpu.CompilerParams(vmem_limit_bytes=56 << 20),
        name="head",
    )(features, up_weight, conv_weight, conv_bias)


def layer_norm(rows, gain):
    centre = jnp.mean(rows, axis=-1, keepdims=True)
    centred = rows - centre
    spread = jnp.mean(centred * centred, axis=-1, keepdims=True)
    return centred * lax.rsqrt(spread + eps_norm) * gain


def by_teams(
    tokens, qkv_weight, out_weight, norm_gain, proj_weight, block_lists, block_counts
):
    local_frames, strip_tokens, model_width = tokens.shape
    head_groups = lax.axis_size("head")
    local_heads = HEADS // head_groups
    head_dim = model_width // HEADS
    own_queries, own_pairs = project(tokens, qkv_weight, head_groups, head_dim)
    queries, all_pairs = exchange(own_queries, own_pairs, head_groups, lax.axis_size("frame"))
    queries = queries.reshape(-1, queries.shape[-1])
    all_pairs = all_pairs.reshape(-1, all_pairs.shape[-1])
    attended = attend(queries, all_pairs, block_lists, block_counts, local_heads, head_dim)
    attended = attended.reshape(local_frames, head_groups, strip_tokens, local_heads * head_dim)
    attended = hand_back(attended).reshape(head_groups, -1, local_heads * head_dim)
    attended = jnp.transpose(attended, (1, 0, 2)).reshape(-1, model_width)
    stream = tokens.reshape(-1, model_width) + jnp.dot(
        attended.astype(f32), out_weight, precision=highest, preferred_element_type=f32
    )
    normed = layer_norm(stream, norm_gain)
    features = jnp.dot(
        normed, proj_weight, precision=highest, preferred_element_type=f32
    ).astype(bf16)
    channels = features.shape[1]
    features = features.reshape(local_frames, strip_tokens, channels)
    forward = [(i, i + 1) for i in range(head_groups - 1)]
    backward = [(i + 1, i) for i in range(head_groups - 1)]
    above = lax.ppermute(features[:, strip_tokens - GRID :], "head", forward)
    below = lax.ppermute(features[:, :GRID], "head", backward)
    return jnp.concatenate([above, features, below], axis=1)


def on_device(
    tokens,
    qkv_weight,
    out_weight,
    norm_gain,
    proj_weight,
    up_weight,
    conv_weight,
    conv_bias,
    block_lists,
    block_counts,
):
    local_frames, strip_tokens, model_width = tokens.shape
    groups, teams = lax.axis_size("head"), lax.axis_size("frame")
    one_head_a_chip = (
        teams * groups == 2 * HEADS and groups % 4 == 0 and strip_tokens == BLOCK and local_frames == 2
        and model_width == 64 * HEADS
    )
    if one_head_a_chip:
        extended = front(
            tokens, qkv_weight, block_lists, block_counts, out_weight, norm_gain, proj_weight,
            teams, groups,
        )
    else:
        extended = by_teams(
            tokens, qkv_weight, out_weight, norm_gain, proj_weight, block_lists, block_counts
        )
    return predict(extended, up_weight, conv_weight, conv_bias, strip_tokens // GRID)


def solution(mesh):
    in_specs = (
        P("frame", "head", None),
        P(),
        P(),
        P(),
        P(),
        P(),
        P(),
        P(),
        P("frame", None),
        P("frame"),
    )
    out_specs = P("frame", "head", None, None)
    return jax.shard_map(
        on_device, mesh=mesh, in_specs=in_specs, out_specs=out_specs, check_vma=False
    )
```

```python
import functools

import jax
import jax.numpy as jnp
from jax import lax
from jax.experimental import pallas as pl
from jax.experimental.pallas import tpu as pltpu
from jax.sharding import PartitionSpec as P

HEADS = 16
GRID = 32
BLOCK = 128
eps_norm = 1e-05
highest = lax.Precision.HIGHEST
f32 = jnp.float32
bf16 = jnp.bfloat16


def divisor_upto(count, most):
    return max(d for d in range(1, most + 1) if count % d == 0)


def split_hi_lo(value):
    hi = value.astype(bf16)
    return hi, (value - hi.astype(f32)).astype(bf16)


def mxu(a, b):
    return jnp.dot(a, b, preferred_element_type=f32)


def qkv_kernel(local_heads, head_dim, x_ref, w_ref, q_ref, kv_ref, x_hi, x_lo):
    @pl.when(pl.program_id(0) == 0)
    def _():
        hi, lo = split_hi_lo(x_ref[...])
        x_hi[...] = hi
        x_lo[...] = lo

    w_hi, w_lo = split_hi_lo(w_ref[...])
    acc = mxu(x_hi[...], w_lo) + mxu(x_lo[...], w_hi)
    acc = acc + mxu(x_hi[...], w_hi)
    pair = 2 * head_dim
    frames, _, strip, _ = q_ref.shape
    rows = frames * strip
    first = lax.broadcasted_iota(jnp.int32, (rows, pair), 1) < head_dim
    parts = [acc[:, n * pair : (n + 1) * pair] for n in range(3)]
    turned = [pltpu.roll(part, head_dim, 1) for part in parts]

    def coded(value):
        rest = value - value.astype(bf16).astype(f32)
        return jnp.where(first, value, rest).astype(bf16).reshape(frames, strip, pair)

    factor = head_dim ** (-0.5)
    queries = [
        coded(jnp.where(first, parts[0], turned[0]) * factor),
        coded(jnp.where(first, turned[1], parts[1]) * factor),
    ]
    keys = [
        coded(jnp.where(first, turned[0], parts[0])),
        coded(jnp.where(first, parts[2], turned[2])),
    ]
    if local_heads == 2:
        for h in range(2):
            q_ref[:, 0, :, h * pair : (h + 1) * pair] = queries[h]
            kv_ref[:, 0, :, h * pair : (h + 1) * pair] = keys[h]
        values = jnp.where(first, parts[1], parts[2]).astype(bf16)
        kv_ref[:, 0, :, 2 * pair :] = values.reshape(frames, strip, pair)
    else:
        for h, values in enumerate((parts[1], turned[2])):
            q_ref[:, h] = queries[h]
            kv_ref[:, h, :, :pair] = keys[h]
            values = values[:, :head_dim].astype(bf16)
            kv_ref[:, h, :, pair:] = values.reshape(frames, strip, head_dim)


def project(tokens, weight, head_groups, head_dim):
    frames, strip, width = tokens.shape
    local_heads = HEADS // head_groups
    share = 2 // local_heads
    columns = 6 * head_dim
    q_width, kv_width = local_heads * 2 * head_dim, local_heads * 3 * head_dim
    return pl.pallas_call(
        functools.partial(qkv_kernel, local_heads, head_dim),
        grid=(HEADS // 2,),
        in_specs=[
            pl.BlockSpec((frames * strip, width), lambda i: (0, 0)),
            pl.BlockSpec((width, columns), lambda i: (0, i)),
        ],
        out_specs=[
            pl.BlockSpec((frames, share, strip, q_width), lambda i: (0, i, 0, 0)),
            pl.BlockSpec((frames, share, strip, kv_width), lambda i: (0, i, 0, 0)),
        ],
        out_shape=[
            jax.ShapeDtypeStruct((frames, head_groups, strip, q_width), bf16),
            jax.ShapeDtypeStruct((frames, head_groups, strip, kv_width), bf16),
        ],
        scratch_shapes=[pltpu.VMEM((frames * strip, width), bf16)] * 2,
        compiler_params=pltpu.CompilerParams(vmem_limit_bytes=48 << 20),
        name="qkv",
    )(tokens.reshape(-1, width), weight)


MESH = pl.DeviceIdType.MESH


def near_first(count):
    return sorted(range(1, count), key=lambda j: (min(j, count - j), j))


def greet(peers):
    barrier = pltpu.get_barrier_semaphore()
    for peer in peers:
        pl.semaphore_signal(barrier, inc=1, device_id=peer, device_id_type=MESH)
    pl.semaphore_wait(barrier, len(peers))


def exchange_kernel(
    groups, teams, q_ref, kv_ref, q_out, pairs, own_sem,
    q_send, q_recv, z_send, z_recv, f_send, f_recv, r_send, r_recv,
):
    frames = q_ref.shape[0]
    team, me = lax.axis_index("frame"), lax.axis_index("head")
    square = teams == 4
    if square:
        side = lax.rem(team, 2)
        beside, across = team + 1 - 2 * side, lax.rem(team + 2, 4)
        direct = [(beside, beside), (across, across)]
    else:
        direct = [
            (lax.rem(team + k, teams), lax.rem(team + teams - k, teams)) for k in range(1, teams)
        ]
    order = near_first(groups)
    peers = [(team, lax.rem(me + j, groups)) for j in order] + [(to, me) for to, _ in direct]
    greet(peers)

    def remote(src, dst, send, recv, target):
        return pltpu.make_async_remote_copy(
            src_ref=src, dst_ref=dst, send_sem=send, recv_sem=recv,
            device_id=target, device_id_type=MESH,
        )

    def z_copy(f, j):
        to = lax.rem(me + j, groups)
        return remote(
            kv_ref.at[f, to], pairs.at[team * frames + f, me],
            z_send.at[f, j], z_recv.at[f, j], (team, to),
        )

    def q_copy(f, j):
        to = lax.rem(me + j, groups)
        return remote(
            q_ref.at[f, to], q_out.at[f, me], q_send.at[f, j], q_recv.at[f, j], (team, to)
        )

    def piece(owner, f, j):
        return pairs.at[owner * frames + f, lax.rem(me + groups - j, groups)]

    def f_copy(k, f, j):
        src = kv_ref.at[f, me] if j == 0 else piece(team, f, j)
        return remote(
            src, piece(team, f, j), f_send.at[k, f, j], f_recv.at[k, f, j], (direct[k][0], me)
        )

    def r_copy(f, j):
        origin, to = (beside, across) if f % 2 == 0 else (across, beside)
        here = piece(origin, f, j)
        return remote(here, here, r_send.at[f, j], r_recv.at[f, j], (to, me))

    own = []
    for f in range(frames):
        own.append(
            pltpu.make_async_copy(kv_ref.at[f, me], pairs.at[team * frames + f, me], own_sem.at[0, f])
        )
        own.append(pltpu.make_async_copy(q_ref.at[f, me], q_out.at[f, me], own_sem.at[1, f]))
    schedule = [(f, j) for j in [0] + order for f in range(frames)]
    for f, j in schedule:
        if j:
            z_copy(f, j).start()
    for f, j in schedule:
        if j:
            q_copy(f, j).start()
    for copy in own:
        copy.start()
    lag = 2 * frames
    for n in range(len(schedule) + lag):
        if n < len(schedule):
            f, j = schedule[n]
            if j:
                z_copy(f, j).wait_recv()
            for k in range(len(direct)):
                f_copy(k, f, j).start()
        if n >= lag and square:
            f, j = schedule[n - lag]
            f_copy(f % 2, f, j).wait_recv()
            r_copy(f, j).start()
    for f, j in schedule:
        for k in range(len(direct)):
            f_copy(k, f, j).wait_send()
            if not (square and k == f % 2):
                f_copy(k, f, j).wait_recv()
        if square:
            r_copy(f, j).wait()
        if j:
            z_copy(f, j).wait_send()
            q_copy(f, j).wait()
    for copy in own:
        copy.wait()


def exchange(queries, own_pairs, groups, teams):
    frames = queries.shape[0]
    sems = lambda *shape: pltpu.SemaphoreType.DMA(shape)
    hops = 2 if teams == 4 else teams - 1
    vmem = pl.BlockSpec(memory_space=pltpu.VMEM)
    anywhere = pl.BlockSpec(memory_space=pl.ANY)
    return pl.pallas_call(
        functools.partial(exchange_kernel, groups, teams),
        in_specs=[vmem, vmem],
        out_specs=[anywhere, anywhere],
        out_shape=[
            jax.ShapeDtypeStruct(queries.shape, bf16),
            jax.ShapeDtypeStruct((teams * frames,) + own_pairs.shape[1:], bf16),
        ],
        scratch_shapes=[sems(2, frames)]
        + [sems(frames, groups)] * 4
        + [sems(hops, frames, groups)] * 2
        + [sems(frames, groups)] * 2,
        compiler_params=pltpu.CompilerParams(collective_id=0, has_side_effects=True),
        name="exchange",
    )(queries, own_pairs)


def hand_back_kernel(groups, src, dst, own_sem, send, recv):
    team, me = lax.axis_index("frame"), lax.axis_index("head")
    order = near_first(groups)
    greet([(team, lax.rem(me + j, groups)) for j in order])
    copies = []
    for j in reversed(order):
        to = lax.rem(me + j, groups)
        copies.append(
            pltpu.make_async_remote_copy(
                src_ref=src.at[:, to], dst_ref=dst.at[me],
                send_sem=send.at[j], recv_sem=recv.at[j],
                device_id=(team, to), device_id_type=MESH,
            )
        )
    copies.append(pltpu.make_async_copy(src.at[:, me], dst.at[me], own_sem))
    for copy in copies:
        copy.start()
    for copy in copies:
        copy.wait()


def hand_back(attended):
    frames, groups, strip, width = attended.shape
    vmem = pl.BlockSpec(memory_space=pltpu.VMEM)
    return pl.pallas_call(
        functools.partial(hand_back_kernel, groups),
        in_specs=[vmem],
        out_specs=vmem,
        out_shape=jax.ShapeDtypeStruct((groups, frames, strip, width), bf16),
        scratch_shapes=[pltpu.SemaphoreType.DMA] + [pltpu.SemaphoreType.DMA((groups,))] * 2,
        compiler_params=pltpu.CompilerParams(collective_id=1, has_side_effects=True),
        name="hand_back",
    )(attended)


def attend_kernel(local_heads, head_dim, span, lists, counts, q_ref, kv_ref, o_ref):
    b = pl.program_id(0)
    count = counts[b]
    pair = 2 * head_dim
    v_at = local_heads * pair
    v_width = local_heads * head_dim
    first = lax.broadcasted_iota(jnp.int32, (BLOCK, pair), 1) < head_dim
    stacked = []
    for h in range(local_heads):
        coded = q_ref[:, h * pair : (h + 1) * pair].astype(f32)
        turned = pltpu.roll(coded, head_dim, 1)
        high, low = jnp.where(first, coded, turned), jnp.where(first, turned, coded)
        stacked.append(jnp.concatenate([high, low], axis=0).astype(bf16))

    def chunk(c, carry):
        offsets = []
        valid = []
        for t in range(span):
            slot = c * span + t
            block = lists[b, jnp.minimum(slot, count - 1)]
            offsets.append(pl.multiple_of(block * BLOCK, BLOCK))
            valid.append(slot < count)
        values = jnp.concatenate(
            [kv_ref[pl.ds(at, BLOCK), v_at : v_at + v_width] for at in offsets], axis=0
        )
        out = []
        for h in range(local_heads):
            top, total, blend = carry[h]
            scores = []
            for at, ok in zip(offsets, valid):
                keys = kv_ref[pl.ds(at, BLOCK), h * pair : (h + 1) * pair]
                both = lax.dot_general(
                    stacked[h], keys, (((1,), (1,)), ((), ())), preferred_element_type=f32
                )
                scores.append(jnp.where(ok, both[:BLOCK] + both[BLOCK:], -jnp.inf))
            peak = functools.reduce(jnp.maximum, scores)
            new_top = jnp.maximum(top, jnp.max(peak, axis=1, keepdims=True))
            scale = jnp.exp(top - new_top)
            weights = [jnp.exp(s - new_top) for s in scores]
            total = total * scale + functools.reduce(jnp.add, weights)
            packed = jnp.concatenate([w.astype(bf16) for w in weights], axis=1)
            blend = blend * scale + mxu(packed, values)
            out.append((new_top, total, blend))
        return tuple(out)

    start = tuple(
        (
            jnp.full((BLOCK, 1), -jnp.inf, f32),
            jnp.zeros((BLOCK, BLOCK), f32),
            jnp.zeros((BLOCK, v_width), f32),
        )
        for _ in range(local_heads)
    )
    final = lax.fori_loop(0, (count + span - 1) // span, chunk, start)
    owner = lax.broadcasted_iota(jnp.int32, (BLOCK, v_width), 1) // head_dim
    result = jnp.zeros((BLOCK, v_width), f32)
    for h in range(local_heads):
        _, total, blend = final[h]
        ready = blend / jnp.sum(total, axis=1, keepdims=True)
        result = jnp.where(owner == h, ready, result)
    o_ref[...] = result.astype(bf16)


def attend(queries, pairs, lists, counts, local_heads, head_dim):
    blocks, slots = lists.shape
    span = -(-slots // (-(-slots // 7)))
    width = local_heads * head_dim
    return pl.pallas_call(
        functools.partial(attend_kernel, local_heads, head_dim, span),
        grid_spec=pltpu.PrefetchScalarGridSpec(
            num_scalar_prefetch=2,
            grid=(blocks,),
            in_specs=[
                pl.BlockSpec((BLOCK, queries.shape[1]), lambda i, *_: (i, 0)),
                pl.BlockSpec(pairs.shape, lambda i, *_: (0, 0), pipeline_mode=pl.Buffered(1)),
            ],
            out_specs=pl.BlockSpec((BLOCK, width), lambda i, *_: (i, 0)),
        ),
        out_shape=jax.ShapeDtypeStruct((blocks * BLOCK, width), bf16),
        compiler_params=pltpu.CompilerParams(vmem_limit_bytes=48 << 20),
        name="attend",
    )(lists, counts, queries, pairs)


def scatter_order(teams, halves, k):
    far = halves - 1 - lax.rem(k, halves)
    turn = lax.rem(k // halves + 1 + 2 * far, teams)
    return turn, far


def front_kernel(
    teams, groups, slots, x_hbm, w_hbm, lists_hbm, counts_hbm, out_hbm, gain_ref, proj_ref, ext_ref,
    w_buf, x_hi, x_lo, msg, msg_scale, got, got_scale, q_ref, kv_ref, stream, out_buf,
    ready, sent, back, lists_all, counts_all, lists, counts,
    w_sem, l_sem, i_sem, m_send, m_recv, s_send, s_recv, f_send, f_recv, a_send, a_recv,
    i_send, i_recv, h_send, h_recv,
):
    planes = groups // 2
    halves = planes // 2
    pairs = teams * halves
    chips = teams * planes
    lanes = msg.shape[-1]
    head_dim = lanes // 2
    columns = 3 * lanes
    rows = stream.shape[0]
    channels = proj_ref.shape[-1]
    team, group = lax.axis_index("frame"), lax.axis_index("head")
    plane, core = group // 2, lax.rem(group, 2)
    half, parity = plane // 2, lax.rem(plane, 2)
    me = team * planes + plane
    sibling = (team, group + 1 - 2 * core)
    above = (team, lax.rem(group + groups - 1, groups))
    below = (team, lax.rem(group + 1, groups))

    def place(k):
        turn, far = scatter_order(teams, halves, k)
        return lax.rem(team + turn, teams), lax.rem(half + far, halves)

    def weight(k):
        to_team, to_half = place(k)
        at = pl.multiple_of((to_team * halves + to_half) * columns, columns)
        return pltpu.make_async_copy(w_hbm.at[:, pl.ds(at, columns)], w_buf.at[k], w_sem.at[k])

    load_x = pltpu.make_async_copy(x_hbm, stream, l_sem.at[0])
    load_out = pltpu.make_async_copy(out_hbm, out_buf, l_sem.at[1])
    load_lists = [
        pltpu.make_async_copy(lists_hbm, lists_all.at[team], l_sem.at[2]),
        pltpu.make_async_copy(counts_hbm, counts_all.at[team], l_sem.at[3]),
    ]
    load_x.start()
    for k in range(pairs):
        weight(k).start()
    for copy in load_lists:
        copy.start()
    load_out.start()

    barrier = pltpu.get_barrier_semaphore()
    for n in range(1, chips):
        peer = (lax.rem(team + n // planes, teams), lax.rem(plane + n % planes, planes) * 2 + core)
        pl.semaphore_signal(barrier, inc=1, device_id=peer, device_id_type=MESH)
    for peer in (above, below):
        pl.semaphore_signal(barrier, inc=1, device_id=peer, device_id_type=MESH)

    first = lax.broadcasted_iota(jnp.int32, (rows, lanes), 1) < head_dim
    lane = lax.broadcasted_iota(jnp.int32, (BLOCK, lanes), 1)
    near = lane < head_dim
    top = 32766.0

    def message(to_team, to_plane):
        to = to_team * planes + to_plane
        target = (to_team, to_plane * 2 + core)
        return [
            pltpu.make_async_remote_copy(
                src_ref=msg.at[to], dst_ref=got.at[me],
                send_sem=m_send.at[to], recv_sem=m_recv.at[me],
                device_id=target, device_id_type=MESH,
            ),
            pltpu.make_async_remote_copy(
                src_ref=msg_scale.at[to], dst_ref=got_scale.at[me],
                send_sem=s_send.at[to], recv_sem=s_recv.at[me],
                device_id=target, device_id_type=MESH,
            ),
        ]

    def peak(value):
        return jnp.maximum(jnp.max(jnp.abs(value), axis=1, keepdims=True), 1e-30)

    def encode(k):
        weight(k).wait()
        w_hi, w_lo = split_hi_lo(w_buf[k])
        acc = mxu(x_hi[...], w_lo) + mxu(x_lo[...], w_hi)
        acc = acc + mxu(x_hi[...], w_hi)
        p0, p1, p2 = [acc[:, n * lanes : (n + 1) * lanes] for n in range(3)]
        t0, t1 = pltpu.roll(p0, head_dim, 1), pltpu.roll(p1, head_dim, 1)
        key_value = [jnp.where(first, t0, t1), p2]
        up, down = slice(0, BLOCK), slice(BLOCK, 2 * BLOCK)
        query = [jnp.where(near, p0[up], t0[down]), jnp.where(near, t1[up], p1[down])]
        to_team, to_half = place(k)
        for i in range(2):
            to = to_team * planes + to_half * 2 + i
            kv, q = key_value[i], query[i]
            peak_k = peak(jnp.where(first, kv, 0.0))
            peak_v = peak(jnp.where(first, 0.0, kv))
            peak_q0 = peak(jnp.where(near, q, 0.0))
            peak_q1 = peak(jnp.where(near, 0.0, q))
            kv = kv * jnp.where(first, top / peak_k, top / peak_v)
            q = q * jnp.where(near, top / peak_q0, top / peak_q1)
            msg[to, 0:2] = jnp.round(kv).astype(jnp.int32).astype(jnp.int16).reshape(2, BLOCK, lanes)
            msg[to, 2] = jnp.round(q).astype(jnp.int32).astype(jnp.int16)
            columns_of = [peak_k[up], peak_k[down], peak_v[up], peak_v[down], peak_q0, peak_q1]
            table = jnp.zeros((BLOCK, lanes), f32)
            for n, column in enumerate(columns_of):
                table = jnp.where(lane == n, column * (1.0 / top), table)
            msg_scale[to] = jnp.transpose(table)[:8]

    def post(k):
        to_team, to_half = place(k)
        for i in range(2):
            to_plane = to_half * 2 + i
            to = to_team * planes + to_plane

            @pl.when(to != me)
            def _():
                for copy in message(to_team, to_plane):
                    copy.start()

            @pl.when(to == me)
            def _():
                got[to] = msg[to]
                got_scale[to] = msg_scale[to]

    load_x.wait()
    hi, lo = split_hi_lo(stream[...])
    x_hi[...] = hi
    x_lo[...] = lo
    encode(0)
    for copy in load_lists:
        copy.wait()
    pl.semaphore_wait(barrier, chips + 1)
    post(0)

    def list_copies(step):
        return [
            pltpu.make_async_remote_copy(
                src_ref=whole.at[team], dst_ref=whole.at[team],
                send_sem=i_send.at[n, step], recv_sem=i_recv.at[n, step],
                device_id=(lax.rem(team + step, teams), group), device_id_type=MESH,
            )
            for n, whole in enumerate((lists_all, counts_all))
        ]

    def list_arrivals(step):
        origin = lax.rem(team + teams - step, teams)
        return [
            pltpu.make_async_remote_copy(
                src_ref=whole.at[origin], dst_ref=whole.at[origin],
                send_sem=i_send.at[n, step], recv_sem=i_recv.at[n, step],
                device_id=sibling, device_id_type=MESH,
            )
            for n, whole in enumerate((lists_all, counts_all))
        ]

    for step in range(1, teams):
        for copy in list_copies(step):
            copy.start()

    def send_step(k, carry):
        encode(k)
        post(k)
        return carry

    lax.fori_loop(1, pairs, send_step, 0)

    for step in range(1, teams):
        for copy in list_arrivals(step):
            copy.wait_recv()
    to_smem = [
        pltpu.make_async_copy(lists_all, lists, i_sem.at[0]),
        pltpu.make_async_copy(counts_all, counts, i_sem.at[1]),
    ]
    for copy in to_smem:
        copy.start()

    factor = head_dim ** (-0.5) * 1.4426950408889634

    def source(n):
        far = n // (2 * teams)
        turn = lax.rem(lax.rem(n, 2 * teams) // 2 + 1 + 2 * far, teams)
        from_team = lax.rem(team + teams - turn, teams)
        from_plane = lax.rem(half + halves - far, halves) * 2 + lax.rem(parity + 1 + n, 2)
        return from_team, from_plane

    def arrival(src):
        return [
            pltpu.make_async_remote_copy(
                src_ref=msg.at[src], dst_ref=got.at[src],
                send_sem=m_send.at[src], recv_sem=m_recv.at[src],
                device_id=sibling, device_id_type=MESH,
            ),
            pltpu.make_async_remote_copy(
                src_ref=msg_scale.at[src], dst_ref=got_scale.at[src],
                send_sem=s_send.at[src], recv_sem=s_recv.at[src],
                device_id=sibling, device_id_type=MESH,
            ),
        ]

    def forward(from_team, from_plane, f, whose):
        src = from_team * planes + from_plane
        block = kv_ref.at[(from_team * 2 + f) * groups + from_plane * 2 + whose]
        return pltpu.make_async_remote_copy(
            src_ref=block, dst_ref=block,
            send_sem=f_send.at[f, src], recv_sem=f_recv.at[f, src],
            device_id=sibling, device_id_type=MESH,
        )

    def take_step(n, carry):
        from_team, from_plane = source(n)
        src = from_team * planes + from_plane

        @pl.when(src != me)
        def _():
            for copy in arrival(src):
                copy.wait_recv()

        scale = jnp.transpose(jnp.concatenate([got_scale[src]] * (BLOCK // 8), axis=0))
        for f in range(2):
            at = (from_team * 2 + f) * groups + from_plane * 2 + core
            kv = got[src, f].astype(jnp.int32).astype(f32)
            kv = kv * jnp.where(near, scale[:, f : f + 1], scale[:, 2 + f : 3 + f])
            high = kv.astype(bf16).astype(f32)
            low = pltpu.roll(kv - high, head_dim, 1)
            kv_ref[at, :, :lanes] = jnp.where(near, high, low).astype(bf16)
            value = jnp.where(near, pltpu.roll(kv, head_dim, 1), 1.0)
            kv_ref[at, :, lanes:] = value.astype(bf16)
            forward(from_team, from_plane, f, core).start()
        q = got[src, 2].astype(jnp.int32).astype(f32)
        q = q * (factor * jnp.where(near, scale[:, 4:5], scale[:, 5:6]))
        high = q.astype(bf16).astype(f32)
        low = q - high
        high_turned, low_turned = pltpu.roll(high, head_dim, 1), pltpu.roll(low, head_dim, 1)
        q_ref[src, 0, :, :lanes] = jnp.where(near, high, high_turned).astype(bf16)
        q_ref[src, 0, :, lanes:] = jnp.where(near, low, low_turned).astype(bf16)
        q_ref[src, 1, :, :lanes] = jnp.where(near, high_turned, high).astype(bf16)
        q_ref[src, 1, :, lanes:] = jnp.where(near, low_turned, low).astype(bf16)
        return carry

    lax.fori_loop(0, chips, take_step, 0)

    def end_step(n, carry):
        from_team, from_plane = source(n)
        src = from_team * planes + from_plane
        for f in range(2):
            forward(from_team, from_plane, f, 1 - core).wait_recv()
        return carry

    for copy in to_smem:
        copy.wait()
    lax.fori_loop(0, chips, end_step, 0)

    def copy_to(to_team, to_plane):
        to = to_team * planes + to_plane
        return pltpu.make_async_remote_copy(
            src_ref=sent.at[to], dst_ref=back.at[me],
            send_sem=a_send.at[to], recv_sem=a_recv.at[me],
            device_id=(to_team, to_plane * 2 + core), device_id_type=MESH,
        )

    def returned(src):
        return pltpu.make_async_remote_copy(
            src_ref=sent.at[src], dst_ref=back.at[src],
            send_sem=a_send.at[src], recv_sem=a_recv.at[src],
            device_id=sibling, device_id_type=MESH,
        )

    def attend_frame(to_team, f):
        scores, values = [], []
        for i in range(planes):
            row = f * groups + i * 2 + core
            count = counts[to_team, row]
            query = q_ref[to_team * planes + i, f]
            for slot in range(slots):
                block = lists[to_team, row, slot]
                keys = kv_ref[block, :, :lanes]
                score = lax.dot_general(
                    query, jnp.concatenate([keys, keys], axis=1), (((1,), (1,)), ((), ())),
                    preferred_element_type=f32,
                )
                scores.append(score if slot == 0 else jnp.where(slot < count, score, -jnp.inf))
                values.append(kv_ref[block, :, lanes:])
        for i in range(planes):
            own = slice(i * slots, (i + 1) * slots)
            top_score = jnp.max(functools.reduce(jnp.maximum, scores[own]), axis=1, keepdims=True)
            packed = jnp.concatenate(
                [jnp.exp2(s - top_score).astype(bf16) for s in scores[own]], axis=1
            )
            total = mxu(packed, jnp.concatenate(values[own], axis=0))
            ready[f, i] = total / total[:, head_dim : head_dim + 1]

    def attend_team(k):
        to_team = lax.rem(team + k, teams)
        for f in range(2):
            attend_frame(to_team, f)
        for i in range(planes):
            to = to_team * planes + i
            both = jnp.where(near, ready[0, i], pltpu.roll(ready[1, i], head_dim, 1)).astype(bf16)
            sent[to] = both

            @pl.when(to != me)
            def _():
                copy_to(to_team, i).start()

            @pl.when(to == me)
            def _():
                back[to] = both

    def absorb(k):
        from_team = lax.rem(team + teams - k, teams)
        deep = planes * head_dim
        pieces = []
        for i in range(0, planes, 2):
            at = from_team * planes + i
            for j in range(2):
                @pl.when(at + j != me)
                def _():
                    returned(at + j).wait_recv()

            one, two = back[at].astype(f32), back[at + 1].astype(f32)
            upper = jnp.where(near, one, pltpu.roll(two, head_dim, 1))
            lower = jnp.where(near, pltpu.roll(one, head_dim, 1), two)
            pieces.append(jnp.concatenate([upper, lower], axis=0).astype(bf16))
        attended = jnp.concatenate(pieces, axis=1)
        w_hi, w_lo = split_hi_lo(out_buf[pl.ds(pl.multiple_of(from_team * deep, deep), deep), :])
        stream[...] += mxu(attended, w_hi) + mxu(attended, w_lo)

    load_out.wait()
    attend_team(1)

    def team_step(k, carry):
        attend_team(k)
        absorb(k - 1)
        return carry

    lax.fori_loop(2, teams + 1, team_step, 0)
    absorb(teams)

    summed = stream[...]
    centre = jnp.mean(summed, axis=-1, keepdims=True)
    centred = summed - centre
    spread = jnp.mean(centred * centred, axis=-1, keepdims=True)
    normed = centred * lax.rsqrt(spread + eps_norm) * gain_ref[...]
    n_hi, n_lo = split_hi_lo(normed)
    p_hi, p_lo = split_hi_lo(proj_ref[...])
    features = mxu(n_hi, p_lo) + mxu(n_lo, p_hi)
    features = (features + mxu(n_hi, p_hi)).astype(bf16)
    ext_ref[:, GRID : GRID + BLOCK, :] = features.reshape(2, BLOCK, channels)

    def halo(side, f):
        at = (GRID, BLOCK)[side]
        to = (GRID + BLOCK, 0)[side]
        return pltpu.make_async_remote_copy(
            src_ref=ext_ref.at[f, pl.ds(at, GRID)], dst_ref=ext_ref.at[f, pl.ds(to, GRID)],
            send_sem=h_send.at[side, f], recv_sem=h_recv.at[side, f],
            device_id=(above, below)[side], device_id_type=MESH,
        )

    for side in range(2):
        for f in range(2):
            halo(side, f).start()

    def drain_step(n, carry):
        from_team, from_plane = source(n)
        src = from_team * planes + from_plane
        for f in range(2):
            forward(from_team, from_plane, f, core).wait_send()

        @pl.when(src != me)
        def _():
            for copy in arrival(src):
                copy.wait_send()
            returned(src).wait_send()

        return carry

    lax.fori_loop(0, chips, drain_step, 0)
    for step in range(1, teams):
        for copy in list_copies(step):
            copy.wait_send()
    for side in range(2):
        for f in range(2):
            halo(side, f).wait()

    blank = jnp.zeros((2, GRID, channels), bf16)

    @pl.when(group == 0)
    def _():
        ext_ref[:, 0:GRID, :] = blank

    @pl.when(group == groups - 1)
    def _():
        ext_ref[:, GRID + BLOCK :, :] = blank


def front(tokens, weight, lists, counts, out_weight, gain, proj, teams, groups):
    frames, strip, width = tokens.shape
    head_dim = width // HEADS
    lanes = 2 * head_dim
    rows = frames * strip
    chips, pairs = HEADS, HEADS // 2
    blocks, slots = lists.shape
    channels = proj.shape[1]
    dma = lambda *shape: pltpu.SemaphoreType.DMA(shape)
    vmem = pl.BlockSpec(memory_space=pltpu.VMEM)
    hbm = pl.BlockSpec(memory_space=pltpu.HBM)
    listed, counted = (teams, blocks, slots), (teams, blocks)
    return pl.pallas_call(
        functools.partial(front_kernel, teams, groups, slots),
        in_specs=[hbm, hbm, hbm, hbm, hbm, vmem, vmem],
        out_specs=vmem,
        out_shape=jax.ShapeDtypeStruct((frames, strip + 2 * GRID, channels), bf16),
        scratch_shapes=[
            pltpu.VMEM((pairs, width, 6 * head_dim), f32),
            pltpu.VMEM((rows, width), bf16),
            pltpu.VMEM((rows, width), bf16),
            pltpu.VMEM((chips, 3, BLOCK, lanes), jnp.int16),
            pltpu.VMEM((chips, 8, BLOCK), f32),
            pltpu.VMEM((chips, 3, BLOCK, lanes), jnp.int16),
            pltpu.VMEM((chips, 8, BLOCK), f32),
            pltpu.VMEM((chips, frames, BLOCK, 2 * lanes), bf16),
            pltpu.VMEM((teams * frames * groups, BLOCK, 2 * lanes), bf16),
            pltpu.VMEM((rows, width), f32),
            pltpu.VMEM((width, width), f32),
            pltpu.VMEM((frames, groups // 2, BLOCK, lanes), f32),
            pltpu.VMEM((chips, BLOCK, lanes), bf16),
            pltpu.VMEM((chips, BLOCK, lanes), bf16),
            pltpu.VMEM(listed, jnp.int32),
            pltpu.VMEM(counted, jnp.int32),
            pltpu.SMEM(listed, jnp.int32),
            pltpu.SMEM(counted, jnp.int32),
            dma(pairs), dma(4), dma(2),
        ]
        + [dma(chips)] * 4
        + [dma(frames, chips)] * 2
        + [dma(chips)] * 2
        + [dma(2, teams)] * 2
        + [dma(2, 2)] * 2,
        compiler_params=pltpu.CompilerParams(
            collective_id=0, has_side_effects=True, vmem_limit_bytes=56 << 20
        ),
        name="front",
    )(tokens.reshape(rows, width), weight, lists, counts, out_weight, gain.reshape(1, width), proj)


def head_kernel(
    token_rows, feat_ref, up_hbm, conv_hbm, bias_ref, out_ref,
    up_ref, conv_ref, up_map, act_map, hid_map, flat, sem,
):
    channels = feat_ref.shape[-1]
    ext = token_rows + 2
    pixel_cols = 4 * GRID
    loads = [
        pltpu.make_async_copy(up_hbm, up_ref, sem.at[0]),
        pltpu.make_async_copy(conv_hbm, conv_ref, sem.at[1]),
    ]

    @pl.when(pl.program_id(0) == 0)
    def _():
        for copy in loads:
            copy.start()
        loads[0].wait()

    def moved(block, step):
        rows = block.shape[0]
        column = lax.broadcasted_iota(jnp.int32, block.shape, 0) % GRID
        turned = pltpu.roll(block, step % rows, 0)
        return jnp.where(column == (0 if step > 0 else GRID - 1), 0.0, turned)

    feat = feat_ref[0]
    for a in range(4):
        for e in range(4):
            at = (4 * a + e) * channels
            lifted = mxu(feat, up_ref[:, at : at + channels])
            plain = lifted.astype(bf16)
            active = jnp.maximum(plain, jnp.zeros((), bf16))
            rim = None
            if e == 0:
                rim, rim_at = jnp.maximum(moved(lifted, -1), 0.0).astype(bf16), 5 * GRID
            if e == 3:
                rim, rim_at = jnp.maximum(moved(lifted, 1), 0.0).astype(bf16), 0
            for r in range(ext):
                own = slice(r * GRID, (r + 1) * GRID)
                up_map[4 * r + a, e * GRID : (e + 1) * GRID, :] = plain[own]
                act_map[4 * r + a, (e + 1) * GRID : (e + 2) * GRID, :] = active[own]
                if rim is not None:
                    act_map[4 * r + a, rim_at : rim_at + GRID, :] = rim[own]

    @pl.when(pl.program_id(0) == 0)
    def _():
        loads[1].wait()

    def conv_rows(source, start, rows, which):
        taps = [
            source[start + dy : start + dy + rows, dx * GRID : dx * GRID + pixel_cols, :].reshape(
                rows * pixel_cols, channels
            )
            for dy in range(3)
            for dx in range(3)
        ]
        weight = conv_ref[which].reshape(9 * channels, channels)
        return mxu(jnp.concatenate(taps, axis=1), weight) + bias_ref[which][None, :]

    hidden_rows = 4 * token_rows + 2
    group = divisor_upto(hidden_rows, 3)
    top = lax.axis_index("head") == 0
    bottom = lax.axis_index("head") == lax.axis_size("head") - 1
    for g in range(hidden_rows // group):
        value = jnp.maximum(conv_rows(act_map, g * group + 2, group, 0), 0.0)
        for r in range(group):
            y = g * group + r
            row = value[r * pixel_cols : (r + 1) * pixel_cols]
            hid_map[y, GRID : GRID + pixel_cols, :] = row.astype(bf16)
            hid_map[y, 0:GRID, :] = moved(row[3 * GRID :], 1).astype(bf16)
            hid_map[y, 5 * GRID :, :] = moved(row[:GRID], -1).astype(bf16)

    @pl.when(top)
    def _():
        hid_map[0] = jnp.zeros(hid_map.shape[1:], bf16)

    @pl.when(bottom)
    def _():
        hid_map[hidden_rows - 1] = jnp.zeros(hid_map.shape[1:], bf16)

    out_rows = 4 * token_rows
    group2 = divisor_upto(out_rows, 4)
    lanes = 128
    for g in range(out_rows // group2):
        value = conv_rows(hid_map, g * group2, group2, 1)
        for r in range(group2):
            y = g * group2 + r
            row = value[r * pixel_cols : (r + 1) * pixel_cols] + up_map[y + 4].astype(f32)
            for n in range(channels // lanes):
                at = slice(n * lanes, (n + 1) * lanes)
                for e in range(4):
                    piece = row[e * GRID : (e + 1) * GRID, at]
                    flat[y % 4, n, pl.ds(e, GRID, stride=4), :] = piece
                out_ref[0, y, :, at] = flat[y % 4, n].astype(bf16)


def predict(features, up_weight, conv_weight, conv_bias, token_rows):
    frames, ext_tokens, channels = features.shape
    pixel_rows, pixel_cols = 4 * token_rows, 4 * GRID
    once = pl.Buffered(1)
    anywhere = pl.BlockSpec(memory_space=pl.ANY)
    return pl.pallas_call(
        functools.partial(head_kernel, token_rows),
        grid=(frames,),
        in_specs=[
            pl.BlockSpec((1, ext_tokens, channels), lambda i: (i, 0, 0)),
            anywhere,
            anywhere,
            pl.BlockSpec(conv_bias.shape, lambda i: (0, 0), pipeline_mode=once),
        ],
        out_specs=pl.BlockSpec((1, pixel_rows, pixel_cols, channels), lambda i: (i, 0, 0, 0)),
        scratch_shapes=[
            pltpu.VMEM(up_weight.shape, bf16),
            pltpu.VMEM(conv_weight.shape, bf16),
            pltpu.VMEM((pixel_rows + 8, pixel_cols, channels), bf16),
            pltpu.VMEM((pixel_rows + 8, pixel_cols + 2 * GRID, channels), bf16),
            pltpu.VMEM((pixel_rows + 2, pixel_cols + 2 * GRID, channels), bf16),
            pltpu.VMEM((4, channels // 128, pixel_cols, 128), f32),
            pltpu.SemaphoreType.DMA((2,)),
        ],
        out_shape=jax.ShapeDtypeStruct((frames, pixel_rows, pixel_cols, channels), bf16),
        compiler_params=pltpu.CompilerParams(vmem_limit_bytes=56 << 20),
        name="head",
    )(features, up_weight, conv_weight, conv_bias)


def layer_norm(rows, gain):
    centre = jnp.mean(rows, axis=-1, keepdims=True)
    centred = rows - centre
    spread = jnp.mean(centred * centred, axis=-1, keepdims=True)
    return centred * lax.rsqrt(spread + eps_norm) * gain


def by_teams(
    tokens, qkv_weight, out_weight, norm_gain, proj_weight, block_lists, block_counts
):
    local_frames, strip_tokens, model_width = tokens.shape
    head_groups = lax.axis_size("head")
    local_heads = HEADS // head_groups
    head_dim = model_width // HEADS
    own_queries, own_pairs = project(tokens, qkv_weight, head_groups, head_dim)
    queries, all_pairs = exchange(own_queries, own_pairs, head_groups, lax.axis_size("frame"))
    queries = queries.reshape(-1, queries.shape[-1])
    all_pairs = all_pairs.reshape(-1, all_pairs.shape[-1])
    attended = attend(queries, all_pairs, block_lists, block_counts, local_heads, head_dim)
    attended = attended.reshape(local_frames, head_groups, strip_tokens, local_heads * head_dim)
    attended = hand_back(attended).reshape(head_groups, -1, local_heads * head_dim)
    attended = jnp.transpose(attended, (1, 0, 2)).reshape(-1, model_width)
    stream = tokens.reshape(-1, model_width) + jnp.dot(
        attended.astype(f32), out_weight, precision=highest, preferred_element_type=f32
    )
    normed = layer_norm(stream, norm_gain)
    features = jnp.dot(
        normed, proj_weight, precision=highest, preferred_element_type=f32
    ).astype(bf16)
    channels = features.shape[1]
    features = features.reshape(local_frames, strip_tokens, channels)
    forward = [(i, i + 1) for i in range(head_groups - 1)]
    backward = [(i + 1, i) for i in range(head_groups - 1)]
    above = lax.ppermute(features[:, strip_tokens - GRID :], "head", forward)
    below = lax.ppermute(features[:, :GRID], "head", backward)
    return jnp.concatenate([above, features, below], axis=1)


def on_device(
    tokens,
    qkv_weight,
    out_weight,
    norm_gain,
    proj_weight,
    up_weight,
    conv_weight,
    conv_bias,
    block_lists,
    block_counts,
):
    local_frames, strip_tokens, model_width = tokens.shape
    groups, teams = lax.axis_size("head"), lax.axis_size("frame")
    one_head_a_chip = (
        teams * groups == 2 * HEADS and groups % 4 == 0 and strip_tokens == BLOCK and local_frames == 2
        and model_width == 64 * HEADS
    )
    if one_head_a_chip:
        extended = front(
            tokens, qkv_weight, block_lists, block_counts, out_weight, norm_gain, proj_weight,
            teams, groups,
        )
    else:
        extended = by_teams(
            tokens, qkv_weight, out_weight, norm_gain, proj_weight, block_lists, block_counts
        )
    return predict(extended, up_weight, conv_weight, conv_bias, strip_tokens // GRID)


def solution(mesh):
    in_specs = (
        P("frame", "head", None),
        P(),
        P(),
        P(),
        P(),
        P(),
        P(),
        P(),
        P("frame", None),
        P("frame"),
    )
    out_specs = P("frame", "head", None, None)
    return jax.shard_map(
        on_device, mesh=mesh, in_specs=in_specs, out_specs=out_specs, check_vma=False
    )
```

```python
import functools

import jax
import jax.numpy as jnp
from jax import lax
from jax.experimental import pallas as pl
from jax.experimental.pallas import tpu as pltpu
from jax.sharding import PartitionSpec as P

HEADS = 16
GRID = 32
BLOCK = 128
eps_norm = 1e-05
highest = lax.Precision.HIGHEST
f32 = jnp.float32
bf16 = jnp.bfloat16


def divisor_upto(count, most):
    return max(d for d in range(1, most + 1) if count % d == 0)


def split_hi_lo(value):
    hi = value.astype(bf16)
    return hi, (value - hi.astype(f32)).astype(bf16)


def mxu(a, b):
    return jnp.dot(a, b, preferred_element_type=f32)


def qkv_kernel(local_heads, head_dim, x_ref, w_ref, q_ref, kv_ref, x_hi, x_lo):
    @pl.when(pl.program_id(0) == 0)
    def _():
        hi, lo = split_hi_lo(x_ref[...])
        x_hi[...] = hi
        x_lo[...] = lo

    w_hi, w_lo = split_hi_lo(w_ref[...])
    acc = mxu(x_hi[...], w_lo) + mxu(x_lo[...], w_hi)
    acc = acc + mxu(x_hi[...], w_hi)
    pair = 2 * head_dim
    frames, _, strip, _ = q_ref.shape
    rows = frames * strip
    first = lax.broadcasted_iota(jnp.int32, (rows, pair), 1) < head_dim
    parts = [acc[:, n * pair : (n + 1) * pair] for n in range(3)]
    turned = [pltpu.roll(part, head_dim, 1) for part in parts]

    def coded(value):
        rest = value - value.astype(bf16).astype(f32)
        return jnp.where(first, value, rest).astype(bf16).reshape(frames, strip, pair)

    factor = head_dim ** (-0.5)
    queries = [
        coded(jnp.where(first, parts[0], turned[0]) * factor),
        coded(jnp.where(first, turned[1], parts[1]) * factor),
    ]
    keys = [
        coded(jnp.where(first, turned[0], parts[0])),
        coded(jnp.where(first, parts[2], turned[2])),
    ]
    if local_heads == 2:
        for h in range(2):
            q_ref[:, 0, :, h * pair : (h + 1) * pair] = queries[h]
            kv_ref[:, 0, :, h * pair : (h + 1) * pair] = keys[h]
        values = jnp.where(first, parts[1], parts[2]).astype(bf16)
        kv_ref[:, 0, :, 2 * pair :] = values.reshape(frames, strip, pair)
    else:
        for h, values in enumerate((parts[1], turned[2])):
            q_ref[:, h] = queries[h]
            kv_ref[:, h, :, :pair] = keys[h]
            values = values[:, :head_dim].astype(bf16)
            kv_ref[:, h, :, pair:] = values.reshape(frames, strip, head_dim)


def project(tokens, weight, head_groups, head_dim):
    frames, strip, width = tokens.shape
    local_heads = HEADS // head_groups
    share = 2 // local_heads
    columns = 6 * head_dim
    q_width, kv_width = local_heads * 2 * head_dim, local_heads * 3 * head_dim
    return pl.pallas_call(
        functools.partial(qkv_kernel, local_heads, head_dim),
        grid=(HEADS // 2,),
        in_specs=[
            pl.BlockSpec((frames * strip, width), lambda i: (0, 0)),
            pl.BlockSpec((width, columns), lambda i: (0, i)),
        ],
        out_specs=[
            pl.BlockSpec((frames, share, strip, q_width), lambda i: (0, i, 0, 0)),
            pl.BlockSpec((frames, share, strip, kv_width), lambda i: (0, i, 0, 0)),
        ],
        out_shape=[
            jax.ShapeDtypeStruct((frames, head_groups, strip, q_width), bf16),
            jax.ShapeDtypeStruct((frames, head_groups, strip, kv_width), bf16),
        ],
        scratch_shapes=[pltpu.VMEM((frames * strip, width), bf16)] * 2,
        compiler_params=pltpu.CompilerParams(vmem_limit_bytes=48 << 20),
        name="qkv",
    )(tokens.reshape(-1, width), weight)


MESH = pl.DeviceIdType.MESH


def near_first(count):
    return sorted(range(1, count), key=lambda j: (min(j, count - j), j))


def greet(peers):
    barrier = pltpu.get_barrier_semaphore()
    for peer in peers:
        pl.semaphore_signal(barrier, inc=1, device_id=peer, device_id_type=MESH)
    pl.semaphore_wait(barrier, len(peers))


def exchange_kernel(
    groups, teams, q_ref, kv_ref, q_out, pairs, own_sem,
    q_send, q_recv, z_send, z_recv, f_send, f_recv, r_send, r_recv,
):
    frames = q_ref.shape[0]
    team, me = lax.axis_index("frame"), lax.axis_index("head")
    square = teams == 4
    if square:
        side = lax.rem(team, 2)
        beside, across = team + 1 - 2 * side, lax.rem(team + 2, 4)
        direct = [(beside, beside), (across, across)]
    else:
        direct = [
            (lax.rem(team + k, teams), lax.rem(team + teams - k, teams)) for k in range(1, teams)
        ]
    order = near_first(groups)
    peers = [(team, lax.rem(me + j, groups)) for j in order] + [(to, me) for to, _ in direct]
    greet(peers)

    def remote(src, dst, send, recv, target):
        return pltpu.make_async_remote_copy(
            src_ref=src, dst_ref=dst, send_sem=send, recv_sem=recv,
            device_id=target, device_id_type=MESH,
        )

    def z_copy(f, j):
        to = lax.rem(me + j, groups)
        return remote(
            kv_ref.at[f, to], pairs.at[team * frames + f, me],
            z_send.at[f, j], z_recv.at[f, j], (team, to),
        )

    def q_copy(f, j):
        to = lax.rem(me + j, groups)
        return remote(
            q_ref.at[f, to], q_out.at[f, me], q_send.at[f, j], q_recv.at[f, j], (team, to)
        )

    def piece(owner, f, j):
        return pairs.at[owner * frames + f, lax.rem(me + groups - j, groups)]

    def f_copy(k, f, j):
        src = kv_ref.at[f, me] if j == 0 else piece(team, f, j)
        return remote(
            src, piece(team, f, j), f_send.at[k, f, j], f_recv.at[k, f, j], (direct[k][0], me)
        )

    def r_copy(f, j):
        origin, to = (beside, across) if f % 2 == 0 else (across, beside)
        here = piece(origin, f, j)
        return remote(here, here, r_send.at[f, j], r_recv.at[f, j], (to, me))

    own = []
    for f in range(frames):
        own.append(
            pltpu.make_async_copy(kv_ref.at[f, me], pairs.at[team * frames + f, me], own_sem.at[0, f])
        )
        own.append(pltpu.make_async_copy(q_ref.at[f, me], q_out.at[f, me], own_sem.at[1, f]))
    schedule = [(f, j) for j in [0] + order for f in range(frames)]
    for f, j in schedule:
        if j:
            z_copy(f, j).start()
    for f, j in schedule:
        if j:
            q_copy(f, j).start()
    for copy in own:
        copy.start()
    lag = 2 * frames
    for n in range(len(schedule) + lag):
        if n < len(schedule):
            f, j = schedule[n]
            if j:
                z_copy(f, j).wait_recv()
            for k in range(len(direct)):
                f_copy(k, f, j).start()
        if n >= lag and square:
            f, j = schedule[n - lag]
            f_copy(f % 2, f, j).wait_recv()
            r_copy(f, j).start()
    for f, j in schedule:
        for k in range(len(direct)):
            f_copy(k, f, j).wait_send()
            if not (square and k == f % 2):
                f_copy(k, f, j).wait_recv()
        if square:
            r_copy(f, j).wait()
        if j:
            z_copy(f, j).wait_send()
            q_copy(f, j).wait()
    for copy in own:
        copy.wait()


def exchange(queries, own_pairs, groups, teams):
    frames = queries.shape[0]
    sems = lambda *shape: pltpu.SemaphoreType.DMA(shape)
    hops = 2 if teams == 4 else teams - 1
    vmem = pl.BlockSpec(memory_space=pltpu.VMEM)
    anywhere = pl.BlockSpec(memory_space=pl.ANY)
    return pl.pallas_call(
        functools.partial(exchange_kernel, groups, teams),
        in_specs=[vmem, vmem],
        out_specs=[anywhere, anywhere],
        out_shape=[
            jax.ShapeDtypeStruct(queries.shape, bf16),
            jax.ShapeDtypeStruct((teams * frames,) + own_pairs.shape[1:], bf16),
        ],
        scratch_shapes=[sems(2, frames)]
        + [sems(frames, groups)] * 4
        + [sems(hops, frames, groups)] * 2
        + [sems(frames, groups)] * 2,
        compiler_params=pltpu.CompilerParams(collective_id=0, has_side_effects=True),
        name="exchange",
    )(queries, own_pairs)


def hand_back_kernel(groups, src, dst, own_sem, send, recv):
    team, me = lax.axis_index("frame"), lax.axis_index("head")
    order = near_first(groups)
    greet([(team, lax.rem(me + j, groups)) for j in order])
    copies = []
    for j in reversed(order):
        to = lax.rem(me + j, groups)
        copies.append(
            pltpu.make_async_remote_copy(
                src_ref=src.at[:, to], dst_ref=dst.at[me],
                send_sem=send.at[j], recv_sem=recv.at[j],
                device_id=(team, to), device_id_type=MESH,
            )
        )
    copies.append(pltpu.make_async_copy(src.at[:, me], dst.at[me], own_sem))
    for copy in copies:
        copy.start()
    for copy in copies:
        copy.wait()


def hand_back(attended):
    frames, groups, strip, width = attended.shape
    vmem = pl.BlockSpec(memory_space=pltpu.VMEM)
    return pl.pallas_call(
        functools.partial(hand_back_kernel, groups),
        in_specs=[vmem],
        out_specs=vmem,
        out_shape=jax.ShapeDtypeStruct((groups, frames, strip, width), bf16),
        scratch_shapes=[pltpu.SemaphoreType.DMA] + [pltpu.SemaphoreType.DMA((groups,))] * 2,
        compiler_params=pltpu.CompilerParams(collective_id=1, has_side_effects=True),
        name="hand_back",
    )(attended)


def attend_kernel(local_heads, head_dim, span, lists, counts, q_ref, kv_ref, o_ref):
    b = pl.program_id(0)
    count = counts[b]
    pair = 2 * head_dim
    v_at = local_heads * pair
    v_width = local_heads * head_dim
    first = lax.broadcasted_iota(jnp.int32, (BLOCK, pair), 1) < head_dim
    stacked = []
    for h in range(local_heads):
        coded = q_ref[:, h * pair : (h + 1) * pair].astype(f32)
        turned = pltpu.roll(coded, head_dim, 1)
        high, low = jnp.where(first, coded, turned), jnp.where(first, turned, coded)
        stacked.append(jnp.concatenate([high, low], axis=0).astype(bf16))

    def chunk(c, carry):
        offsets = []
        valid = []
        for t in range(span):
            slot = c * span + t
            block = lists[b, jnp.minimum(slot, count - 1)]
            offsets.append(pl.multiple_of(block * BLOCK, BLOCK))
            valid.append(slot < count)
        values = jnp.concatenate(
            [kv_ref[pl.ds(at, BLOCK), v_at : v_at + v_width] for at in offsets], axis=0
        )
        out = []
        for h in range(local_heads):
            top, total, blend = carry[h]
            scores = []
            for at, ok in zip(offsets, valid):
                keys = kv_ref[pl.ds(at, BLOCK), h * pair : (h + 1) * pair]
                both = lax.dot_general(
                    stacked[h], keys, (((1,), (1,)), ((), ())), preferred_element_type=f32
                )
                scores.append(jnp.where(ok, both[:BLOCK] + both[BLOCK:], -jnp.inf))
            peak = functools.reduce(jnp.maximum, scores)
            new_top = jnp.maximum(top, jnp.max(peak, axis=1, keepdims=True))
            scale = jnp.exp(top - new_top)
            weights = [jnp.exp(s - new_top) for s in scores]
            total = total * scale + functools.reduce(jnp.add, weights)
            packed = jnp.concatenate([w.astype(bf16) for w in weights], axis=1)
            blend = blend * scale + mxu(packed, values)
            out.append((new_top, total, blend))
        return tuple(out)

    start = tuple(
        (
            jnp.full((BLOCK, 1), -jnp.inf, f32),
            jnp.zeros((BLOCK, BLOCK), f32),
            jnp.zeros((BLOCK, v_width), f32),
        )
        for _ in range(local_heads)
    )
    final = lax.fori_loop(0, (count + span - 1) // span, chunk, start)
    owner = lax.broadcasted_iota(jnp.int32, (BLOCK, v_width), 1) // head_dim
    result = jnp.zeros((BLOCK, v_width), f32)
    for h in range(local_heads):
        _, total, blend = final[h]
        ready = blend / jnp.sum(total, axis=1, keepdims=True)
        result = jnp.where(owner == h, ready, result)
    o_ref[...] = result.astype(bf16)


def attend(queries, pairs, lists, counts, local_heads, head_dim):
    blocks, slots = lists.shape
    span = -(-slots // (-(-slots // 7)))
    width = local_heads * head_dim
    return pl.pallas_call(
        functools.partial(attend_kernel, local_heads, head_dim, span),
        grid_spec=pltpu.PrefetchScalarGridSpec(
            num_scalar_prefetch=2,
            grid=(blocks,),
            in_specs=[
                pl.BlockSpec((BLOCK, queries.shape[1]), lambda i, *_: (i, 0)),
                pl.BlockSpec(pairs.shape, lambda i, *_: (0, 0), pipeline_mode=pl.Buffered(1)),
            ],
            out_specs=pl.BlockSpec((BLOCK, width), lambda i, *_: (i, 0)),
        ),
        out_shape=jax.ShapeDtypeStruct((blocks * BLOCK, width), bf16),
        compiler_params=pltpu.CompilerParams(vmem_limit_bytes=48 << 20),
        name="attend",
    )(lists, counts, queries, pairs)


def scatter_order(teams, halves, k):
    far = halves - 1 - lax.rem(k, halves)
    turn = lax.rem(k // halves + 1 + 2 * far, teams)
    return turn, far


def front_kernel(
    teams, groups, slots, x_hbm, w_hbm, lists_hbm, counts_hbm, out_hbm, gain_hbm, proj_hbm, ext_ref,
    w_buf, x_hi, x_lo, msg, msg_scale, got, got_scale, q_ref, kv_ref, stream, out_buf,
    ready, gain_ref, proj_ref, sent, back, lists_all, counts_all, lists, counts,
    w_sem, l_sem, i_sem, m_send, m_recv, s_send, s_recv, f_send, f_recv, a_send, a_recv,
    i_send, i_recv, h_send, h_recv,
):
    planes = groups // 2
    halves = planes // 2
    pairs = teams * halves
    chips = teams * planes
    lanes = msg.shape[-1]
    head_dim = lanes // 2
    columns = 3 * lanes
    rows = stream.shape[0]
    channels = proj_ref.shape[-1]
    team, group = lax.axis_index("frame"), lax.axis_index("head")
    plane, core = group // 2, lax.rem(group, 2)
    half, parity = plane // 2, lax.rem(plane, 2)
    me = team * planes + plane
    sibling = (team, group + 1 - 2 * core)
    above = (team, lax.rem(group + groups - 1, groups))
    below = (team, lax.rem(group + 1, groups))

    def place(k):
        turn, far = scatter_order(teams, halves, k)
        return lax.rem(team + turn, teams), lax.rem(half + far, halves)

    def weight(k):
        to_team, to_half = place(k)
        at = pl.multiple_of((to_team * halves + to_half) * columns, columns)
        return pltpu.make_async_copy(w_hbm.at[:, pl.ds(at, columns)], w_buf.at[k], w_sem.at[k])

    load_x = pltpu.make_async_copy(x_hbm, stream, l_sem.at[0])
    load_out = [
        pltpu.make_async_copy(out_hbm, out_buf, l_sem.at[1]),
        pltpu.make_async_copy(gain_hbm, gain_ref, l_sem.at[4]),
        pltpu.make_async_copy(proj_hbm, proj_ref, l_sem.at[5]),
    ]
    load_lists = [
        pltpu.make_async_copy(lists_hbm, lists_all.at[team], l_sem.at[2]),
        pltpu.make_async_copy(counts_hbm, counts_all.at[team], l_sem.at[3]),
    ]
    load_x.start()
    for k in range(pairs):
        weight(k).start()
    for copy in load_lists:
        copy.start()
    for copy in load_out:
        copy.start()

    barrier = pltpu.get_barrier_semaphore()
    for n in range(1, chips):
        peer = (lax.rem(team + n // planes, teams), lax.rem(plane + n % planes, planes) * 2 + core)
        pl.semaphore_signal(barrier, inc=1, device_id=peer, device_id_type=MESH)
    for peer in (above, below):
        pl.semaphore_signal(barrier, inc=1, device_id=peer, device_id_type=MESH)

    first = lax.broadcasted_iota(jnp.int32, (rows, lanes), 1) < head_dim
    lane = lax.broadcasted_iota(jnp.int32, (BLOCK, lanes), 1)
    near = lane < head_dim
    top = 32766.0

    def message(to_team, to_plane):
        to = to_team * planes + to_plane
        target = (to_team, to_plane * 2 + core)
        return [
            pltpu.make_async_remote_copy(
                src_ref=msg.at[to], dst_ref=got.at[me],
                send_sem=m_send.at[to], recv_sem=m_recv.at[me],
                device_id=target, device_id_type=MESH,
            ),
            pltpu.make_async_remote_copy(
                src_ref=msg_scale.at[to], dst_ref=got_scale.at[me],
                send_sem=s_send.at[to], recv_sem=s_recv.at[me],
                device_id=target, device_id_type=MESH,
            ),
        ]

    def peak(value):
        return jnp.maximum(jnp.max(jnp.abs(value), axis=1, keepdims=True), 1e-30)

    def encode(k):
        weight(k).wait()
        w_hi, w_lo = split_hi_lo(w_buf[k])
        acc = mxu(x_hi[...], w_lo) + mxu(x_lo[...], w_hi)
        acc = acc + mxu(x_hi[...], w_hi)
        p0, p1, p2 = [acc[:, n * lanes : (n + 1) * lanes] for n in range(3)]
        t0, t1 = pltpu.roll(p0, head_dim, 1), pltpu.roll(p1, head_dim, 1)
        key_value = [jnp.where(first, t0, t1), p2]
        up, down = slice(0, BLOCK), slice(BLOCK, 2 * BLOCK)
        query = [jnp.where(near, p0[up], t0[down]), jnp.where(near, t1[up], p1[down])]
        to_team, to_half = place(k)
        for i in range(2):
            to = to_team * planes + to_half * 2 + i
            kv, q = key_value[i], query[i]
            peak_k = peak(jnp.where(first, kv, 0.0))
            peak_v = peak(jnp.where(first, 0.0, kv))
            peak_q0 = peak(jnp.where(near, q, 0.0))
            peak_q1 = peak(jnp.where(near, 0.0, q))
            kv = kv * jnp.where(first, top / peak_k, top / peak_v)
            q = q * jnp.where(near, top / peak_q0, top / peak_q1)
            msg[to, 0:2] = jnp.round(kv).astype(jnp.int32).astype(jnp.int16).reshape(2, BLOCK, lanes)
            msg[to, 2] = jnp.round(q).astype(jnp.int32).astype(jnp.int16)
            columns_of = [peak_k[up], peak_k[down], peak_v[up], peak_v[down], peak_q0, peak_q1]
            table = jnp.zeros((BLOCK, lanes), f32)
            for n, column in enumerate(columns_of):
                table = jnp.where(lane == n, column * (1.0 / top), table)
            msg_scale[to] = jnp.transpose(table)[:8]

    def post(k):
        to_team, to_half = place(k)
        for i in range(2):
            to_plane = to_half * 2 + i
            to = to_team * planes + to_plane

            @pl.when(to != me)
            def _():
                for copy in message(to_team, to_plane):
                    copy.start()

            @pl.when(to == me)
            def _():
                got[to] = msg[to]
                got_scale[to] = msg_scale[to]

    load_x.wait()
    hi, lo = split_hi_lo(stream[...])
    x_hi[...] = hi
    x_lo[...] = lo
    encode(0)
    for copy in load_lists:
        copy.wait()
    pl.semaphore_wait(barrier, chips + 1)
    post(0)

    def list_copies(step):
        return [
            pltpu.make_async_remote_copy(
                src_ref=whole.at[team], dst_ref=whole.at[team],
                send_sem=i_send.at[n, step], recv_sem=i_recv.at[n, step],
                device_id=(lax.rem(team + step, teams), group), device_id_type=MESH,
            )
            for n, whole in enumerate((lists_all, counts_all))
        ]

    def list_arrivals(step):
        origin = lax.rem(team + teams - step, teams)
        return [
            pltpu.make_async_remote_copy(
                src_ref=whole.at[origin], dst_ref=whole.at[origin],
                send_sem=i_send.at[n, step], recv_sem=i_recv.at[n, step],
                device_id=sibling, device_id_type=MESH,
            )
            for n, whole in enumerate((lists_all, counts_all))
        ]

    for step in range(1, teams):
        for copy in list_copies(step):
            copy.start()

    def send_step(k, carry):
        encode(k)
        post(k)
        return carry

    lax.fori_loop(1, pairs, send_step, 0)

    for step in range(1, teams):
        for copy in list_arrivals(step):
            copy.wait_recv()
    to_smem = [
        pltpu.make_async_copy(lists_all, lists, i_sem.at[0]),
        pltpu.make_async_copy(counts_all, counts, i_sem.at[1]),
    ]
    for copy in to_smem:
        copy.start()

    factor = head_dim ** (-0.5) * 1.4426950408889634

    def source(n):
        far = n // (2 * teams)
        turn = lax.rem(lax.rem(n, 2 * teams) // 2 + 1 + 2 * far, teams)
        from_team = lax.rem(team + teams - turn, teams)
        from_plane = lax.rem(half + halves - far, halves) * 2 + lax.rem(parity + 1 + n, 2)
        return from_team, from_plane

    def arrival(src):
        return [
            pltpu.make_async_remote_copy(
                src_ref=msg.at[src], dst_ref=got.at[src],
                send_sem=m_send.at[src], recv_sem=m_recv.at[src],
                device_id=sibling, device_id_type=MESH,
            ),
            pltpu.make_async_remote_copy(
                src_ref=msg_scale.at[src], dst_ref=got_scale.at[src],
                send_sem=s_send.at[src], recv_sem=s_recv.at[src],
                device_id=sibling, device_id_type=MESH,
            ),
        ]

    def forward(from_team, from_plane, f, whose):
        src = from_team * planes + from_plane
        block = kv_ref.at[(from_team * 2 + f) * groups + from_plane * 2 + whose]
        return pltpu.make_async_remote_copy(
            src_ref=block, dst_ref=block,
            send_sem=f_send.at[f, src], recv_sem=f_recv.at[f, src],
            device_id=sibling, device_id_type=MESH,
        )

    def take_step(n, carry):
        from_team, from_plane = source(n)
        src = from_team * planes + from_plane

        @pl.when(src != me)
        def _():
            for copy in arrival(src):
                copy.wait_recv()

        scale = jnp.transpose(jnp.concatenate([got_scale[src]] * (BLOCK // 8), axis=0))
        for f in range(2):
            at = (from_team * 2 + f) * groups + from_plane * 2 + core
            kv = got[src, f].astype(jnp.int32).astype(f32)
            kv = kv * jnp.where(near, scale[:, f : f + 1], scale[:, 2 + f : 3 + f])
            high = kv.astype(bf16).astype(f32)
            low = pltpu.roll(kv - high, head_dim, 1)
            kv_ref[at, :, :lanes] = jnp.where(near, high, low).astype(bf16)
            value = jnp.where(near, pltpu.roll(kv, head_dim, 1), 1.0)
            kv_ref[at, :, lanes:] = value.astype(bf16)
            forward(from_team, from_plane, f, core).start()
        q = got[src, 2].astype(jnp.int32).astype(f32)
        q = q * (factor * jnp.where(near, scale[:, 4:5], scale[:, 5:6]))
        high = q.astype(bf16).astype(f32)
        low = q - high
        high_turned, low_turned = pltpu.roll(high, head_dim, 1), pltpu.roll(low, head_dim, 1)
        q_ref[src, 0, :, :lanes] = jnp.where(near, high, high_turned).astype(bf16)
        q_ref[src, 0, :, lanes:] = jnp.where(near, low, low_turned).astype(bf16)
        q_ref[src, 1, :, :lanes] = jnp.where(near, high_turned, high).astype(bf16)
        q_ref[src, 1, :, lanes:] = jnp.where(near, low_turned, low).astype(bf16)
        return carry

    lax.fori_loop(0, chips, take_step, 0)

    def end_step(n, carry):
        from_team, from_plane = source(n)
        src = from_team * planes + from_plane
        for f in range(2):
            forward(from_team, from_plane, f, 1 - core).wait_recv()
        return carry

    for copy in to_smem:
        copy.wait()
    lax.fori_loop(0, chips, end_step, 0)

    def copy_to(to_team, to_plane):
        to = to_team * planes + to_plane
        return pltpu.make_async_remote_copy(
            src_ref=sent.at[to], dst_ref=back.at[me],
            send_sem=a_send.at[to], recv_sem=a_recv.at[me],
            device_id=(to_team, to_plane * 2 + core), device_id_type=MESH,
        )

    def returned(src):
        return pltpu.make_async_remote_copy(
            src_ref=sent.at[src], dst_ref=back.at[src],
            send_sem=a_send.at[src], recv_sem=a_recv.at[src],
            device_id=sibling, device_id_type=MESH,
        )

    def attend_pair(to_team, to_half):
        items = [(to_half * 2 + i, f) for i in range(2) for f in range(2)]
        scores, values = [], []
        for to_plane, f in items:
            row = f * groups + to_plane * 2 + core
            count = counts[to_team, row]
            query = q_ref[to_team * planes + to_plane, f]
            for slot in range(slots):
                block = lists[to_team, row, slot]
                keys = kv_ref[block, :, :lanes]
                score = lax.dot_general(
                    query, jnp.concatenate([keys, keys], axis=1), (((1,), (1,)), ((), ())),
                    preferred_element_type=f32,
                )
                scores.append(score if slot == 0 else jnp.where(slot < count, score, -jnp.inf))
                values.append(kv_ref[block, :, lanes:])
        for n in range(len(items)):
            own = slice(n * slots, (n + 1) * slots)
            top_score = jnp.max(functools.reduce(jnp.maximum, scores[own]), axis=1, keepdims=True)
            packed = jnp.concatenate(
                [jnp.exp2(s - top_score).astype(bf16) for s in scores[own]], axis=1
            )
            total = mxu(packed, jnp.concatenate(values[own], axis=0))
            ready[n] = total / total[:, head_dim : head_dim + 1]
        for i in range(2):
            to_plane = to_half * 2 + i
            to = to_team * planes + to_plane
            both = jnp.where(near, ready[2 * i], pltpu.roll(ready[2 * i + 1], head_dim, 1))
            sent[to] = both.astype(bf16)

            @pl.when(to != me)
            def _():
                copy_to(to_team, to_plane).start()

            @pl.when(to == me)
            def _():
                back[to] = both.astype(bf16)

    def attend_team(k):
        to_team = lax.rem(team + k, teams)

        def part(n, carry):
            attend_pair(to_team, lax.rem(half + halves - 1 - n, halves))
            return carry

        lax.fori_loop(0, halves, part, 0)

    def absorb(k):
        from_team = lax.rem(team + teams - k, teams)
        deep = planes * head_dim
        pieces = []
        for i in range(0, planes, 2):
            at = from_team * planes + i
            for j in range(2):
                @pl.when(at + j != me)
                def _():
                    returned(at + j).wait_recv()

            one, two = back[at].astype(f32), back[at + 1].astype(f32)
            upper = jnp.where(near, one, pltpu.roll(two, head_dim, 1))
            lower = jnp.where(near, pltpu.roll(one, head_dim, 1), two)
            pieces.append(jnp.concatenate([upper, lower], axis=0).astype(bf16))
        attended = jnp.concatenate(pieces, axis=1)
        w_hi, w_lo = split_hi_lo(out_buf[pl.ds(pl.multiple_of(from_team * deep, deep), deep), :])
        stream[...] += mxu(attended, w_hi) + mxu(attended, w_lo)

    for copy in load_out:
        copy.wait()
    attend_team(1)

    def team_step(k, carry):
        attend_team(k)
        absorb(k - 1)
        return carry

    lax.fori_loop(2, teams + 1, team_step, 0)
    absorb(teams)

    p_hi, p_lo = split_hi_lo(proj_ref[...])

    def finish(spans):
        summed = jnp.concatenate([stream[f * BLOCK + at : f * BLOCK + end] for f, at, end in spans])
        centre = jnp.mean(summed, axis=-1, keepdims=True)
        centred = summed - centre
        spread = jnp.mean(centred * centred, axis=-1, keepdims=True)
        normed = centred * lax.rsqrt(spread + eps_norm) * gain_ref[...]
        n_hi, n_lo = split_hi_lo(normed)
        features = mxu(n_hi, p_lo) + mxu(n_lo, p_hi)
        features = (features + mxu(n_hi, p_hi)).astype(bf16)
        row = 0
        for f, at, end in spans:
            ext_ref[f, GRID + at : GRID + end, :] = features[row : row + end - at]
            row += end - at

    def halo(side, f):
        at = (GRID, BLOCK)[side]
        to = (GRID + BLOCK, 0)[side]
        return pltpu.make_async_remote_copy(
            src_ref=ext_ref.at[f, pl.ds(at, GRID)], dst_ref=ext_ref.at[f, pl.ds(to, GRID)],
            send_sem=h_send.at[side, f], recv_sem=h_recv.at[side, f],
            device_id=(above, below)[side], device_id_type=MESH,
        )

    edges = ((0, GRID), (BLOCK - GRID, BLOCK))
    finish([(f, at, end) for f in range(2) for at, end in edges])
    for side in range(2):
        for f in range(2):
            halo(side, f).start()
    finish([(f, GRID, BLOCK - GRID) for f in range(2)])

    def drain_step(n, carry):
        from_team, from_plane = source(n)
        src = from_team * planes + from_plane
        for f in range(2):
            forward(from_team, from_plane, f, core).wait_send()

        @pl.when(src != me)
        def _():
            for copy in arrival(src):
                copy.wait_send()
            returned(src).wait_send()

        return carry

    lax.fori_loop(0, chips, drain_step, 0)
    for step in range(1, teams):
        for copy in list_copies(step):
            copy.wait_send()
    for side in range(2):
        for f in range(2):
            halo(side, f).wait()

    blank = jnp.zeros((2, GRID, channels), bf16)

    @pl.when(group == 0)
    def _():
        ext_ref[:, 0:GRID, :] = blank

    @pl.when(group == groups - 1)
    def _():
        ext_ref[:, GRID + BLOCK :, :] = blank


def front(tokens, weight, lists, counts, out_weight, gain, proj, teams, groups):
    frames, strip, width = tokens.shape
    head_dim = width // HEADS
    lanes = 2 * head_dim
    rows = frames * strip
    chips, pairs = HEADS, HEADS // 2
    blocks, slots = lists.shape
    channels = proj.shape[1]
    dma = lambda *shape: pltpu.SemaphoreType.DMA(shape)
    vmem = pl.BlockSpec(memory_space=pltpu.VMEM)
    hbm = pl.BlockSpec(memory_space=pltpu.HBM)
    listed, counted = (teams, blocks, slots), (teams, blocks)
    return pl.pallas_call(
        functools.partial(front_kernel, teams, groups, slots),
        in_specs=[hbm] * 7,
        out_specs=vmem,
        out_shape=jax.ShapeDtypeStruct((frames, strip + 2 * GRID, channels), bf16),
        scratch_shapes=[
            pltpu.VMEM((pairs, width, 6 * head_dim), f32),
            pltpu.VMEM((rows, width), bf16),
            pltpu.VMEM((rows, width), bf16),
            pltpu.VMEM((chips, 3, BLOCK, lanes), jnp.int16),
            pltpu.VMEM((chips, 8, BLOCK), f32),
            pltpu.VMEM((chips, 3, BLOCK, lanes), jnp.int16),
            pltpu.VMEM((chips, 8, BLOCK), f32),
            pltpu.VMEM((chips, frames, BLOCK, 2 * lanes), bf16),
            pltpu.VMEM((teams * frames * groups, BLOCK, 2 * lanes), bf16),
            pltpu.VMEM((rows, width), f32),
            pltpu.VMEM((width, width), f32),
            pltpu.VMEM((4, BLOCK, lanes), f32),
            pltpu.VMEM((1, width), f32),
            pltpu.VMEM((width, channels), f32),
            pltpu.VMEM((chips, BLOCK, lanes), bf16),
            pltpu.VMEM((chips, BLOCK, lanes), bf16),
            pltpu.VMEM(listed, jnp.int32),
            pltpu.VMEM(counted, jnp.int32),
            pltpu.SMEM(listed, jnp.int32),
            pltpu.SMEM(counted, jnp.int32),
            dma(pairs), dma(6), dma(2),
        ]
        + [dma(chips)] * 4
        + [dma(frames, chips)] * 2
        + [dma(chips)] * 2
        + [dma(2, teams)] * 2
        + [dma(2, 2)] * 2,
        compiler_params=pltpu.CompilerParams(
            collective_id=0, has_side_effects=True, vmem_limit_bytes=56 << 20
        ),
        name="front",
    )(tokens.reshape(rows, width), weight, lists, counts, out_weight, gain.reshape(1, width), proj)


def head_kernel(
    token_rows, feat_ref, up_hbm, conv_hbm, bias_ref, out_ref,
    up_ref, conv_ref, up_map, act_map, hid_map, flat, sem,
):
    channels = feat_ref.shape[-1]
    ext = token_rows + 2
    pixel_cols = 4 * GRID
    loads = [
        pltpu.make_async_copy(up_hbm, up_ref, sem.at[0]),
        pltpu.make_async_copy(conv_hbm, conv_ref, sem.at[1]),
    ]

    @pl.when(pl.program_id(0) == 0)
    def _():
        for copy in loads:
            copy.start()
        loads[0].wait()

    def moved(block, step):
        rows = block.shape[0]
        column = lax.broadcasted_iota(jnp.int32, block.shape, 0) % GRID
        turned = pltpu.roll(block, step % rows, 0)
        return jnp.where(column == (0 if step > 0 else GRID - 1), 0.0, turned)

    feat = feat_ref[0]
    for a in range(4):
        for e in range(4):
            at = (4 * a + e) * channels
            lifted = mxu(feat, up_ref[:, at : at + channels])
            plain = lifted.astype(bf16)
            active = jnp.maximum(plain, jnp.zeros((), bf16))
            rim = None
            if e == 0:
                rim, rim_at = jnp.maximum(moved(lifted, -1), 0.0).astype(bf16), 5 * GRID
            if e == 3:
                rim, rim_at = jnp.maximum(moved(lifted, 1), 0.0).astype(bf16), 0
            for r in range(ext):
                own = slice(r * GRID, (r + 1) * GRID)
                up_map[4 * r + a, e * GRID : (e + 1) * GRID, :] = plain[own]
                act_map[4 * r + a, (e + 1) * GRID : (e + 2) * GRID, :] = active[own]
                if rim is not None:
                    act_map[4 * r + a, rim_at : rim_at + GRID, :] = rim[own]

    @pl.when(pl.program_id(0) == 0)
    def _():
        loads[1].wait()

    def conv_rows(source, start, rows, which):
        taps = [
            source[start + dy : start + dy + rows, dx * GRID : dx * GRID + pixel_cols, :].reshape(
                rows * pixel_cols, channels
            )
            for dy in range(3)
            for dx in range(3)
        ]
        weight = conv_ref[which].reshape(9 * channels, channels)
        return mxu(jnp.concatenate(taps, axis=1), weight) + bias_ref[which][None, :]

    hidden_rows = 4 * token_rows + 2
    group = divisor_upto(hidden_rows, 3)
    top = lax.axis_index("head") == 0
    bottom = lax.axis_index("head") == lax.axis_size("head") - 1
    for g in range(hidden_rows // group):
        value = jnp.maximum(conv_rows(act_map, g * group + 2, group, 0), 0.0)
        for r in range(group):
            y = g * group + r
            row = value[r * pixel_cols : (r + 1) * pixel_cols]
            hid_map[y, GRID : GRID + pixel_cols, :] = row.astype(bf16)
            hid_map[y, 0:GRID, :] = moved(row[3 * GRID :], 1).astype(bf16)
            hid_map[y, 5 * GRID :, :] = moved(row[:GRID], -1).astype(bf16)

    @pl.when(top)
    def _():
        hid_map[0] = jnp.zeros(hid_map.shape[1:], bf16)

    @pl.when(bottom)
    def _():
        hid_map[hidden_rows - 1] = jnp.zeros(hid_map.shape[1:], bf16)

    out_rows = 4 * token_rows
    group2 = divisor_upto(out_rows, 4)
    lanes = 128
    for g in range(out_rows // group2):
        value = conv_rows(hid_map, g * group2, group2, 1)
        for r in range(group2):
            y = g * group2 + r
            row = value[r * pixel_cols : (r + 1) * pixel_cols] + up_map[y + 4].astype(f32)
            for n in range(channels // lanes):
                at = slice(n * lanes, (n + 1) * lanes)
                for e in range(4):
                    piece = row[e * GRID : (e + 1) * GRID, at]
                    flat[y % 4, n, pl.ds(e, GRID, stride=4), :] = piece
                out_ref[0, y, :, at] = flat[y % 4, n].astype(bf16)


def predict(features, up_weight, conv_weight, conv_bias, token_rows):
    frames, ext_tokens, channels = features.shape
    pixel_rows, pixel_cols = 4 * token_rows, 4 * GRID
    once = pl.Buffered(1)
    anywhere = pl.BlockSpec(memory_space=pl.ANY)
    return pl.pallas_call(
        functools.partial(head_kernel, token_rows),
        grid=(frames,),
        in_specs=[
            pl.BlockSpec((1, ext_tokens, channels), lambda i: (i, 0, 0)),
            anywhere,
            anywhere,
            pl.BlockSpec(conv_bias.shape, lambda i: (0, 0), pipeline_mode=once),
        ],
        out_specs=pl.BlockSpec((1, pixel_rows, pixel_cols, channels), lambda i: (i, 0, 0, 0)),
        scratch_shapes=[
            pltpu.VMEM(up_weight.shape, bf16),
            pltpu.VMEM(conv_weight.shape, bf16),
            pltpu.VMEM((pixel_rows + 8, pixel_cols, channels), bf16),
            pltpu.VMEM((pixel_rows + 8, pixel_cols + 2 * GRID, channels), bf16),
            pltpu.VMEM((pixel_rows + 2, pixel_cols + 2 * GRID, channels), bf16),
            pltpu.VMEM((4, channels // 128, pixel_cols, 128), f32),
            pltpu.SemaphoreType.DMA((2,)),
        ],
        out_shape=jax.ShapeDtypeStruct((frames, pixel_rows, pixel_cols, channels), bf16),
        compiler_params=pltpu.CompilerParams(vmem_limit_bytes=56 << 20),
        name="head",
    )(features, up_weight, conv_weight, conv_bias)


def layer_norm(rows, gain):
    centre = jnp.mean(rows, axis=-1, keepdims=True)
    centred = rows - centre
    spread = jnp.mean(centred * centred, axis=-1, keepdims=True)
    return centred * lax.rsqrt(spread + eps_norm) * gain


def by_teams(
    tokens, qkv_weight, out_weight, norm_gain, proj_weight, block_lists, block_counts
):
    local_frames, strip_tokens, model_width = tokens.shape
    head_groups = lax.axis_size("head")
    local_heads = HEADS // head_groups
    head_dim = model_width // HEADS
    own_queries, own_pairs = project(tokens, qkv_weight, head_groups, head_dim)
    queries, all_pairs = exchange(own_queries, own_pairs, head_groups, lax.axis_size("frame"))
    queries = queries.reshape(-1, queries.shape[-1])
    all_pairs = all_pairs.reshape(-1, all_pairs.shape[-1])
    attended = attend(queries, all_pairs, block_lists, block_counts, local_heads, head_dim)
    attended = attended.reshape(local_frames, head_groups, strip_tokens, local_heads * head_dim)
    attended = hand_back(attended).reshape(head_groups, -1, local_heads * head_dim)
    attended = jnp.transpose(attended, (1, 0, 2)).reshape(-1, model_width)
    stream = tokens.reshape(-1, model_width) + jnp.dot(
        attended.astype(f32), out_weight, precision=highest, preferred_element_type=f32
    )
    normed = layer_norm(stream, norm_gain)
    features = jnp.dot(
        normed, proj_weight, precision=highest, preferred_element_type=f32
    ).astype(bf16)
    channels = features.shape[1]
    features = features.reshape(local_frames, strip_tokens, channels)
    forward = [(i, i + 1) for i in range(head_groups - 1)]
    backward = [(i + 1, i) for i in range(head_groups - 1)]
    above = lax.ppermute(features[:, strip_tokens - GRID :], "head", forward)
    below = lax.ppermute(features[:, :GRID], "head", backward)
    return jnp.concatenate([above, features, below], axis=1)


def on_device(
    tokens,
    qkv_weight,
    out_weight,
    norm_gain,
    proj_weight,
    up_weight,
    conv_weight,
    conv_bias,
    block_lists,
    block_counts,
):
    local_frames, strip_tokens, model_width = tokens.shape
    groups, teams = lax.axis_size("head"), lax.axis_size("frame")
    one_head_a_chip = (
        teams * groups == 2 * HEADS and groups % 4 == 0 and strip_tokens == BLOCK and local_frames == 2
        and model_width == 64 * HEADS
    )
    if one_head_a_chip:
        extended = front(
            tokens, qkv_weight, block_lists, block_counts, out_weight, norm_gain, proj_weight,
            teams, groups,
        )
    else:
        extended = by_teams(
            tokens, qkv_weight, out_weight, norm_gain, proj_weight, block_lists, block_counts
        )
    return predict(extended, up_weight, conv_weight, conv_bias, strip_tokens // GRID)


def solution(mesh):
    in_specs = (
        P("frame", "head", None),
        P(),
        P(),
        P(),
        P(),
        P(),
        P(),
        P(),
        P("frame", None),
        P("frame"),
    )
    out_specs = P("frame", "head", None, None)
    return jax.shard_map(
        on_device, mesh=mesh, in_specs=in_specs, out_specs=out_specs, check_vma=False
    )
```

```python
import functools

import jax
import jax.numpy as jnp
from jax import lax
from jax.experimental import pallas as pl
from jax.experimental.pallas import tpu as pltpu
from jax.sharding import PartitionSpec as P

HEADS = 16
GRID = 32
BLOCK = 128
eps_norm = 1e-05
highest = lax.Precision.HIGHEST
f32 = jnp.float32
bf16 = jnp.bfloat16


def divisor_upto(count, most):
    return max(d for d in range(1, most + 1) if count % d == 0)


def split_hi_lo(value):
    hi = value.astype(bf16)
    return hi, (value - hi.astype(f32)).astype(bf16)


def mxu(a, b):
    return jnp.dot(a, b, preferred_element_type=f32)


def qkv_kernel(local_heads, head_dim, x_ref, w_ref, q_ref, kv_ref, x_hi, x_lo):
    @pl.when(pl.program_id(0) == 0)
    def _():
        hi, lo = split_hi_lo(x_ref[...])
        x_hi[...] = hi
        x_lo[...] = lo

    w_hi, w_lo = split_hi_lo(w_ref[...])
    acc = mxu(x_hi[...], w_lo) + mxu(x_lo[...], w_hi)
    acc = acc + mxu(x_hi[...], w_hi)
    pair = 2 * head_dim
    frames, _, strip, _ = q_ref.shape
    rows = frames * strip
    first = lax.broadcasted_iota(jnp.int32, (rows, pair), 1) < head_dim
    parts = [acc[:, n * pair : (n + 1) * pair] for n in range(3)]
    turned = [pltpu.roll(part, head_dim, 1) for part in parts]

    def coded(value):
        rest = value - value.astype(bf16).astype(f32)
        return jnp.where(first, value, rest).astype(bf16).reshape(frames, strip, pair)

    factor = head_dim ** (-0.5)
    queries = [
        coded(jnp.where(first, parts[0], turned[0]) * factor),
        coded(jnp.where(first, turned[1], parts[1]) * factor),
    ]
    keys = [
        coded(jnp.where(first, turned[0], parts[0])),
        coded(jnp.where(first, parts[2], turned[2])),
    ]
    if local_heads == 2:
        for h in range(2):
            q_ref[:, 0, :, h * pair : (h + 1) * pair] = queries[h]
            kv_ref[:, 0, :, h * pair : (h + 1) * pair] = keys[h]
        values = jnp.where(first, parts[1], parts[2]).astype(bf16)
        kv_ref[:, 0, :, 2 * pair :] = values.reshape(frames, strip, pair)
    else:
        for h, values in enumerate((parts[1], turned[2])):
            q_ref[:, h] = queries[h]
            kv_ref[:, h, :, :pair] = keys[h]
            values = values[:, :head_dim].astype(bf16)
            kv_ref[:, h, :, pair:] = values.reshape(frames, strip, head_dim)


def project(tokens, weight, head_groups, head_dim):
    frames, strip, width = tokens.shape
    local_heads = HEADS // head_groups
    share = 2 // local_heads
    columns = 6 * head_dim
    q_width, kv_width = local_heads * 2 * head_dim, local_heads * 3 * head_dim
    return pl.pallas_call(
        functools.partial(qkv_kernel, local_heads, head_dim),
        grid=(HEADS // 2,),
        in_specs=[
            pl.BlockSpec((frames * strip, width), lambda i: (0, 0)),
            pl.BlockSpec((width, columns), lambda i: (0, i)),
        ],
        out_specs=[
            pl.BlockSpec((frames, share, strip, q_width), lambda i: (0, i, 0, 0)),
            pl.BlockSpec((frames, share, strip, kv_width), lambda i: (0, i, 0, 0)),
        ],
        out_shape=[
            jax.ShapeDtypeStruct((frames, head_groups, strip, q_width), bf16),
            jax.ShapeDtypeStruct((frames, head_groups, strip, kv_width), bf16),
        ],
        scratch_shapes=[pltpu.VMEM((frames * strip, width), bf16)] * 2,
        compiler_params=pltpu.CompilerParams(vmem_limit_bytes=48 << 20),
        name="qkv",
    )(tokens.reshape(-1, width), weight)


MESH = pl.DeviceIdType.MESH


def near_first(count):
    return sorted(range(1, count), key=lambda j: (min(j, count - j), j))


def greet(peers):
    barrier = pltpu.get_barrier_semaphore()
    for peer in peers:
        pl.semaphore_signal(barrier, inc=1, device_id=peer, device_id_type=MESH)
    pl.semaphore_wait(barrier, len(peers))


def exchange_kernel(
    groups, teams, q_ref, kv_ref, q_out, pairs, own_sem,
    q_send, q_recv, z_send, z_recv, f_send, f_recv, r_send, r_recv,
):
    frames = q_ref.shape[0]
    team, me = lax.axis_index("frame"), lax.axis_index("head")
    square = teams == 4
    if square:
        side = lax.rem(team, 2)
        beside, across = team + 1 - 2 * side, lax.rem(team + 2, 4)
        direct = [(beside, beside), (across, across)]
    else:
        direct = [
            (lax.rem(team + k, teams), lax.rem(team + teams - k, teams)) for k in range(1, teams)
        ]
    order = near_first(groups)
    peers = [(team, lax.rem(me + j, groups)) for j in order] + [(to, me) for to, _ in direct]
    greet(peers)

    def remote(src, dst, send, recv, target):
        return pltpu.make_async_remote_copy(
            src_ref=src, dst_ref=dst, send_sem=send, recv_sem=recv,
            device_id=target, device_id_type=MESH,
        )

    def z_copy(f, j):
        to = lax.rem(me + j, groups)
        return remote(
            kv_ref.at[f, to], pairs.at[team * frames + f, me],
            z_send.at[f, j], z_recv.at[f, j], (team, to),
        )

    def q_copy(f, j):
        to = lax.rem(me + j, groups)
        return remote(
            q_ref.at[f, to], q_out.at[f, me], q_send.at[f, j], q_recv.at[f, j], (team, to)
        )

    def piece(owner, f, j):
        return pairs.at[owner * frames + f, lax.rem(me + groups - j, groups)]

    def f_copy(k, f, j):
        src = kv_ref.at[f, me] if j == 0 else piece(team, f, j)
        return remote(
            src, piece(team, f, j), f_send.at[k, f, j], f_recv.at[k, f, j], (direct[k][0], me)
        )

    def r_copy(f, j):
        origin, to = (beside, across) if f % 2 == 0 else (across, beside)
        here = piece(origin, f, j)
        return remote(here, here, r_send.at[f, j], r_recv.at[f, j], (to, me))

    own = []
    for f in range(frames):
        own.append(
            pltpu.make_async_copy(kv_ref.at[f, me], pairs.at[team * frames + f, me], own_sem.at[0, f])
        )
        own.append(pltpu.make_async_copy(q_ref.at[f, me], q_out.at[f, me], own_sem.at[1, f]))
    schedule = [(f, j) for j in [0] + order for f in range(frames)]
    for f, j in schedule:
        if j:
            z_copy(f, j).start()
    for f, j in schedule:
        if j:
            q_copy(f, j).start()
    for copy in own:
        copy.start()
    lag = 2 * frames
    for n in range(len(schedule) + lag):
        if n < len(schedule):
            f, j = schedule[n]
            if j:
                z_copy(f, j).wait_recv()
            for k in range(len(direct)):
                f_copy(k, f, j).start()
        if n >= lag and square:
            f, j = schedule[n - lag]
            f_copy(f % 2, f, j).wait_recv()
            r_copy(f, j).start()
    for f, j in schedule:
        for k in range(len(direct)):
            f_copy(k, f, j).wait_send()
            if not (square and k == f % 2):
                f_copy(k, f, j).wait_recv()
        if square:
            r_copy(f, j).wait()
        if j:
            z_copy(f, j).wait_send()
            q_copy(f, j).wait()
    for copy in own:
        copy.wait()


def exchange(queries, own_pairs, groups, teams):
    frames = queries.shape[0]
    sems = lambda *shape: pltpu.SemaphoreType.DMA(shape)
    hops = 2 if teams == 4 else teams - 1
    vmem = pl.BlockSpec(memory_space=pltpu.VMEM)
    anywhere = pl.BlockSpec(memory_space=pl.ANY)
    return pl.pallas_call(
        functools.partial(exchange_kernel, groups, teams),
        in_specs=[vmem, vmem],
        out_specs=[anywhere, anywhere],
        out_shape=[
            jax.ShapeDtypeStruct(queries.shape, bf16),
            jax.ShapeDtypeStruct((teams * frames,) + own_pairs.shape[1:], bf16),
        ],
        scratch_shapes=[sems(2, frames)]
        + [sems(frames, groups)] * 4
        + [sems(hops, frames, groups)] * 2
        + [sems(frames, groups)] * 2,
        compiler_params=pltpu.CompilerParams(collective_id=0, has_side_effects=True),
        name="exchange",
    )(queries, own_pairs)


def hand_back_kernel(groups, src, dst, own_sem, send, recv):
    team, me = lax.axis_index("frame"), lax.axis_index("head")
    order = near_first(groups)
    greet([(team, lax.rem(me + j, groups)) for j in order])
    copies = []
    for j in reversed(order):
        to = lax.rem(me + j, groups)
        copies.append(
            pltpu.make_async_remote_copy(
                src_ref=src.at[:, to], dst_ref=dst.at[me],
                send_sem=send.at[j], recv_sem=recv.at[j],
                device_id=(team, to), device_id_type=MESH,
            )
        )
    copies.append(pltpu.make_async_copy(src.at[:, me], dst.at[me], own_sem))
    for copy in copies:
        copy.start()
    for copy in copies:
        copy.wait()


def hand_back(attended):
    frames, groups, strip, width = attended.shape
    vmem = pl.BlockSpec(memory_space=pltpu.VMEM)
    return pl.pallas_call(
        functools.partial(hand_back_kernel, groups),
        in_specs=[vmem],
        out_specs=vmem,
        out_shape=jax.ShapeDtypeStruct((groups, frames, strip, width), bf16),
        scratch_shapes=[pltpu.SemaphoreType.DMA] + [pltpu.SemaphoreType.DMA((groups,))] * 2,
        compiler_params=pltpu.CompilerParams(collective_id=1, has_side_effects=True),
        name="hand_back",
    )(attended)


def attend_kernel(local_heads, head_dim, span, lists, counts, q_ref, kv_ref, o_ref):
    b = pl.program_id(0)
    count = counts[b]
    pair = 2 * head_dim
    v_at = local_heads * pair
    v_width = local_heads * head_dim
    first = lax.broadcasted_iota(jnp.int32, (BLOCK, pair), 1) < head_dim
    stacked = []
    for h in range(local_heads):
        coded = q_ref[:, h * pair : (h + 1) * pair].astype(f32)
        turned = pltpu.roll(coded, head_dim, 1)
        high, low = jnp.where(first, coded, turned), jnp.where(first, turned, coded)
        stacked.append(jnp.concatenate([high, low], axis=0).astype(bf16))

    def chunk(c, carry):
        offsets = []
        valid = []
        for t in range(span):
            slot = c * span + t
            block = lists[b, jnp.minimum(slot, count - 1)]
            offsets.append(pl.multiple_of(block * BLOCK, BLOCK))
            valid.append(slot < count)
        values = jnp.concatenate(
            [kv_ref[pl.ds(at, BLOCK), v_at : v_at + v_width] for at in offsets], axis=0
        )
        out = []
        for h in range(local_heads):
            top, total, blend = carry[h]
            scores = []
            for at, ok in zip(offsets, valid):
                keys = kv_ref[pl.ds(at, BLOCK), h * pair : (h + 1) * pair]
                both = lax.dot_general(
                    stacked[h], keys, (((1,), (1,)), ((), ())), preferred_element_type=f32
                )
                scores.append(jnp.where(ok, both[:BLOCK] + both[BLOCK:], -jnp.inf))
            peak = functools.reduce(jnp.maximum, scores)
            new_top = jnp.maximum(top, jnp.max(peak, axis=1, keepdims=True))
            scale = jnp.exp(top - new_top)
            weights = [jnp.exp(s - new_top) for s in scores]
            total = total * scale + functools.reduce(jnp.add, weights)
            packed = jnp.concatenate([w.astype(bf16) for w in weights], axis=1)
            blend = blend * scale + mxu(packed, values)
            out.append((new_top, total, blend))
        return tuple(out)

    start = tuple(
        (
            jnp.full((BLOCK, 1), -jnp.inf, f32),
            jnp.zeros((BLOCK, BLOCK), f32),
            jnp.zeros((BLOCK, v_width), f32),
        )
        for _ in range(local_heads)
    )
    final = lax.fori_loop(0, (count + span - 1) // span, chunk, start)
    owner = lax.broadcasted_iota(jnp.int32, (BLOCK, v_width), 1) // head_dim
    result = jnp.zeros((BLOCK, v_width), f32)
    for h in range(local_heads):
        _, total, blend = final[h]
        ready = blend / jnp.sum(total, axis=1, keepdims=True)
        result = jnp.where(owner == h, ready, result)
    o_ref[...] = result.astype(bf16)


def attend(queries, pairs, lists, counts, local_heads, head_dim):
    blocks, slots = lists.shape
    span = -(-slots // (-(-slots // 7)))
    width = local_heads * head_dim
    return pl.pallas_call(
        functools.partial(attend_kernel, local_heads, head_dim, span),
        grid_spec=pltpu.PrefetchScalarGridSpec(
            num_scalar_prefetch=2,
            grid=(blocks,),
            in_specs=[
                pl.BlockSpec((BLOCK, queries.shape[1]), lambda i, *_: (i, 0)),
                pl.BlockSpec(pairs.shape, lambda i, *_: (0, 0), pipeline_mode=pl.Buffered(1)),
            ],
            out_specs=pl.BlockSpec((BLOCK, width), lambda i, *_: (i, 0)),
        ),
        out_shape=jax.ShapeDtypeStruct((blocks * BLOCK, width), bf16),
        compiler_params=pltpu.CompilerParams(vmem_limit_bytes=48 << 20),
        name="attend",
    )(lists, counts, queries, pairs)


def scatter_order(teams, halves, k):
    far = halves - 1 - lax.rem(k, halves)
    turn = lax.rem(k // halves + 1 + 2 * far, teams)
    return turn, far


def front_kernel(
    teams, groups, slots, x_hbm, w_hbm, lists_hbm, counts_hbm, out_hbm, gain_hbm, proj_hbm, ext_ref,
    w_buf, x_hi, x_lo, msg, msg_scale, got, got_scale, q_ref, kv_ref, stream, out_buf,
    ready, gain_ref, proj_ref, sent, back, lists_all, counts_all, lists, counts,
    w_sem, l_sem, i_sem, m_send, m_recv, s_send, s_recv, f_send, f_recv, a_send, a_recv,
    i_send, i_recv, h_send, h_recv,
):
    planes = groups // 2
    halves = planes // 2
    pairs = teams * halves
    chips = teams * planes
    lanes = msg.shape[-1]
    head_dim = lanes // 2
    columns = 3 * lanes
    rows = stream.shape[0]
    channels = proj_ref.shape[-1]
    team, group = lax.axis_index("frame"), lax.axis_index("head")
    plane, core = group // 2, lax.rem(group, 2)
    half, parity = plane // 2, lax.rem(plane, 2)
    me = team * planes + plane
    sibling = (team, group + 1 - 2 * core)
    above = (team, lax.rem(group + groups - 1, groups))
    below = (team, lax.rem(group + 1, groups))

    def place(k):
        turn, far = scatter_order(teams, halves, k)
        return lax.rem(team + turn, teams), lax.rem(half + far, halves)

    def weight(k):
        to_team, to_half = place(k)
        at = pl.multiple_of((to_team * halves + to_half) * columns, columns)
        return pltpu.make_async_copy(w_hbm.at[:, pl.ds(at, columns)], w_buf.at[k], w_sem.at[k])

    load_x = pltpu.make_async_copy(x_hbm, stream, l_sem.at[0])
    load_out = [
        pltpu.make_async_copy(out_hbm, out_buf, l_sem.at[1]),
        pltpu.make_async_copy(gain_hbm, gain_ref, l_sem.at[4]),
        pltpu.make_async_copy(proj_hbm, proj_ref, l_sem.at[5]),
    ]
    load_lists = [
        pltpu.make_async_copy(lists_hbm, lists_all.at[team], l_sem.at[2]),
        pltpu.make_async_copy(counts_hbm, counts_all.at[team], l_sem.at[3]),
    ]
    load_x.start()
    for k in range(pairs):
        weight(k).start()
    for copy in load_lists:
        copy.start()
    for copy in load_out:
        copy.start()

    barrier = pltpu.get_barrier_semaphore()
    for n in range(1, chips):
        peer = (lax.rem(team + n // planes, teams), lax.rem(plane + n % planes, planes) * 2 + core)
        pl.semaphore_signal(barrier, inc=1, device_id=peer, device_id_type=MESH)
    for peer in (above, below):
        pl.semaphore_signal(barrier, inc=1, device_id=peer, device_id_type=MESH)

    first = lax.broadcasted_iota(jnp.int32, (rows, lanes), 1) < head_dim
    lane = lax.broadcasted_iota(jnp.int32, (BLOCK, lanes), 1)
    near = lane < head_dim
    top = 32766.0

    def message(to_team, to_plane):
        to = to_team * planes + to_plane
        target = (to_team, to_plane * 2 + core)
        return [
            pltpu.make_async_remote_copy(
                src_ref=msg.at[to], dst_ref=got.at[me],
                send_sem=m_send.at[to], recv_sem=m_recv.at[me],
                device_id=target, device_id_type=MESH,
            ),
            pltpu.make_async_remote_copy(
                src_ref=msg_scale.at[to], dst_ref=got_scale.at[me],
                send_sem=s_send.at[to], recv_sem=s_recv.at[me],
                device_id=target, device_id_type=MESH,
            ),
        ]

    def peak(value):
        return jnp.maximum(jnp.max(jnp.abs(value), axis=1, keepdims=True), 1e-30)

    def encode(k):
        weight(k).wait()
        w_hi, w_lo = split_hi_lo(w_buf[k])
        acc = mxu(x_hi[...], w_lo) + mxu(x_lo[...], w_hi)
        acc = acc + mxu(x_hi[...], w_hi)
        p0, p1, p2 = [acc[:, n * lanes : (n + 1) * lanes] for n in range(3)]
        t0, t1 = pltpu.roll(p0, head_dim, 1), pltpu.roll(p1, head_dim, 1)
        key_value = [jnp.where(first, t0, t1), p2]
        up, down = slice(0, BLOCK), slice(BLOCK, 2 * BLOCK)
        query = [jnp.where(near, p0[up], t0[down]), jnp.where(near, t1[up], p1[down])]
        to_team, to_half = place(k)
        for i in range(2):
            to = to_team * planes + to_half * 2 + i
            kv, q = key_value[i], query[i]
            peak_k = peak(jnp.where(first, kv, 0.0))
            peak_v = peak(jnp.where(first, 0.0, kv))
            peak_q0 = peak(jnp.where(near, q, 0.0))
            peak_q1 = peak(jnp.where(near, 0.0, q))
            kv = kv * jnp.where(first, top / peak_k, top / peak_v)
            q = q * jnp.where(near, top / peak_q0, top / peak_q1)
            msg[to, 0:2] = jnp.round(kv).astype(jnp.int32).astype(jnp.int16).reshape(2, BLOCK, lanes)
            msg[to, 2] = jnp.round(q).astype(jnp.int32).astype(jnp.int16)
            columns_of = [peak_k[up], peak_k[down], peak_v[up], peak_v[down], peak_q0, peak_q1]
            table = jnp.zeros((BLOCK, lanes), f32)
            for n, column in enumerate(columns_of):
                table = jnp.where(lane == n, column * (1.0 / top), table)
            msg_scale[to] = jnp.transpose(table)[:8]

    def post(k):
        to_team, to_half = place(k)
        for i in range(2):
            to_plane = to_half * 2 + i
            to = to_team * planes + to_plane

            @pl.when(to != me)
            def _():
                for copy in message(to_team, to_plane):
                    copy.start()

            @pl.when(to == me)
            def _():
                got[to] = msg[to]
                got_scale[to] = msg_scale[to]

    load_x.wait()
    hi, lo = split_hi_lo(stream[...])
    x_hi[...] = hi
    x_lo[...] = lo
    encode(0)
    for copy in load_lists:
        copy.wait()
    pl.semaphore_wait(barrier, chips + 1)
    post(0)

    def list_copies(step):
        return [
            pltpu.make_async_remote_copy(
                src_ref=whole.at[team], dst_ref=whole.at[team],
                send_sem=i_send.at[n, step], recv_sem=i_recv.at[n, step],
                device_id=(lax.rem(team + step, teams), group), device_id_type=MESH,
            )
            for n, whole in enumerate((lists_all, counts_all))
        ]

    def list_arrivals(step):
        origin = lax.rem(team + teams - step, teams)
        return [
            pltpu.make_async_remote_copy(
                src_ref=whole.at[origin], dst_ref=whole.at[origin],
                send_sem=i_send.at[n, step], recv_sem=i_recv.at[n, step],
                device_id=sibling, device_id_type=MESH,
            )
            for n, whole in enumerate((lists_all, counts_all))
        ]

    for step in range(1, teams):
        for copy in list_copies(step):
            copy.start()

    def send_step(k, carry):
        encode(k)
        post(k)
        return carry

    lax.fori_loop(1, pairs, send_step, 0)

    for step in range(1, teams):
        for copy in list_arrivals(step):
            copy.wait_recv()
    to_smem = [
        pltpu.make_async_copy(lists_all, lists, i_sem.at[0]),
        pltpu.make_async_copy(counts_all, counts, i_sem.at[1]),
    ]
    for copy in to_smem:
        copy.start()

    factor = head_dim ** (-0.5) * 1.4426950408889634

    def source(n):
        far = n // (2 * teams)
        turn = lax.rem(lax.rem(n, 2 * teams) // 2 + 1 + 2 * far, teams)
        from_team = lax.rem(team + teams - turn, teams)
        from_plane = lax.rem(half + halves - far, halves) * 2 + lax.rem(parity + 1 + n, 2)
        return from_team, from_plane

    def arrival(src):
        return [
            pltpu.make_async_remote_copy(
                src_ref=msg.at[src], dst_ref=got.at[src],
                send_sem=m_send.at[src], recv_sem=m_recv.at[src],
                device_id=sibling, device_id_type=MESH,
            ),
            pltpu.make_async_remote_copy(
                src_ref=msg_scale.at[src], dst_ref=got_scale.at[src],
                send_sem=s_send.at[src], recv_sem=s_recv.at[src],
                device_id=sibling, device_id_type=MESH,
            ),
        ]

    def forward(from_team, from_plane, f, whose):
        src = from_team * planes + from_plane
        block = kv_ref.at[(from_team * 2 + f) * groups + from_plane * 2 + whose]
        return pltpu.make_async_remote_copy(
            src_ref=block, dst_ref=block,
            send_sem=f_send.at[f, src], recv_sem=f_recv.at[f, src],
            device_id=sibling, device_id_type=MESH,
        )

    def take_step(n, carry):
        from_team, from_plane = source(n)
        src = from_team * planes + from_plane

        @pl.when(src != me)
        def _():
            for copy in arrival(src):
                copy.wait_recv()

        scale = jnp.transpose(jnp.concatenate([got_scale[src]] * (BLOCK // 8), axis=0))
        for f in range(2):
            at = (from_team * 2 + f) * groups + from_plane * 2 + core
            kv = got[src, f].astype(jnp.int32).astype(f32)
            kv = kv * jnp.where(near, scale[:, f : f + 1], scale[:, 2 + f : 3 + f])
            high = kv.astype(bf16).astype(f32)
            low = pltpu.roll(kv - high, head_dim, 1)
            kv_ref[at, :, :lanes] = jnp.where(near, high, low).astype(bf16)
            value = jnp.where(near, pltpu.roll(kv, head_dim, 1), 1.0)
            kv_ref[at, :, lanes:] = value.astype(bf16)
            forward(from_team, from_plane, f, core).start()
        q = got[src, 2].astype(jnp.int32).astype(f32)
        q = q * (factor * jnp.where(near, scale[:, 4:5], scale[:, 5:6]))
        high = q.astype(bf16).astype(f32)
        low = q - high
        high_turned, low_turned = pltpu.roll(high, head_dim, 1), pltpu.roll(low, head_dim, 1)
        q_ref[src, 0, :, :lanes] = jnp.where(near, high, high_turned).astype(bf16)
        q_ref[src, 0, :, lanes:] = jnp.where(near, low, low_turned).astype(bf16)
        q_ref[src, 1, :, :lanes] = jnp.where(near, high_turned, high).astype(bf16)
        q_ref[src, 1, :, lanes:] = jnp.where(near, low_turned, low).astype(bf16)
        return carry

    lax.fori_loop(0, chips, take_step, 0)

    def end_step(n, carry):
        from_team, from_plane = source(n)
        src = from_team * planes + from_plane
        for f in range(2):
            forward(from_team, from_plane, f, 1 - core).wait_recv()
        return carry

    for copy in to_smem:
        copy.wait()
    lax.fori_loop(0, chips, end_step, 0)

    def copy_to(to_team, to_plane):
        to = to_team * planes + to_plane
        return pltpu.make_async_remote_copy(
            src_ref=sent.at[to], dst_ref=back.at[me],
            send_sem=a_send.at[to], recv_sem=a_recv.at[me],
            device_id=(to_team, to_plane * 2 + core), device_id_type=MESH,
        )

    def returned(src):
        return pltpu.make_async_remote_copy(
            src_ref=sent.at[src], dst_ref=back.at[src],
            send_sem=a_send.at[src], recv_sem=a_recv.at[src],
            device_id=sibling, device_id_type=MESH,
        )

    def attend_pair(to_team, to_half):
        items = [(to_half * 2 + i, f) for i in range(2) for f in range(2)]
        scores, values = [], []
        for to_plane, f in items:
            row = f * groups + to_plane * 2 + core
            count = counts[to_team, row]
            query = q_ref[to_team * planes + to_plane, f]
            for slot in range(slots):
                block = lists[to_team, row, slot]
                keys = kv_ref[block, :, :lanes]
                score = lax.dot_general(
                    query, jnp.concatenate([keys, keys], axis=1), (((1,), (1,)), ((), ())),
                    preferred_element_type=f32,
                )
                scores.append(score if slot == 0 else jnp.where(slot < count, score, -jnp.inf))
                values.append(kv_ref[block, :, lanes:])
        for n in range(len(items)):
            own = slice(n * slots, (n + 1) * slots)
            top_score = jnp.max(functools.reduce(jnp.maximum, scores[own]), axis=1, keepdims=True)
            packed = jnp.concatenate(
                [jnp.exp2(s - top_score).astype(bf16) for s in scores[own]], axis=1
            )
            total = mxu(packed, jnp.concatenate(values[own], axis=0))
            ready[n] = total / total[:, head_dim : head_dim + 1]
        for i in range(2):
            to_plane = to_half * 2 + i
            to = to_team * planes + to_plane
            both = jnp.where(near, ready[2 * i], pltpu.roll(ready[2 * i + 1], head_dim, 1))
            sent[to] = both.astype(bf16)

            @pl.when(to != me)
            def _():
                copy_to(to_team, to_plane).start()

            @pl.when(to == me)
            def _():
                back[to] = both.astype(bf16)

    def attend_team(k):
        to_team = lax.rem(team + k, teams)

        def part(n, carry):
            attend_pair(to_team, lax.rem(half + halves - 1 - n, halves))
            return carry

        lax.fori_loop(0, halves, part, 0)

    def absorb(k):
        from_team = lax.rem(team + teams - k, teams)
        deep = planes * head_dim
        pieces = []
        for i in range(0, planes, 2):
            at = from_team * planes + i
            for j in range(2):
                @pl.when(at + j != me)
                def _():
                    returned(at + j).wait_recv()

            one, two = back[at].astype(f32), back[at + 1].astype(f32)
            upper = jnp.where(near, one, pltpu.roll(two, head_dim, 1))
            lower = jnp.where(near, pltpu.roll(one, head_dim, 1), two)
            pieces.append(jnp.concatenate([upper, lower], axis=0).astype(bf16))
        attended = jnp.concatenate(pieces, axis=1)
        w_hi, w_lo = split_hi_lo(out_buf[pl.ds(pl.multiple_of(from_team * deep, deep), deep), :])
        stream[...] += mxu(attended, w_hi) + mxu(attended, w_lo)

    for copy in load_out:
        copy.wait()
    attend_team(1)

    def team_step(k, carry):
        attend_team(k)
        absorb(k - 1)
        return carry

    lax.fori_loop(2, teams + 1, team_step, 0)
    absorb(teams)

    p_hi, p_lo = split_hi_lo(proj_ref[...])

    def finish(spans):
        summed = jnp.concatenate([stream[f * BLOCK + at : f * BLOCK + end] for f, at, end in spans])
        centre = jnp.mean(summed, axis=-1, keepdims=True)
        centred = summed - centre
        spread = jnp.mean(centred * centred, axis=-1, keepdims=True)
        normed = centred * lax.rsqrt(spread + eps_norm) * gain_ref[...]
        n_hi, n_lo = split_hi_lo(normed)
        features = mxu(n_hi, p_lo) + mxu(n_lo, p_hi)
        features = (features + mxu(n_hi, p_hi)).astype(bf16)
        row = 0
        for f, at, end in spans:
            ext_ref[f, GRID + at : GRID + end, :] = features[row : row + end - at]
            row += end - at

    def halo(side, f):
        at = (GRID, BLOCK)[side]
        to = (GRID + BLOCK, 0)[side]
        return pltpu.make_async_remote_copy(
            src_ref=ext_ref.at[f, pl.ds(at, GRID)], dst_ref=ext_ref.at[f, pl.ds(to, GRID)],
            send_sem=h_send.at[side, f], recv_sem=h_recv.at[side, f],
            device_id=(above, below)[side], device_id_type=MESH,
        )

    edges = ((0, GRID), (BLOCK - GRID, BLOCK))
    finish([(f, at, end) for f in range(2) for at, end in edges])
    for side in range(2):
        for f in range(2):
            halo(side, f).start()
    finish([(f, GRID, BLOCK - GRID) for f in range(2)])

    def drain_step(n, carry):
        from_team, from_plane = source(n)
        src = from_team * planes + from_plane
        for f in range(2):
            forward(from_team, from_plane, f, core).wait_send()

        @pl.when(src != me)
        def _():
            for copy in arrival(src):
                copy.wait_send()
            returned(src).wait_send()

        return carry

    lax.fori_loop(0, chips, drain_step, 0)
    for step in range(1, teams):
        for copy in list_copies(step):
            copy.wait_send()
    for side in range(2):
        for f in range(2):
            halo(side, f).wait()

    blank = jnp.zeros((2, GRID, channels), bf16)

    @pl.when(group == 0)
    def _():
        ext_ref[:, 0:GRID, :] = blank

    @pl.when(group == groups - 1)
    def _():
        ext_ref[:, GRID + BLOCK :, :] = blank


def front(tokens, weight, lists, counts, out_weight, gain, proj, teams, groups):
    frames, strip, width = tokens.shape
    head_dim = width // HEADS
    lanes = 2 * head_dim
    rows = frames * strip
    chips, pairs = HEADS, HEADS // 2
    blocks, slots = lists.shape
    channels = proj.shape[1]
    dma = lambda *shape: pltpu.SemaphoreType.DMA(shape)
    vmem = pl.BlockSpec(memory_space=pltpu.VMEM)
    hbm = pl.BlockSpec(memory_space=pltpu.HBM)
    listed, counted = (teams, blocks, slots), (teams, blocks)
    return pl.pallas_call(
        functools.partial(front_kernel, teams, groups, slots),
        in_specs=[hbm] * 7,
        out_specs=vmem,
        out_shape=jax.ShapeDtypeStruct((frames, strip + 2 * GRID, channels), bf16),
        scratch_shapes=[
            pltpu.VMEM((pairs, width, 6 * head_dim), f32),
            pltpu.VMEM((rows, width), bf16),
            pltpu.VMEM((rows, width), bf16),
            pltpu.VMEM((chips, 3, BLOCK, lanes), jnp.int16),
            pltpu.VMEM((chips, 8, BLOCK), f32),
            pltpu.VMEM((chips, 3, BLOCK, lanes), jnp.int16),
            pltpu.VMEM((chips, 8, BLOCK), f32),
            pltpu.VMEM((chips, frames, BLOCK, 2 * lanes), bf16),
            pltpu.VMEM((teams * frames * groups, BLOCK, 2 * lanes), bf16),
            pltpu.VMEM((rows, width), f32),
            pltpu.VMEM((width, width), f32),
            pltpu.VMEM((4, BLOCK, lanes), f32),
            pltpu.VMEM((1, width), f32),
            pltpu.VMEM((width, channels), f32),
            pltpu.VMEM((chips, BLOCK, lanes), bf16),
            pltpu.VMEM((chips, BLOCK, lanes), bf16),
            pltpu.VMEM(listed, jnp.int32),
            pltpu.VMEM(counted, jnp.int32),
            pltpu.SMEM(listed, jnp.int32),
            pltpu.SMEM(counted, jnp.int32),
            dma(pairs), dma(6), dma(2),
        ]
        + [dma(chips)] * 4
        + [dma(frames, chips)] * 2
        + [dma(chips)] * 2
        + [dma(2, teams)] * 2
        + [dma(2, 2)] * 2,
        compiler_params=pltpu.CompilerParams(
            collective_id=0, has_side_effects=True, vmem_limit_bytes=56 << 20
        ),
        name="front",
    )(tokens.reshape(rows, width), weight, lists, counts, out_weight, gain.reshape(1, width), proj)


def head_kernel(
    token_rows, feat_ref, up_ref, conv_ref, bias_ref, out_ref, up_map, act_map, hid_map, flat
):
    channels = feat_ref.shape[-1]
    ext = token_rows + 2
    pixel_cols = 4 * GRID
    def moved(block, step):
        rows = block.shape[0]
        column = lax.broadcasted_iota(jnp.int32, block.shape, 0) % GRID
        turned = pltpu.roll(block, step % rows, 0)
        return jnp.where(column == (0 if step > 0 else GRID - 1), 0.0, turned)

    feat = feat_ref[pl.program_id(0)]
    for a in range(4):
        for e in range(4):
            at = (4 * a + e) * channels
            lifted = mxu(feat, up_ref[:, at : at + channels])
            plain = lifted.astype(bf16)
            active = jnp.maximum(plain, jnp.zeros((), bf16))
            rim = None
            if e == 0:
                rim, rim_at = jnp.maximum(moved(lifted, -1), 0.0).astype(bf16), 5 * GRID
            if e == 3:
                rim, rim_at = jnp.maximum(moved(lifted, 1), 0.0).astype(bf16), 0
            for r in range(ext):
                own = slice(r * GRID, (r + 1) * GRID)
                up_map[4 * r + a, e * GRID : (e + 1) * GRID, :] = plain[own]
                act_map[4 * r + a, (e + 1) * GRID : (e + 2) * GRID, :] = active[own]
                if rim is not None:
                    act_map[4 * r + a, rim_at : rim_at + GRID, :] = rim[own]

    def conv_rows(source, start, rows, which):
        taps = [
            source[start + dy : start + dy + rows, dx * GRID : dx * GRID + pixel_cols, :].reshape(
                rows * pixel_cols, channels
            )
            for dy in range(3)
            for dx in range(3)
        ]
        weight = conv_ref[which].reshape(9 * channels, channels)
        return mxu(jnp.concatenate(taps, axis=1), weight) + bias_ref[which][None, :]

    hidden_rows = 4 * token_rows + 2
    group = divisor_upto(hidden_rows, 3)
    top = lax.axis_index("head") == 0
    bottom = lax.axis_index("head") == lax.axis_size("head") - 1
    for g in range(hidden_rows // group):
        value = jnp.maximum(conv_rows(act_map, g * group + 2, group, 0), 0.0)
        for r in range(group):
            y = g * group + r
            row = value[r * pixel_cols : (r + 1) * pixel_cols]
            hid_map[y, GRID : GRID + pixel_cols, :] = row.astype(bf16)
            hid_map[y, 0:GRID, :] = moved(row[3 * GRID :], 1).astype(bf16)
            hid_map[y, 5 * GRID :, :] = moved(row[:GRID], -1).astype(bf16)

    @pl.when(top)
    def _():
        hid_map[0] = jnp.zeros(hid_map.shape[1:], bf16)

    @pl.when(bottom)
    def _():
        hid_map[hidden_rows - 1] = jnp.zeros(hid_map.shape[1:], bf16)

    out_rows = 4 * token_rows
    group2 = divisor_upto(out_rows, 4)
    lanes = 128
    for g in range(out_rows // group2):
        value = conv_rows(hid_map, g * group2, group2, 1)
        for r in range(group2):
            y = g * group2 + r
            row = value[r * pixel_cols : (r + 1) * pixel_cols] + up_map[y + 4].astype(f32)
            for n in range(channels // lanes):
                at = slice(n * lanes, (n + 1) * lanes)
                for e in range(4):
                    piece = row[e * GRID : (e + 1) * GRID, at]
                    flat[y % 4, n, pl.ds(e, GRID, stride=4), :] = piece
                out_ref[0, y, :, at] = flat[y % 4, n].astype(bf16)


def predict(features, up_weight, conv_weight, conv_bias, token_rows):
    frames, _, channels = features.shape
    pixel_rows, pixel_cols = 4 * token_rows, 4 * GRID
    once = pl.Buffered(1)
    vmem = pl.BlockSpec(memory_space=pltpu.VMEM)
    return pl.pallas_call(
        functools.partial(head_kernel, token_rows),
        grid=(frames,),
        in_specs=[
            vmem,
            vmem,
            vmem,
            pl.BlockSpec(conv_bias.shape, lambda i: (0, 0), pipeline_mode=once),
        ],
        out_specs=pl.BlockSpec((1, pixel_rows, pixel_cols, channels), lambda i: (i, 0, 0, 0)),
        scratch_shapes=[
            pltpu.VMEM((pixel_rows + 8, pixel_cols, channels), bf16),
            pltpu.VMEM((pixel_rows + 8, pixel_cols + 2 * GRID, channels), bf16),
            pltpu.VMEM((pixel_rows + 2, pixel_cols + 2 * GRID, channels), bf16),
            pltpu.VMEM((4, channels // 128, pixel_cols, 128), f32),
        ],
        out_shape=jax.ShapeDtypeStruct((frames, pixel_rows, pixel_cols, channels), bf16),
        compiler_params=pltpu.CompilerParams(vmem_limit_bytes=20 << 20),
        name="head",
    )(features, up_weight, conv_weight, conv_bias)


def layer_norm(rows, gain):
    centre = jnp.mean(rows, axis=-1, keepdims=True)
    centred = rows - centre
    spread = jnp.mean(centred * centred, axis=-1, keepdims=True)
    return centred * lax.rsqrt(spread + eps_norm) * gain


def by_teams(
    tokens, qkv_weight, out_weight, norm_gain, proj_weight, block_lists, block_counts
):
    local_frames, strip_tokens, model_width = tokens.shape
    head_groups = lax.axis_size("head")
    local_heads = HEADS // head_groups
    head_dim = model_width // HEADS
    own_queries, own_pairs = project(tokens, qkv_weight, head_groups, head_dim)
    queries, all_pairs = exchange(own_queries, own_pairs, head_groups, lax.axis_size("frame"))
    queries = queries.reshape(-1, queries.shape[-1])
    all_pairs = all_pairs.reshape(-1, all_pairs.shape[-1])
    attended = attend(queries, all_pairs, block_lists, block_counts, local_heads, head_dim)
    attended = attended.reshape(local_frames, head_groups, strip_tokens, local_heads * head_dim)
    attended = hand_back(attended).reshape(head_groups, -1, local_heads * head_dim)
    attended = jnp.transpose(attended, (1, 0, 2)).reshape(-1, model_width)
    stream = tokens.reshape(-1, model_width) + jnp.dot(
        attended.astype(f32), out_weight, precision=highest, preferred_element_type=f32
    )
    normed = layer_norm(stream, norm_gain)
    features = jnp.dot(
        normed, proj_weight, precision=highest, preferred_element_type=f32
    ).astype(bf16)
    channels = features.shape[1]
    features = features.reshape(local_frames, strip_tokens, channels)
    forward = [(i, i + 1) for i in range(head_groups - 1)]
    backward = [(i + 1, i) for i in range(head_groups - 1)]
    above = lax.ppermute(features[:, strip_tokens - GRID :], "head", forward)
    below = lax.ppermute(features[:, :GRID], "head", backward)
    return jnp.concatenate([above, features, below], axis=1)


def on_device(
    tokens,
    qkv_weight,
    out_weight,
    norm_gain,
    proj_weight,
    up_weight,
    conv_weight,
    conv_bias,
    block_lists,
    block_counts,
):
    local_frames, strip_tokens, model_width = tokens.shape
    groups, teams = lax.axis_size("head"), lax.axis_size("frame")
    one_head_a_chip = (
        teams * groups == 2 * HEADS and groups % 4 == 0 and strip_tokens == BLOCK and local_frames == 2
        and model_width == 64 * HEADS
    )
    if one_head_a_chip:
        extended = front(
            tokens, qkv_weight, block_lists, block_counts, out_weight, norm_gain, proj_weight,
            teams, groups,
        )
    else:
        extended = by_teams(
            tokens, qkv_weight, out_weight, norm_gain, proj_weight, block_lists, block_counts
        )
    return predict(extended, up_weight, conv_weight, conv_bias, strip_tokens // GRID)


def solution(mesh):
    in_specs = (
        P("frame", "head", None),
        P(),
        P(),
        P(),
        P(),
        P(),
        P(),
        P(),
        P("frame", None),
        P("frame"),
    )
    out_specs = P("frame", "head", None, None)
    return jax.shard_map(
        on_device, mesh=mesh, in_specs=in_specs, out_specs=out_specs, check_vma=False
    )
```

```python
import functools

import jax
import jax.numpy as jnp
from jax import lax
from jax.experimental import pallas as pl
from jax.experimental.pallas import tpu as pltpu
from jax.sharding import PartitionSpec as P

HEADS = 16
GRID = 32
BLOCK = 128
eps_norm = 1e-05
highest = lax.Precision.HIGHEST
f32 = jnp.float32
bf16 = jnp.bfloat16


def divisor_upto(count, most):
    return max(d for d in range(1, most + 1) if count % d == 0)


def split_hi_lo(value):
    hi = value.astype(bf16)
    return hi, (value - hi.astype(f32)).astype(bf16)


def mxu(a, b):
    return jnp.dot(a, b, preferred_element_type=f32)


def qkv_kernel(local_heads, head_dim, x_ref, w_ref, q_ref, kv_ref, x_hi, x_lo):
    @pl.when(pl.program_id(0) == 0)
    def _():
        hi, lo = split_hi_lo(x_ref[...])
        x_hi[...] = hi
        x_lo[...] = lo

    w_hi, w_lo = split_hi_lo(w_ref[...])
    acc = mxu(x_hi[...], w_lo) + mxu(x_lo[...], w_hi)
    acc = acc + mxu(x_hi[...], w_hi)
    pair = 2 * head_dim
    frames, _, strip, _ = q_ref.shape
    rows = frames * strip
    first = lax.broadcasted_iota(jnp.int32, (rows, pair), 1) < head_dim
    parts = [acc[:, n * pair : (n + 1) * pair] for n in range(3)]
    turned = [pltpu.roll(part, head_dim, 1) for part in parts]

    def coded(value):
        rest = value - value.astype(bf16).astype(f32)
        return jnp.where(first, value, rest).astype(bf16).reshape(frames, strip, pair)

    factor = head_dim ** (-0.5)
    queries = [
        coded(jnp.where(first, parts[0], turned[0]) * factor),
        coded(jnp.where(first, turned[1], parts[1]) * factor),
    ]
    keys = [
        coded(jnp.where(first, turned[0], parts[0])),
        coded(jnp.where(first, parts[2], turned[2])),
    ]
    if local_heads == 2:
        for h in range(2):
            q_ref[:, 0, :, h * pair : (h + 1) * pair] = queries[h]
            kv_ref[:, 0, :, h * pair : (h + 1) * pair] = keys[h]
        values = jnp.where(first, parts[1], parts[2]).astype(bf16)
        kv_ref[:, 0, :, 2 * pair :] = values.reshape(frames, strip, pair)
    else:
        for h, values in enumerate((parts[1], turned[2])):
            q_ref[:, h] = queries[h]
            kv_ref[:, h, :, :pair] = keys[h]
            values = values[:, :head_dim].astype(bf16)
            kv_ref[:, h, :, pair:] = values.reshape(frames, strip, head_dim)


def project(tokens, weight, head_groups, head_dim):
    frames, strip, width = tokens.shape
    local_heads = HEADS // head_groups
    share = 2 // local_heads
    columns = 6 * head_dim
    q_width, kv_width = local_heads * 2 * head_dim, local_heads * 3 * head_dim
    return pl.pallas_call(
        functools.partial(qkv_kernel, local_heads, head_dim),
        grid=(HEADS // 2,),
        in_specs=[
            pl.BlockSpec((frames * strip, width), lambda i: (0, 0)),
            pl.BlockSpec((width, columns), lambda i: (0, i)),
        ],
        out_specs=[
            pl.BlockSpec((frames, share, strip, q_width), lambda i: (0, i, 0, 0)),
            pl.BlockSpec((frames, share, strip, kv_width), lambda i: (0, i, 0, 0)),
        ],
        out_shape=[
            jax.ShapeDtypeStruct((frames, head_groups, strip, q_width), bf16),
            jax.ShapeDtypeStruct((frames, head_groups, strip, kv_width), bf16),
        ],
        scratch_shapes=[pltpu.VMEM((frames * strip, width), bf16)] * 2,
        compiler_params=pltpu.CompilerParams(vmem_limit_bytes=48 << 20),
        name="qkv",
    )(tokens.reshape(-1, width), weight)


MESH = pl.DeviceIdType.MESH


def near_first(count):
    return sorted(range(1, count), key=lambda j: (min(j, count - j), j))


def greet(peers):
    barrier = pltpu.get_barrier_semaphore()
    for peer in peers:
        pl.semaphore_signal(barrier, inc=1, device_id=peer, device_id_type=MESH)
    pl.semaphore_wait(barrier, len(peers))


def exchange_kernel(
    groups, teams, q_ref, kv_ref, q_out, pairs, own_sem,
    q_send, q_recv, z_send, z_recv, f_send, f_recv, r_send, r_recv,
):
    frames = q_ref.shape[0]
    team, me = lax.axis_index("frame"), lax.axis_index("head")
    square = teams == 4
    if square:
        side = lax.rem(team, 2)
        beside, across = team + 1 - 2 * side, lax.rem(team + 2, 4)
        direct = [(beside, beside), (across, across)]
    else:
        direct = [
            (lax.rem(team + k, teams), lax.rem(team + teams - k, teams)) for k in range(1, teams)
        ]
    order = near_first(groups)
    peers = [(team, lax.rem(me + j, groups)) for j in order] + [(to, me) for to, _ in direct]
    greet(peers)

    def remote(src, dst, send, recv, target):
        return pltpu.make_async_remote_copy(
            src_ref=src, dst_ref=dst, send_sem=send, recv_sem=recv,
            device_id=target, device_id_type=MESH,
        )

    def z_copy(f, j):
        to = lax.rem(me + j, groups)
        return remote(
            kv_ref.at[f, to], pairs.at[team * frames + f, me],
            z_send.at[f, j], z_recv.at[f, j], (team, to),
        )

    def q_copy(f, j):
        to = lax.rem(me + j, groups)
        return remote(
            q_ref.at[f, to], q_out.at[f, me], q_send.at[f, j], q_recv.at[f, j], (team, to)
        )

    def piece(owner, f, j):
        return pairs.at[owner * frames + f, lax.rem(me + groups - j, groups)]

    def f_copy(k, f, j):
        src = kv_ref.at[f, me] if j == 0 else piece(team, f, j)
        return remote(
            src, piece(team, f, j), f_send.at[k, f, j], f_recv.at[k, f, j], (direct[k][0], me)
        )

    def r_copy(f, j):
        origin, to = (beside, across) if f % 2 == 0 else (across, beside)
        here = piece(origin, f, j)
        return remote(here, here, r_send.at[f, j], r_recv.at[f, j], (to, me))

    own = []
    for f in range(frames):
        own.append(
            pltpu.make_async_copy(kv_ref.at[f, me], pairs.at[team * frames + f, me], own_sem.at[0, f])
        )
        own.append(pltpu.make_async_copy(q_ref.at[f, me], q_out.at[f, me], own_sem.at[1, f]))
    schedule = [(f, j) for j in [0] + order for f in range(frames)]
    for f, j in schedule:
        if j:
            z_copy(f, j).start()
    for f, j in schedule:
        if j:
            q_copy(f, j).start()
    for copy in own:
        copy.start()
    lag = 2 * frames
    for n in range(len(schedule) + lag):
        if n < len(schedule):
            f, j = schedule[n]
            if j:
                z_copy(f, j).wait_recv()
            for k in range(len(direct)):
                f_copy(k, f, j).start()
        if n >= lag and square:
            f, j = schedule[n - lag]
            f_copy(f % 2, f, j).wait_recv()
            r_copy(f, j).start()
    for f, j in schedule:
        for k in range(len(direct)):
            f_copy(k, f, j).wait_send()
            if not (square and k == f % 2):
                f_copy(k, f, j).wait_recv()
        if square:
            r_copy(f, j).wait()
        if j:
            z_copy(f, j).wait_send()
            q_copy(f, j).wait()
    for copy in own:
        copy.wait()


def exchange(queries, own_pairs, groups, teams):
    frames = queries.shape[0]
    sems = lambda *shape: pltpu.SemaphoreType.DMA(shape)
    hops = 2 if teams == 4 else teams - 1
    vmem = pl.BlockSpec(memory_space=pltpu.VMEM)
    anywhere = pl.BlockSpec(memory_space=pl.ANY)
    return pl.pallas_call(
        functools.partial(exchange_kernel, groups, teams),
        in_specs=[vmem, vmem],
        out_specs=[anywhere, anywhere],
        out_shape=[
            jax.ShapeDtypeStruct(queries.shape, bf16),
            jax.ShapeDtypeStruct((teams * frames,) + own_pairs.shape[1:], bf16),
        ],
        scratch_shapes=[sems(2, frames)]
        + [sems(frames, groups)] * 4
        + [sems(hops, frames, groups)] * 2
        + [sems(frames, groups)] * 2,
        compiler_params=pltpu.CompilerParams(collective_id=0, has_side_effects=True),
        name="exchange",
    )(queries, own_pairs)


def hand_back_kernel(groups, src, dst, own_sem, send, recv):
    team, me = lax.axis_index("frame"), lax.axis_index("head")
    order = near_first(groups)
    greet([(team, lax.rem(me + j, groups)) for j in order])
    copies = []
    for j in reversed(order):
        to = lax.rem(me + j, groups)
        copies.append(
            pltpu.make_async_remote_copy(
                src_ref=src.at[:, to], dst_ref=dst.at[me],
                send_sem=send.at[j], recv_sem=recv.at[j],
                device_id=(team, to), device_id_type=MESH,
            )
        )
    copies.append(pltpu.make_async_copy(src.at[:, me], dst.at[me], own_sem))
    for copy in copies:
        copy.start()
    for copy in copies:
        copy.wait()


def hand_back(attended):
    frames, groups, strip, width = attended.shape
    vmem = pl.BlockSpec(memory_space=pltpu.VMEM)
    return pl.pallas_call(
        functools.partial(hand_back_kernel, groups),
        in_specs=[vmem],
        out_specs=vmem,
        out_shape=jax.ShapeDtypeStruct((groups, frames, strip, width), bf16),
        scratch_shapes=[pltpu.SemaphoreType.DMA] + [pltpu.SemaphoreType.DMA((groups,))] * 2,
        compiler_params=pltpu.CompilerParams(collective_id=1, has_side_effects=True),
        name="hand_back",
    )(attended)


def attend_kernel(local_heads, head_dim, span, lists, counts, q_ref, kv_ref, o_ref):
    b = pl.program_id(0)
    count = counts[b]
    pair = 2 * head_dim
    v_at = local_heads * pair
    v_width = local_heads * head_dim
    first = lax.broadcasted_iota(jnp.int32, (BLOCK, pair), 1) < head_dim
    stacked = []
    for h in range(local_heads):
        coded = q_ref[:, h * pair : (h + 1) * pair].astype(f32)
        turned = pltpu.roll(coded, head_dim, 1)
        high, low = jnp.where(first, coded, turned), jnp.where(first, turned, coded)
        stacked.append(jnp.concatenate([high, low], axis=0).astype(bf16))

    def chunk(c, carry):
        offsets = []
        valid = []
        for t in range(span):
            slot = c * span + t
            block = lists[b, jnp.minimum(slot, count - 1)]
            offsets.append(pl.multiple_of(block * BLOCK, BLOCK))
            valid.append(slot < count)
        values = jnp.concatenate(
            [kv_ref[pl.ds(at, BLOCK), v_at : v_at + v_width] for at in offsets], axis=0
        )
        out = []
        for h in range(local_heads):
            top, total, blend = carry[h]
            scores = []
            for at, ok in zip(offsets, valid):
                keys = kv_ref[pl.ds(at, BLOCK), h * pair : (h + 1) * pair]
                both = lax.dot_general(
                    stacked[h], keys, (((1,), (1,)), ((), ())), preferred_element_type=f32
                )
                scores.append(jnp.where(ok, both[:BLOCK] + both[BLOCK:], -jnp.inf))
            peak = functools.reduce(jnp.maximum, scores)
            new_top = jnp.maximum(top, jnp.max(peak, axis=1, keepdims=True))
            scale = jnp.exp(top - new_top)
            weights = [jnp.exp(s - new_top) for s in scores]
            total = total * scale + functools.reduce(jnp.add, weights)
            packed = jnp.concatenate([w.astype(bf16) for w in weights], axis=1)
            blend = blend * scale + mxu(packed, values)
            out.append((new_top, total, blend))
        return tuple(out)

    start = tuple(
        (
            jnp.full((BLOCK, 1), -jnp.inf, f32),
            jnp.zeros((BLOCK, BLOCK), f32),
            jnp.zeros((BLOCK, v_width), f32),
        )
        for _ in range(local_heads)
    )
    final = lax.fori_loop(0, (count + span - 1) // span, chunk, start)
    owner = lax.broadcasted_iota(jnp.int32, (BLOCK, v_width), 1) // head_dim
    result = jnp.zeros((BLOCK, v_width), f32)
    for h in range(local_heads):
        _, total, blend = final[h]
        ready = blend / jnp.sum(total, axis=1, keepdims=True)
        result = jnp.where(owner == h, ready, result)
    o_ref[...] = result.astype(bf16)


def attend(queries, pairs, lists, counts, local_heads, head_dim):
    blocks, slots = lists.shape
    span = -(-slots // (-(-slots // 7)))
    width = local_heads * head_dim
    return pl.pallas_call(
        functools.partial(attend_kernel, local_heads, head_dim, span),
        grid_spec=pltpu.PrefetchScalarGridSpec(
            num_scalar_prefetch=2,
            grid=(blocks,),
            in_specs=[
                pl.BlockSpec((BLOCK, queries.shape[1]), lambda i, *_: (i, 0)),
                pl.BlockSpec(pairs.shape, lambda i, *_: (0, 0), pipeline_mode=pl.Buffered(1)),
            ],
            out_specs=pl.BlockSpec((BLOCK, width), lambda i, *_: (i, 0)),
        ),
        out_shape=jax.ShapeDtypeStruct((blocks * BLOCK, width), bf16),
        compiler_params=pltpu.CompilerParams(vmem_limit_bytes=48 << 20),
        name="attend",
    )(lists, counts, queries, pairs)


def scatter_order(teams, halves, k):
    far = halves - 1 - lax.rem(k, halves)
    turn = lax.rem(k // halves + 1 + 2 * far, teams)
    return turn, far


def front_kernel(
    teams, groups, slots, x_hbm, w_hbm, lists_hbm, counts_hbm, out_hbm, gain_hbm, proj_hbm, ext_ref,
    w_buf, x_hi, x_lo, msg, msg_scale, got, got_scale, q_ref, kv_ref, stream, out_buf,
    ready, gain_ref, proj_ref, sent, back, lists_all, counts_all, lists, counts,
    w_sem, l_sem, i_sem, m_send, m_recv, s_send, s_recv, f_send, f_recv, a_send, a_recv,
    i_send, i_recv, h_send, h_recv,
):
    planes = groups // 2
    halves = planes // 2
    pairs = teams * halves
    chips = teams * planes
    lanes = msg.shape[-1]
    head_dim = lanes // 2
    columns = 3 * lanes
    rows = stream.shape[0]
    channels = proj_ref.shape[-1]
    team, group = lax.axis_index("frame"), lax.axis_index("head")
    plane, core = group // 2, lax.rem(group, 2)
    half, parity = plane // 2, lax.rem(plane, 2)
    me = team * planes + plane
    sibling = (team, group + 1 - 2 * core)
    above = (team, lax.rem(group + groups - 1, groups))
    below = (team, lax.rem(group + 1, groups))

    def place(k):
        turn, far = scatter_order(teams, halves, k)
        return lax.rem(team + turn, teams), lax.rem(half + far, halves)

    def weight(k):
        to_team, to_half = place(k)
        at = pl.multiple_of((to_team * halves + to_half) * columns, columns)
        return pltpu.make_async_copy(w_hbm.at[:, pl.ds(at, columns)], w_buf.at[k], w_sem.at[k])

    load_x = pltpu.make_async_copy(x_hbm, stream, l_sem.at[0])
    load_out = [
        pltpu.make_async_copy(out_hbm, out_buf, l_sem.at[1]),
        pltpu.make_async_copy(gain_hbm, gain_ref, l_sem.at[4]),
        pltpu.make_async_copy(proj_hbm, proj_ref, l_sem.at[5]),
    ]
    load_lists = [
        pltpu.make_async_copy(lists_hbm, lists_all.at[team], l_sem.at[2]),
        pltpu.make_async_copy(counts_hbm, counts_all.at[team], l_sem.at[3]),
    ]
    load_x.start()
    for k in range(2):
        weight(k).start()
    for copy in load_lists:
        copy.start()

    barrier = pltpu.get_barrier_semaphore()
    for n in range(1, chips):
        peer = (lax.rem(team + n // planes, teams), lax.rem(plane + n % planes, planes) * 2 + core)
        pl.semaphore_signal(barrier, inc=1, device_id=peer, device_id_type=MESH)
    for peer in (above, below):
        pl.semaphore_signal(barrier, inc=1, device_id=peer, device_id_type=MESH)

    first = lax.broadcasted_iota(jnp.int32, (rows, lanes), 1) < head_dim
    lane = lax.broadcasted_iota(jnp.int32, (BLOCK, lanes), 1)
    near = lane < head_dim
    top = 32766.0

    def message(to_team, to_plane):
        to = to_team * planes + to_plane
        target = (to_team, to_plane * 2 + core)
        return [
            pltpu.make_async_remote_copy(
                src_ref=msg.at[to], dst_ref=got.at[me],
                send_sem=m_send.at[to], recv_sem=m_recv.at[me],
                device_id=target, device_id_type=MESH,
            ),
            pltpu.make_async_remote_copy(
                src_ref=msg_scale.at[to], dst_ref=got_scale.at[me],
                send_sem=s_send.at[to], recv_sem=s_recv.at[me],
                device_id=target, device_id_type=MESH,
            ),
        ]

    def peak(value):
        return jnp.maximum(jnp.max(jnp.abs(value), axis=1, keepdims=True), 1e-30)

    def encode(k):
        weight(k).wait()

        @pl.when(k + 2 < pairs)
        def _():
            weight(k + 2).start()

        w_hi, w_lo = split_hi_lo(w_buf[k])
        acc = mxu(x_hi[...], w_lo) + mxu(x_lo[...], w_hi)
        acc = acc + mxu(x_hi[...], w_hi)
        p0, p1, p2 = [acc[:, n * lanes : (n + 1) * lanes] for n in range(3)]
        t0, t1 = pltpu.roll(p0, head_dim, 1), pltpu.roll(p1, head_dim, 1)
        key_value = [jnp.where(first, t0, t1), p2]
        up, down = slice(0, BLOCK), slice(BLOCK, 2 * BLOCK)
        query = [jnp.where(near, p0[up], t0[down]), jnp.where(near, t1[up], p1[down])]
        to_team, to_half = place(k)
        for i in range(2):
            to = to_team * planes + to_half * 2 + i
            kv, q = key_value[i], query[i]
            peak_k = peak(jnp.where(first, kv, 0.0))
            peak_v = peak(jnp.where(first, 0.0, kv))
            peak_q0 = peak(jnp.where(near, q, 0.0))
            peak_q1 = peak(jnp.where(near, 0.0, q))
            kv = kv * jnp.where(first, top / peak_k, top / peak_v)
            q = q * jnp.where(near, top / peak_q0, top / peak_q1)
            msg[to, 0:2] = jnp.round(kv).astype(jnp.int32).astype(jnp.int16).reshape(2, BLOCK, lanes)
            msg[to, 2] = jnp.round(q).astype(jnp.int32).astype(jnp.int16)
            columns_of = [peak_k[up], peak_k[down], peak_v[up], peak_v[down], peak_q0, peak_q1]
            table = jnp.zeros((BLOCK, lanes), f32)
            for n, column in enumerate(columns_of):
                table = jnp.where(lane == n, column * (1.0 / top), table)
            msg_scale[to] = jnp.transpose(table)[:8]

    def post(k):
        to_team, to_half = place(k)
        for i in range(2):
            to_plane = to_half * 2 + i
            to = to_team * planes + to_plane

            @pl.when(to != me)
            def _():
                for copy in message(to_team, to_plane):
                    copy.start()

            @pl.when(to == me)
            def _():
                got[to] = msg[to]
                got_scale[to] = msg_scale[to]

    load_x.wait()
    hi, lo = split_hi_lo(stream[...])
    x_hi[...] = hi
    x_lo[...] = lo
    encode(0)
    for copy in load_lists:
        copy.wait()
    pl.semaphore_wait(barrier, chips + 1)
    post(0)

    def list_copies(step):
        return [
            pltpu.make_async_remote_copy(
                src_ref=whole.at[team], dst_ref=whole.at[team],
                send_sem=i_send.at[n, step], recv_sem=i_recv.at[n, step],
                device_id=(lax.rem(team + step, teams), group), device_id_type=MESH,
            )
            for n, whole in enumerate((lists_all, counts_all))
        ]

    def list_arrivals(step):
        origin = lax.rem(team + teams - step, teams)
        return [
            pltpu.make_async_remote_copy(
                src_ref=whole.at[origin], dst_ref=whole.at[origin],
                send_sem=i_send.at[n, step], recv_sem=i_recv.at[n, step],
                device_id=sibling, device_id_type=MESH,
            )
            for n, whole in enumerate((lists_all, counts_all))
        ]

    for step in range(1, teams):
        for copy in list_copies(step):
            copy.start()

    def send_step(k, carry):
        encode(k)
        post(k)
        return carry

    lax.fori_loop(1, pairs, send_step, 0)
    for copy in load_out:
        copy.start()

    for step in range(1, teams):
        for copy in list_arrivals(step):
            copy.wait_recv()
    to_smem = [
        pltpu.make_async_copy(lists_all, lists, i_sem.at[0]),
        pltpu.make_async_copy(counts_all, counts, i_sem.at[1]),
    ]
    for copy in to_smem:
        copy.start()

    factor = head_dim ** (-0.5) * 1.4426950408889634

    def source(n):
        far = n // (2 * teams)
        turn = lax.rem(lax.rem(n, 2 * teams) // 2 + 1 + 2 * far, teams)
        from_team = lax.rem(team + teams - turn, teams)
        from_plane = lax.rem(half + halves - far, halves) * 2 + lax.rem(parity + 1 + n, 2)
        return from_team, from_plane

    def arrival(src):
        return [
            pltpu.make_async_remote_copy(
                src_ref=msg.at[src], dst_ref=got.at[src],
                send_sem=m_send.at[src], recv_sem=m_recv.at[src],
                device_id=sibling, device_id_type=MESH,
            ),
            pltpu.make_async_remote_copy(
                src_ref=msg_scale.at[src], dst_ref=got_scale.at[src],
                send_sem=s_send.at[src], recv_sem=s_recv.at[src],
                device_id=sibling, device_id_type=MESH,
            ),
        ]

    def forward(from_team, from_plane, f, whose):
        src = from_team * planes + from_plane
        block = kv_ref.at[(from_team * 2 + f) * groups + from_plane * 2 + whose]
        return pltpu.make_async_remote_copy(
            src_ref=block, dst_ref=block,
            send_sem=f_send.at[f, src], recv_sem=f_recv.at[f, src],
            device_id=sibling, device_id_type=MESH,
        )

    def take_step(n, carry):
        from_team, from_plane = source(n)
        src = from_team * planes + from_plane

        @pl.when(src != me)
        def _():
            for copy in arrival(src):
                copy.wait_recv()

        scale = jnp.transpose(jnp.concatenate([got_scale[src]] * (BLOCK // 8), axis=0))
        for f in range(2):
            at = (from_team * 2 + f) * groups + from_plane * 2 + core
            kv = got[src, f].astype(jnp.int32).astype(f32)
            kv = kv * jnp.where(near, scale[:, f : f + 1], scale[:, 2 + f : 3 + f])
            high = kv.astype(bf16).astype(f32)
            low = pltpu.roll(kv - high, head_dim, 1)
            kv_ref[at, :, :lanes] = jnp.where(near, high, low).astype(bf16)
            value = jnp.where(near, pltpu.roll(kv, head_dim, 1), 1.0)
            kv_ref[at, :, lanes:] = value.astype(bf16)
            forward(from_team, from_plane, f, core).start()
        q = got[src, 2].astype(jnp.int32).astype(f32)
        q = q * (factor * jnp.where(near, scale[:, 4:5], scale[:, 5:6]))
        high = q.astype(bf16).astype(f32)
        low = q - high
        high_turned, low_turned = pltpu.roll(high, head_dim, 1), pltpu.roll(low, head_dim, 1)
        q_ref[src, 0, :, :lanes] = jnp.where(near, high, high_turned).astype(bf16)
        q_ref[src, 0, :, lanes:] = jnp.where(near, low, low_turned).astype(bf16)
        q_ref[src, 1, :, :lanes] = jnp.where(near, high_turned, high).astype(bf16)
        q_ref[src, 1, :, lanes:] = jnp.where(near, low_turned, low).astype(bf16)
        return carry

    lax.fori_loop(0, chips, take_step, 0)

    def end_step(n, carry):
        from_team, from_plane = source(n)
        src = from_team * planes + from_plane
        for f in range(2):
            forward(from_team, from_plane, f, 1 - core).wait_recv()
        return carry

    for copy in to_smem:
        copy.wait()
    lax.fori_loop(0, chips, end_step, 0)

    def copy_to(to_team, to_plane):
        to = to_team * planes + to_plane
        return pltpu.make_async_remote_copy(
            src_ref=sent.at[to], dst_ref=back.at[me],
            send_sem=a_send.at[to], recv_sem=a_recv.at[me],
            device_id=(to_team, to_plane * 2 + core), device_id_type=MESH,
        )

    def returned(src):
        return pltpu.make_async_remote_copy(
            src_ref=sent.at[src], dst_ref=back.at[src],
            send_sem=a_send.at[src], recv_sem=a_recv.at[src],
            device_id=sibling, device_id_type=MESH,
        )

    def attend_pair(to_team, to_half):
        items = [(to_half * 2 + i, f) for i in range(2) for f in range(2)]
        scores, values = [], []
        for to_plane, f in items:
            row = f * groups + to_plane * 2 + core
            count = counts[to_team, row]
            query = q_ref[to_team * planes + to_plane, f]
            for slot in range(slots):
                block = lists[to_team, row, slot]
                keys = kv_ref[block, :, :lanes]
                score = lax.dot_general(
                    query, jnp.concatenate([keys, keys], axis=1), (((1,), (1,)), ((), ())),
                    preferred_element_type=f32,
                )
                scores.append(score if slot == 0 else jnp.where(slot < count, score, -jnp.inf))
                values.append(kv_ref[block, :, lanes:])
        for n in range(len(items)):
            own = slice(n * slots, (n + 1) * slots)
            top_score = jnp.max(functools.reduce(jnp.maximum, scores[own]), axis=1, keepdims=True)
            packed = jnp.concatenate(
                [jnp.exp2(s - top_score).astype(bf16) for s in scores[own]], axis=1
            )
            total = mxu(packed, jnp.concatenate(values[own], axis=0))
            ready[n] = total / total[:, head_dim : head_dim + 1]
        for i in range(2):
            to_plane = to_half * 2 + i
            to = to_team * planes + to_plane
            both = jnp.where(near, ready[2 * i], pltpu.roll(ready[2 * i + 1], head_dim, 1))
            sent[to] = both.astype(bf16)

            @pl.when(to != me)
            def _():
                copy_to(to_team, to_plane).start()

            @pl.when(to == me)
            def _():
                back[to] = both.astype(bf16)

    def attend_team(k):
        to_team = lax.rem(team + k, teams)

        def part(n, carry):
            attend_pair(to_team, lax.rem(half + halves - 1 - n, halves))
            return carry

        lax.fori_loop(0, halves, part, 0)

    def absorb(k):
        from_team = lax.rem(team + teams - k, teams)
        deep = planes * head_dim
        pieces = []
        for i in range(0, planes, 2):
            at = from_team * planes + i
            for j in range(2):
                @pl.when(at + j != me)
                def _():
                    returned(at + j).wait_recv()

            one, two = back[at].astype(f32), back[at + 1].astype(f32)
            upper = jnp.where(near, one, pltpu.roll(two, head_dim, 1))
            lower = jnp.where(near, pltpu.roll(one, head_dim, 1), two)
            pieces.append(jnp.concatenate([upper, lower], axis=0).astype(bf16))
        attended = jnp.concatenate(pieces, axis=1)
        w_hi, w_lo = split_hi_lo(out_buf[pl.ds(pl.multiple_of(from_team * deep, deep), deep), :])
        stream[...] += mxu(attended, w_hi) + mxu(attended, w_lo)

    for copy in load_out:
        copy.wait()
    attend_team(1)

    def team_step(k, carry):
        attend_team(k)
        absorb(k - 1)
        return carry

    lax.fori_loop(2, teams + 1, team_step, 0)
    absorb(teams)

    p_hi, p_lo = split_hi_lo(proj_ref[...])

    def finish(spans):
        summed = jnp.concatenate([stream[f * BLOCK + at : f * BLOCK + end] for f, at, end in spans])
        centre = jnp.mean(summed, axis=-1, keepdims=True)
        centred = summed - centre
        spread = jnp.mean(centred * centred, axis=-1, keepdims=True)
        normed = centred * lax.rsqrt(spread + eps_norm) * gain_ref[...]
        n_hi, n_lo = split_hi_lo(normed)
        features = mxu(n_hi, p_lo) + mxu(n_lo, p_hi)
        features = (features + mxu(n_hi, p_hi)).astype(bf16)
        row = 0
        for f, at, end in spans:
            ext_ref[f, GRID + at : GRID + end, :] = features[row : row + end - at]
            row += end - at

    def halo(side, f):
        at = (GRID, BLOCK)[side]
        to = (GRID + BLOCK, 0)[side]
        return pltpu.make_async_remote_copy(
            src_ref=ext_ref.at[f, pl.ds(at, GRID)], dst_ref=ext_ref.at[f, pl.ds(to, GRID)],
            send_sem=h_send.at[side, f], recv_sem=h_recv.at[side, f],
            device_id=(above, below)[side], device_id_type=MESH,
        )

    edges = ((0, GRID), (BLOCK - GRID, BLOCK))
    finish([(f, at, end) for f in range(2) for at, end in edges])
    for side in range(2):
        for f in range(2):
            halo(side, f).start()
    finish([(f, GRID, BLOCK - GRID) for f in range(2)])

    def drain_step(n, carry):
        from_team, from_plane = source(n)
        src = from_team * planes + from_plane
        for f in range(2):
            forward(from_team, from_plane, f, core).wait_send()

        @pl.when(src != me)
        def _():
            for copy in arrival(src):
                copy.wait_send()
            returned(src).wait_send()

        return carry

    lax.fori_loop(0, chips, drain_step, 0)
    for step in range(1, teams):
        for copy in list_copies(step):
            copy.wait_send()
    for side in range(2):
        for f in range(2):
            halo(side, f).wait()

    blank = jnp.zeros((2, GRID, channels), bf16)

    @pl.when(group == 0)
    def _():
        ext_ref[:, 0:GRID, :] = blank

    @pl.when(group == groups - 1)
    def _():
        ext_ref[:, GRID + BLOCK :, :] = blank


def front(tokens, weight, lists, counts, out_weight, gain, proj, teams, groups):
    frames, strip, width = tokens.shape
    head_dim = width // HEADS
    lanes = 2 * head_dim
    rows = frames * strip
    chips, pairs = HEADS, HEADS // 2
    blocks, slots = lists.shape
    channels = proj.shape[1]
    dma = lambda *shape: pltpu.SemaphoreType.DMA(shape)
    vmem = pl.BlockSpec(memory_space=pltpu.VMEM)
    hbm = pl.BlockSpec(memory_space=pltpu.HBM)
    listed, counted = (teams, blocks, slots), (teams, blocks)
    return pl.pallas_call(
        functools.partial(front_kernel, teams, groups, slots),
        in_specs=[hbm] * 7,
        out_specs=vmem,
        out_shape=jax.ShapeDtypeStruct((frames, strip + 2 * GRID, channels), bf16),
        scratch_shapes=[
            pltpu.VMEM((pairs, width, 6 * head_dim), f32),
            pltpu.VMEM((rows, width), bf16),
            pltpu.VMEM((rows, width), bf16),
            pltpu.VMEM((chips, 3, BLOCK, lanes), jnp.int16),
            pltpu.VMEM((chips, 8, BLOCK), f32),
            pltpu.VMEM((chips, 3, BLOCK, lanes), jnp.int16),
            pltpu.VMEM((chips, 8, BLOCK), f32),
            pltpu.VMEM((chips, frames, BLOCK, 2 * lanes), bf16),
            pltpu.VMEM((teams * frames * groups, BLOCK, 2 * lanes), bf16),
            pltpu.VMEM((rows, width), f32),
            pltpu.VMEM((width, width), f32),
            pltpu.VMEM((4, BLOCK, lanes), f32),
            pltpu.VMEM((1, width), f32),
            pltpu.VMEM((width, channels), f32),
            pltpu.VMEM((chips, BLOCK, lanes), bf16),
            pltpu.VMEM((chips, BLOCK, lanes), bf16),
            pltpu.VMEM(listed, jnp.int32),
            pltpu.VMEM(counted, jnp.int32),
            pltpu.SMEM(listed, jnp.int32),
            pltpu.SMEM(counted, jnp.int32),
            dma(pairs), dma(6), dma(2),
        ]
        + [dma(chips)] * 4
        + [dma(frames, chips)] * 2
        + [dma(chips)] * 2
        + [dma(2, teams)] * 2
        + [dma(2, 2)] * 2,
        compiler_params=pltpu.CompilerParams(
            collective_id=0, has_side_effects=True, vmem_limit_bytes=56 << 20
        ),
        name="front",
    )(tokens.reshape(rows, width), weight, lists, counts, out_weight, gain.reshape(1, width), proj)


def head_kernel(
    token_rows, feat_ref, up_ref, conv_ref, bias_ref, out_ref, up_map, act_map, hid_map, flat
):
    channels = feat_ref.shape[-1]
    ext = token_rows + 2
    pixel_cols = 4 * GRID
    def moved(block, step):
        rows = block.shape[0]
        column = lax.broadcasted_iota(jnp.int32, block.shape, 0) % GRID
        turned = pltpu.roll(block, step % rows, 0)
        return jnp.where(column == (0 if step > 0 else GRID - 1), 0.0, turned)

    feat = feat_ref[pl.program_id(0)]
    for a in range(4):
        for e in range(4):
            at = (4 * a + e) * channels
            lifted = mxu(feat, up_ref[:, at : at + channels])
            plain = lifted.astype(bf16)
            active = jnp.maximum(plain, jnp.zeros((), bf16))
            rim = None
            if e == 0:
                rim, rim_at = jnp.maximum(moved(lifted, -1), 0.0).astype(bf16), 5 * GRID
            if e == 3:
                rim, rim_at = jnp.maximum(moved(lifted, 1), 0.0).astype(bf16), 0
            for r in range(ext):
                own = slice(r * GRID, (r + 1) * GRID)
                up_map[4 * r + a, e * GRID : (e + 1) * GRID, :] = plain[own]
                act_map[4 * r + a, (e + 1) * GRID : (e + 2) * GRID, :] = active[own]
                if rim is not None:
                    act_map[4 * r + a, rim_at : rim_at + GRID, :] = rim[own]

    def conv_rows(source, start, rows, which):
        taps = [
            source[start + dy : start + dy + rows, dx * GRID : dx * GRID + pixel_cols, :].reshape(
                rows * pixel_cols, channels
            )
            for dy in range(3)
            for dx in range(3)
        ]
        weight = conv_ref[which].reshape(9 * channels, channels)
        return mxu(jnp.concatenate(taps, axis=1), weight) + bias_ref[which][None, :]

    hidden_rows = 4 * token_rows + 2
    group = divisor_upto(hidden_rows, 3)
    top = lax.axis_index("head") == 0
    bottom = lax.axis_index("head") == lax.axis_size("head") - 1
    for g in range(hidden_rows // group):
        value = jnp.maximum(conv_rows(act_map, g * group + 2, group, 0), 0.0)
        for r in range(group):
            y = g * group + r
            row = value[r * pixel_cols : (r + 1) * pixel_cols]
            hid_map[y, GRID : GRID + pixel_cols, :] = row.astype(bf16)
            hid_map[y, 0:GRID, :] = moved(row[3 * GRID :], 1).astype(bf16)
            hid_map[y, 5 * GRID :, :] = moved(row[:GRID], -1).astype(bf16)

    @pl.when(top)
    def _():
        hid_map[0] = jnp.zeros(hid_map.shape[1:], bf16)

    @pl.when(bottom)
    def _():
        hid_map[hidden_rows - 1] = jnp.zeros(hid_map.shape[1:], bf16)

    out_rows = 4 * token_rows
    group2 = divisor_upto(out_rows, 4)
    lanes = 128
    for g in range(out_rows // group2):
        value = conv_rows(hid_map, g * group2, group2, 1)
        for r in range(group2):
            y = g * group2 + r
            row = value[r * pixel_cols : (r + 1) * pixel_cols] + up_map[y + 4].astype(f32)
            for n in range(channels // lanes):
                at = slice(n * lanes, (n + 1) * lanes)
                for e in range(4):
                    piece = row[e * GRID : (e + 1) * GRID, at]
                    flat[y % 4, n, pl.ds(e, GRID, stride=4), :] = piece
                out_ref[0, y, :, at] = flat[y % 4, n].astype(bf16)


def predict(features, up_weight, conv_weight, conv_bias, token_rows):
    frames, _, channels = features.shape
    pixel_rows, pixel_cols = 4 * token_rows, 4 * GRID
    once = pl.Buffered(1)
    vmem = pl.BlockSpec(memory_space=pltpu.VMEM)
    return pl.pallas_call(
        functools.partial(head_kernel, token_rows),
        grid=(frames,),
        in_specs=[
            vmem,
            vmem,
            vmem,
            pl.BlockSpec(conv_bias.shape, lambda i: (0, 0), pipeline_mode=once),
        ],
        out_specs=pl.BlockSpec((1, pixel_rows, pixel_cols, channels), lambda i: (i, 0, 0, 0)),
        scratch_shapes=[
            pltpu.VMEM((pixel_rows + 8, pixel_cols, channels), bf16),
            pltpu.VMEM((pixel_rows + 8, pixel_cols + 2 * GRID, channels), bf16),
            pltpu.VMEM((pixel_rows + 2, pixel_cols + 2 * GRID, channels), bf16),
            pltpu.VMEM((4, channels // 128, pixel_cols, 128), f32),
        ],
        out_shape=jax.ShapeDtypeStruct((frames, pixel_rows, pixel_cols, channels), bf16),
        compiler_params=pltpu.CompilerParams(vmem_limit_bytes=20 << 20),
        name="head",
    )(features, up_weight, conv_weight, conv_bias)


def layer_norm(rows, gain):
    centre = jnp.mean(rows, axis=-1, keepdims=True)
    centred = rows - centre
    spread = jnp.mean(centred * centred, axis=-1, keepdims=True)
    return centred * lax.rsqrt(spread + eps_norm) * gain


def by_teams(
    tokens, qkv_weight, out_weight, norm_gain, proj_weight, block_lists, block_counts
):
    local_frames, strip_tokens, model_width = tokens.shape
    head_groups = lax.axis_size("head")
    local_heads = HEADS // head_groups
    head_dim = model_width // HEADS
    own_queries, own_pairs = project(tokens, qkv_weight, head_groups, head_dim)
    queries, all_pairs = exchange(own_queries, own_pairs, head_groups, lax.axis_size("frame"))
    queries = queries.reshape(-1, queries.shape[-1])
    all_pairs = all_pairs.reshape(-1, all_pairs.shape[-1])
    attended = attend(queries, all_pairs, block_lists, block_counts, local_heads, head_dim)
    attended = attended.reshape(local_frames, head_groups, strip_tokens, local_heads * head_dim)
    attended = hand_back(attended).reshape(head_groups, -1, local_heads * head_dim)
    attended = jnp.transpose(attended, (1, 0, 2)).reshape(-1, model_width)
    stream = tokens.reshape(-1, model_width) + jnp.dot(
        attended.astype(f32), out_weight, precision=highest, preferred_element_type=f32
    )
    normed = layer_norm(stream, norm_gain)
    features = jnp.dot(
        normed, proj_weight, precision=highest, preferred_element_type=f32
    ).astype(bf16)
    channels = features.shape[1]
    features = features.reshape(local_frames, strip_tokens, channels)
    forward = [(i, i + 1) for i in range(head_groups - 1)]
    backward = [(i + 1, i) for i in range(head_groups - 1)]
    above = lax.ppermute(features[:, strip_tokens - GRID :], "head", forward)
    below = lax.ppermute(features[:, :GRID], "head", backward)
    return jnp.concatenate([above, features, below], axis=1)


def on_device(
    tokens,
    qkv_weight,
    out_weight,
    norm_gain,
    proj_weight,
    up_weight,
    conv_weight,
    conv_bias,
    block_lists,
    block_counts,
):
    local_frames, strip_tokens, model_width = tokens.shape
    groups, teams = lax.axis_size("head"), lax.axis_size("frame")
    one_head_a_chip = (
        teams * groups == 2 * HEADS and groups % 4 == 0 and strip_tokens == BLOCK and local_frames == 2
        and model_width == 64 * HEADS
    )
    if one_head_a_chip:
        extended = front(
            tokens, qkv_weight, block_lists, block_counts, out_weight, norm_gain, proj_weight,
            teams, groups,
        )
    else:
        extended = by_teams(
            tokens, qkv_weight, out_weight, norm_gain, proj_weight, block_lists, block_counts
        )
    return predict(extended, up_weight, conv_weight, conv_bias, strip_tokens // GRID)


def solution(mesh):
    in_specs = (
        P("frame", "head", None),
        P(),
        P(),
        P(),
        P(),
        P(),
        P(),
        P(),
        P("frame", None),
        P("frame"),
    )
    out_specs = P("frame", "head", None, None)
    return jax.shard_map(
        on_device, mesh=mesh, in_specs=in_specs, out_specs=out_specs, check_vma=False
    )
```
